128 devices in a mesh: row: 4 (over y), col: 32 (over x, z, core).
Axes of the slice: x: 4, y: 4, z: 4, core: 2. Of those that a mesh axis runs over, the one named last changes fastest.
Arguments:
- charges: float32 [16, 32, 16, 256], P('row', 'col'), may hold values from -6 to 6
- column_order: int32 [32], replicated, may hold values from 0 to 31, as said below
- vertices: float32 [3, 66177], replicated, as said below
- panel_vertices: int32 [3, 131072], replicated, may hold values from 0 to 66176, as said below
- near_pairs: int32 [2, 2048], replicated, may hold values from 0 to 511, as said below
Outputs:
- potential_one: float32 [16, 32, 16, 256], P('row', 'col')
- potential_two: float32 [16, 32, 16, 256], P('row', 'col')
The draws below stay inside these ranges and needn't reach their ends.
Inputs may be any that keep to these rules, and one draw needn't show every extreme that they name: column_order is a permutation of 0 to 31. `panel_vertices`: panels b * 256 to (b + 1) * 256 - 1 cover block b, a patch of 8 x 16 lattice quads each cut into two triangles along one of its diagonals; vertex ids are lattice row * 513 + lattice column. `vertices`: a jittered lattice of spacing 1.8 in x and y with heights in z; every panel has positive area. `near_pairs`: each column is a pair of distinct block ids, lower first, listed once; the higher block lies at most 3 grid rows below and within squared grid distance 12 of the lower one; entries 512 * b to 512 * (b + 1) - 1 are exactly the pairs whose lower block lies in grid rows 4 * b to 4 * (b + 1) - 1.
All inputs are finite; a program needn't handle non-finite values.
Results may differ from the reference program's by a relative error of at most 0.0003.
Values sent between devices are 32-bit elements; how exact they have to be, the bound alone decides.
A program may use at most 320 MiB of HBM per device.

```python
import math
import jax
import jax.numpy as jnp
import numpy as np
from jax import lax

QUAD_ROWS = 8
QUAD_COLS = 16
PANELS = 256
NRHS = 16
BAND_ROWS = 4
GRID_ROWS = 16
GRID_COLS = 32
NBLK = 512
BAND_PAIRS = 512
NVERT = 66177
NPANEL = 131072


def draw_column_order(key, part):
    return jax.random.permutation(key, GRID_COLS).astype(jnp.int32)


def draw_vertices(key, part):
    lattice_cols = GRID_COLS * QUAD_COLS + 1
    vertex_index = jnp.arange(NVERT, dtype=jnp.int32)
    lattice_row = (vertex_index // lattice_cols).astype(jnp.float32)
    lattice_col = (vertex_index % lattice_cols).astype(jnp.float32)
    spacing = 1.8
    across_key, along_key, height_key = jax.random.split(key, 3)
    shift_x = 0.08 * spacing * jnp.clip(jax.random.normal(across_key, (NVERT,), jnp.float32), -1.8, 1.8)
    shift_y = 0.08 * spacing * jnp.clip(jax.random.normal(along_key, (NVERT,), jnp.float32), -1.8, 1.8)
    height = 0.3 * spacing * jnp.clip(jax.random.normal(height_key, (NVERT,), jnp.float32), -3.0, 3.0)
    coord_x = spacing * lattice_col + shift_x
    coord_y = spacing * lattice_row + shift_y
    return jnp.stack([coord_x, coord_y, height]).astype(jnp.float32)


def draw_panel_vertices(key, part):
    lattice_cols = GRID_COLS * QUAD_COLS + 1
    panel_index = jnp.arange(NPANEL, dtype=jnp.int32)
    block_id = panel_index // PANELS
    within = panel_index % PANELS
    quad_index = within // 2
    second_half = within % 2
    vertex_row = block_id // GRID_COLS * QUAD_ROWS + quad_index // QUAD_COLS
    vertex_col = block_id % GRID_COLS * QUAD_COLS + quad_index % QUAD_COLS
    corner_a = vertex_row * lattice_cols + vertex_col
    corner_b = corner_a + 1
    corner_c = corner_a + lattice_cols
    corner_d = corner_c + 1
    flips = jax.random.randint(key, (NPANEL // 2,), 0, 2, dtype=jnp.int32)[panel_index // 2]
    first_corner = jnp.where(second_half == 0, corner_a, jnp.where(flips == 0, corner_a, corner_b))
    second_corner = jnp.where(second_half == 0, corner_b, corner_d)
    third_corner = jnp.where(second_half == 0, jnp.where(flips == 0, corner_d, corner_c), corner_c)
    return jnp.stack([first_corner, second_corner, third_corner]).astype(jnp.int32)


def draw_near_pairs(key, part):
    row_steps = jnp.array([0, 0, 0, 1, 1, 1, 1, 1, 1, 1, 2, 2, 2, 2, 2, 3, 3, 3], dtype=jnp.int32)
    col_steps = jnp.array([1, 2, 3, -3, -2, -1, 0, 1, 2, 3, -2, -1, 0, 1, 2, -1, 0, 1], dtype=jnp.int32)
    band_total = GRID_ROWS // BAND_ROWS
    per_band = BAND_ROWS * GRID_COLS * 18
    candidates = jnp.arange(per_band, dtype=jnp.int32)
    local_row = candidates // (GRID_COLS * 18)
    grid_col = candidates // 18 % GRID_COLS
    offset = candidates % 18
    band_ids = jnp.arange(band_total, dtype=jnp.int32)[:, None]
    grid_row = band_ids * BAND_ROWS + local_row[None, :]
    far_row = grid_row + row_steps[offset][None, :]
    far_col = grid_col + col_steps[offset]
    inside = (far_row < GRID_ROWS) & ((far_col >= 0) & (far_col < GRID_COLS))[None, :]
    start_key, random_key = jax.random.split(key)
    crowded_start = jax.random.randint(start_key, (), 0, GRID_COLS, dtype=jnp.int32)
    crowded = (grid_col - crowded_start) % GRID_COLS < max(GRID_COLS // 4, 1)
    random_part = jax.random.randint(random_key, (band_total, per_band), 0, 16384, dtype=jnp.int32)
    low_all = grid_row * GRID_COLS + grid_col[None, :]
    high_all = far_row * GRID_COLS + far_col[None, :]
    forced = (low_all == 0) & (high_all == 1) | (low_all == NBLK - 2) & (high_all == NBLK - 1)
    priority = random_part + jnp.where(crowded, 8192, 0)[None, :]
    priority = jnp.where(forced & inside, 30000, priority)
    ranking = jnp.where(inside, priority * per_band + candidates[None, :], -1 - candidates[None, :])
    chosen = lax.top_k(ranking, BAND_PAIRS)[1]
    low_pick = jnp.take_along_axis(low_all, chosen, axis=1)
    high_pick = jnp.take_along_axis(high_all, chosen, axis=1)
    ordering = jnp.argsort(low_pick * NBLK + high_pick, axis=1, stable=True)
    low_sorted = jnp.take_along_axis(low_pick, ordering, axis=1).reshape(-1)
    high_sorted = jnp.take_along_axis(high_pick, ordering, axis=1).reshape(-1)
    return jnp.stack([low_sorted, high_sorted]).astype(jnp.int32)


def shard_levels(rng, shape, cuts, low, top_value):
    level, own = 1.0, jax.random.fold_in(rng, 6)
    for axis_at, blocks in cuts:
        draws = jnp.exp(jax.random.uniform(jax.random.fold_in(own, axis_at), (blocks,), jnp.float32, low / len(cuts), top_value / len(cuts)))
        level = level * jnp.repeat(draws, shape[axis_at] // blocks).reshape([-1 if axis == axis_at else 1 for axis in range(len(shape))])
    return level


def scatter_about(key, dims, width, limit, shards=(), kind=jnp.bfloat16):
    values = jax.random.normal(key, dims, jnp.float32) * width
    if len(shards) > 0:
        values = shard_levels(key, dims, shards, -0.22, 0.18) * values
    return jnp.clip(values, min=-limit, max=limit).astype(kind)


def setup_inputs(seed: int = 0) -> dict:
    key_of = jax.random.split(jax.random.key(seed), 6)
    return {
        "charges": scatter_about(key_of[0], (GRID_ROWS, GRID_COLS, NRHS, PANELS), 1.0, 6.0, ((0, 4), (1, 32)), jnp.float32),
        "column_order": draw_column_order(jax.random.fold_in(key_of[5], 71), 0),
        "vertices": draw_vertices(jax.random.fold_in(key_of[5], 71), 0),
        "panel_vertices": draw_panel_vertices(jax.random.fold_in(key_of[5], 71), 0),
        "near_pairs": draw_near_pairs(jax.random.fold_in(key_of[5], 71), 0),
    }


def rule_tables():
    gauss_two = np.array([-1.0, 1.0]) / math.sqrt(3.0)
    gauss_four = np.array([-0.8611363115940526, -0.3399810435848563, 0.3399810435848563, 0.8611363115940526])
    weight_four = np.array([0.3478548451374538, 0.6521451548625461, 0.6521451548625461, 0.3478548451374538])
    corner_weights = []
    point_weights = []
    for first_index in range(2):
        for second_index in range(4):
            along = 0.5 * (1.0 + gauss_two[first_index])
            across = 0.5 * (1.0 + gauss_four[second_index])
            corner_weights.append([along, (1.0 - along) * across, (1.0 - along) * (1.0 - across)])
            point_weights.append(2.0 * 0.5 * 0.5 * weight_four[second_index] * (1.0 - along))
    return (np.array(corner_weights), np.array(point_weights))

def block_geometry(vertices, panel_vertices, block_ids):

    def take_block(block_id):
        return lax.dynamic_slice_in_dim(panel_vertices, (block_id * PANELS).astype(jnp.int32), PANELS, 1)
    indices = jax.vmap(take_block)(block_ids)
    corners = jnp.moveaxis(vertices[:, indices], 0, 1)
    centre = (corners[:, :, 0] + corners[:, :, 1] + corners[:, :, 2]) / 3.0
    first_edge = corners[:, :, 1] - corners[:, :, 0]
    second_edge = corners[:, :, 2] - corners[:, :, 0]
    normal_x = first_edge[:, 1] * second_edge[:, 2] - first_edge[:, 2] * second_edge[:, 1]
    normal_y = first_edge[:, 2] * second_edge[:, 0] - first_edge[:, 0] * second_edge[:, 2]
    normal_z = first_edge[:, 0] * second_edge[:, 1] - first_edge[:, 1] * second_edge[:, 0]
    panel_area = 0.5 * jnp.sqrt(normal_x * normal_x + normal_y * normal_y + normal_z * normal_z)
    corner_weights, _ = rule_tables()
    points = jnp.einsum('kc,gxcp->gxkp', jnp.asarray(corner_weights, corners.dtype), corners, precision=lax.Precision.HIGHEST)
    return (centre, points, panel_area)

def tile_block(target, source):
    target_centre, target_points, target_area = target
    source_centre, source_points, source_area = source
    _, point_weights = rule_tables()
    kernel_sum = jnp.zeros((target_centre.shape[0], target_centre.shape[2], source_centre.shape[2]), target_centre.dtype)
    for point_index in range(8):
        weight = float(point_weights[point_index])
        distance = target_centre[:, :, :, None] - source_points[:, :, point_index, None, :]
        kernel_sum = kernel_sum + weight / jnp.sqrt(lax.optimization_barrier(jnp.sum(distance * distance, axis=1)) + 0.01)
        distance = target_points[:, :, point_index, :, None] - source_centre[:, :, None, :]
        kernel_sum = kernel_sum + weight / jnp.sqrt(lax.optimization_barrier(jnp.sum(distance * distance, axis=1)) + 0.01)
    return kernel_sum * target_area[:, :, None] * source_area[:, None, :] / (8.0 * math.pi)

def near_product(block_values, vertices, panel_vertices, near_pairs):
    all_blocks = jnp.arange(NBLK, dtype=jnp.int32).reshape(GRID_ROWS, GRID_COLS)

    def self_part(block_ids):
        geometry = block_geometry(vertices, panel_vertices, block_ids)
        tile_stack = tile_block(geometry, geometry)
        return jnp.einsum('grq,gpq->grp', block_values[block_ids], tile_stack, precision=lax.Precision.HIGHEST)
    result = lax.map(self_part, all_blocks).reshape(NBLK, NRHS, PANELS)
    pair_batches = jnp.transpose(near_pairs.reshape(2, -1, GRID_COLS), (1, 0, 2))

    def pair_part(carried, batch):
        low_blocks = batch[0]
        high_blocks = batch[1]
        tile_stack = tile_block(block_geometry(vertices, panel_vertices, low_blocks), block_geometry(vertices, panel_vertices, high_blocks))
        to_low = jnp.einsum('grq,gpq->grp', block_values[high_blocks], tile_stack, precision=lax.Precision.HIGHEST)
        to_high = jnp.einsum('grp,gpq->grq', block_values[low_blocks], tile_stack, precision=lax.Precision.HIGHEST)
        carried = carried.at[low_blocks].add(to_low).at[high_blocks].add(to_high)
        return (carried, None)
    result, _ = lax.scan(pair_part, result, pair_batches)
    return result

def reference(charges, column_order, vertices, panel_vertices, near_pairs):
    position_of = jnp.zeros((GRID_COLS,), jnp.int32).at[column_order].set(jnp.arange(GRID_COLS, dtype=jnp.int32))
    block_charges = charges[:, position_of].reshape(NBLK, NRHS, PANELS)
    first_block = near_product(block_charges, vertices, panel_vertices, near_pairs)
    second_block = near_product(first_block, vertices, panel_vertices, near_pairs)

    def layout(block_result):
        return block_result.reshape(GRID_ROWS, GRID_COLS, NRHS, PANELS)[:, column_order]
    return (layout(first_block), layout(second_block))
```

```python
import math

import jax
import jax.numpy as jnp
import numpy as np
from jax import lax
from jax.sharding import PartitionSpec as P

PANELS = 256
REACH = 4


def shifted(value, axis, by):
    length = lax.axis_size(axis)
    pairs = [(i, i + by) for i in range(length) if 0 <= i + by < length]
    return lax.ppermute(value, axis, pairs)


def rule_tables():
    gauss_two = np.array([-1.0, 1.0]) / math.sqrt(3.0)
    gauss_four = np.array(
        [-0.8611363115940526, -0.3399810435848563, 0.3399810435848563, 0.8611363115940526]
    )
    weight_four = np.array(
        [0.3478548451374538, 0.6521451548625461, 0.6521451548625461, 0.3478548451374538]
    )
    corner_weights = []
    point_weights = []
    for first_index in range(2):
        for second_index in range(4):
            along = 0.5 * (1.0 + gauss_two[first_index])
            across = 0.5 * (1.0 + gauss_four[second_index])
            corner_weights.append([along, (1.0 - along) * across, (1.0 - along) * (1.0 - across)])
            point_weights.append(2.0 * 0.5 * 0.5 * weight_four[second_index] * (1.0 - along))
    return (np.array(corner_weights), np.array(point_weights))


def block_geometry(vertices, panel_vertices, block_ids):
    panels = panel_vertices.reshape(3, -1, PANELS)[:, block_ids]
    corners = jnp.transpose(vertices[:, panels], (2, 1, 0, 3))
    centre = (corners[:, 0] + corners[:, 1] + corners[:, 2]) / 3.0
    first_edge = corners[:, 1] - corners[:, 0]
    second_edge = corners[:, 2] - corners[:, 0]
    normal_x = first_edge[:, 1] * second_edge[:, 2] - first_edge[:, 2] * second_edge[:, 1]
    normal_y = first_edge[:, 2] * second_edge[:, 0] - first_edge[:, 0] * second_edge[:, 2]
    normal_z = first_edge[:, 0] * second_edge[:, 1] - first_edge[:, 1] * second_edge[:, 0]
    panel_area = 0.5 * jnp.sqrt(normal_x * normal_x + normal_y * normal_y + normal_z * normal_z)
    corner_weights, _ = rule_tables()
    points = jnp.einsum(
        "kc,gcxp->gxkp",
        jnp.asarray(corner_weights, corners.dtype),
        corners,
        precision=lax.Precision.HIGHEST,
    )
    return (centre, points, panel_area)


def tile_block(target, source):
    target_centre, target_points, target_area = target
    source_centre, source_points, source_area = source
    _, point_weights = rule_tables()
    kernel_sum = jnp.zeros(
        (target_centre.shape[0], target_centre.shape[2], source_centre.shape[2]), jnp.float32
    )
    for point_index in range(8):
        weight = float(point_weights[point_index])
        distance = target_centre[:, :, :, None] - source_points[:, :, point_index, None, :]
        kernel_sum = kernel_sum + weight * lax.rsqrt(jnp.sum(distance * distance, axis=1) + 0.01)
        distance = target_points[:, :, point_index, :, None] - source_centre[:, :, None, :]
        kernel_sum = kernel_sum + weight * lax.rsqrt(jnp.sum(distance * distance, axis=1) + 0.01)
    return kernel_sum * target_area[:, :, None] * source_area[:, None, :] / (8.0 * math.pi)


def apply_tiles(source_values, tile_stack):
    return jnp.einsum("grq,gpq->grp", source_values, tile_stack, precision=lax.Precision.HIGHEST)


def apply_transposed(source_values, tile_stack):
    return jnp.einsum("grp,gpq->grq", source_values, tile_stack, precision=lax.Precision.HIGHEST)


def prepare(column_order, vertices, panel_vertices, near_pairs, band_rows):
    columns = lax.axis_size("col")
    band_count = lax.axis_size("row")
    band_index = lax.axis_index("row")
    column_index = lax.axis_index("col")
    positions = jnp.arange(columns, dtype=jnp.int32)
    position_of = jnp.sum(
        jnp.where(column_order[:, None] == positions[None, :], positions[:, None], 0), axis=0
    )
    home_column = jnp.sum(jnp.where(positions == column_index, column_order, 0))
    first_row = band_index * band_rows
    own_blocks = (first_row + jnp.arange(band_rows, dtype=jnp.int32)) * columns + home_column
    band_pairs = near_pairs.shape[1] // band_count
    share = band_pairs // columns
    segment = lax.dynamic_slice_in_dim(
        near_pairs, band_index * band_pairs + column_index * share, share, 1
    )
    low_blocks = segment[0]
    high_blocks = segment[1]
    targets = jnp.concatenate([own_blocks, low_blocks])
    sources = jnp.concatenate([own_blocks, high_blocks])
    tiles = tile_block(
        block_geometry(vertices, panel_vertices, targets),
        block_geometry(vertices, panel_vertices, sources),
    )
    self_tiles = tiles[:band_rows]
    pair_tiles = tiles[band_rows:]
    low_row = low_blocks // columns - first_row
    high_row = high_blocks // columns - first_row
    low_pos = position_of[low_blocks % columns]
    high_pos = position_of[high_blocks % columns]
    slot_table = (low_row, low_pos, high_row, high_pos)
    return (self_tiles, pair_tiles, slot_table)


def near_product(block_values, prepared):
    self_tiles, pair_tiles, slot_table = prepared
    band_rows = block_values.shape[0]
    low_row, low_pos, high_row, high_pos = slot_table
    self_term = apply_tiles(block_values[:, 0], self_tiles)
    later = shifted(block_values[:REACH], "row", -1)
    source_table = lax.all_gather(
        jnp.concatenate([block_values, later], axis=0), "col", axis=1, tiled=True
    )
    to_low = apply_tiles(source_table[high_row, high_pos], pair_tiles)
    to_high = apply_transposed(source_table[low_row, low_pos], pair_tiles)
    partial_value = jnp.zeros(source_table.shape, jnp.float32)
    partial_value = partial_value.at[low_row, low_pos].add(to_low).at[high_row, high_pos].add(to_high)
    summed = lax.psum_scatter(partial_value, "col", scatter_dimension=1, tiled=True)
    carried_down = shifted(summed[band_rows:], "row", 1)
    head = summed[:REACH] + carried_down
    own = jnp.concatenate([head, summed[REACH:band_rows]], axis=0)
    return own + self_term[:, None]


def body(charges, column_order, vertices, panel_vertices, near_pairs):
    prepared = prepare(column_order, vertices, panel_vertices, near_pairs, charges.shape[0])
    potential_one = near_product(charges, prepared)
    potential_two = near_product(potential_one, prepared)
    return (potential_one, potential_two)


def solution(mesh):
    return jax.shard_map(
        body,
        mesh=mesh,
        in_specs=(P("row", "col", None, None), P(), P(), P(), P()),
        out_specs=(P("row", "col", None, None), P("row", "col", None, None)),
        check_vma=False,
    )
```

```python
import math

import jax
import jax.numpy as jnp
import numpy as np
from jax import lax
from jax.sharding import PartitionSpec as P

PANELS = 256
REACH = 4
QUAD_ROWS = 8
QUAD_COLS = 16


def shifted(value, axis, by):
    length = lax.axis_size(axis)
    pairs = [(i, i + by) for i in range(length) if 0 <= i + by < length]
    return lax.ppermute(value, axis, pairs)


def rule_tables():
    gauss_two = np.array([-1.0, 1.0]) / math.sqrt(3.0)
    gauss_four = np.array(
        [-0.8611363115940526, -0.3399810435848563, 0.3399810435848563, 0.8611363115940526]
    )
    weight_four = np.array(
        [0.3478548451374538, 0.6521451548625461, 0.6521451548625461, 0.3478548451374538]
    )
    corner_weights = []
    point_weights = []
    for first_index in range(2):
        for second_index in range(4):
            along = 0.5 * (1.0 + gauss_two[first_index])
            across = 0.5 * (1.0 + gauss_four[second_index])
            corner_weights.append([along, (1.0 - along) * across, (1.0 - along) * (1.0 - across)])
            point_weights.append(2.0 * 0.5 * 0.5 * weight_four[second_index] * (1.0 - along))
    return (np.array(corner_weights), np.array(point_weights))


def block_corners(vertices, panel_vertices, block_ids, lattice_cols):
    patch_rows, patch_cols = QUAD_ROWS + 1, QUAD_COLS + 1
    panels = panel_vertices.reshape(3, -1, PANELS)[:, block_ids]
    lattice_row = panels // lattice_cols
    lattice_col = panels % lattice_cols
    base_row = jnp.min(lattice_row, axis=(0, 2))
    base_col = jnp.min(lattice_col, axis=(0, 2))
    local = (lattice_row - base_row[None, :, None]) * patch_cols + (
        lattice_col - base_col[None, :, None]
    )
    grid = vertices.reshape(3, -1, lattice_cols)

    def take_patch(row, col):
        return lax.dynamic_slice(grid, (0, row, col), (3, patch_rows, patch_cols))

    patch = jax.vmap(take_patch)(base_row, base_col).reshape(
        block_ids.shape[0], 3, patch_rows * patch_cols
    )
    pick = (
        local[:, :, :, None] == jnp.arange(patch_rows * patch_cols, dtype=jnp.int32)
    ).astype(jnp.float32)
    return jnp.einsum("gxl,cgpl->gcxp", patch, pick, precision=lax.Precision.HIGHEST)


def block_geometry(vertices, panel_vertices, block_ids, lattice_cols):
    corners = block_corners(vertices, panel_vertices, block_ids, lattice_cols)
    centre = (corners[:, 0] + corners[:, 1] + corners[:, 2]) / 3.0
    first_edge = corners[:, 1] - corners[:, 0]
    second_edge = corners[:, 2] - corners[:, 0]
    normal_x = first_edge[:, 1] * second_edge[:, 2] - first_edge[:, 2] * second_edge[:, 1]
    normal_y = first_edge[:, 2] * second_edge[:, 0] - first_edge[:, 0] * second_edge[:, 2]
    normal_z = first_edge[:, 0] * second_edge[:, 1] - first_edge[:, 1] * second_edge[:, 0]
    panel_area = 0.5 * jnp.sqrt(normal_x * normal_x + normal_y * normal_y + normal_z * normal_z)
    corner_weights, _ = rule_tables()
    points = jnp.einsum(
        "kc,gcxp->gxkp",
        jnp.asarray(corner_weights, corners.dtype),
        corners,
        precision=lax.Precision.HIGHEST,
    )
    return (centre, points, panel_area)


def tile_block(target, source):
    target_centre, target_points, target_area = target
    source_centre, source_points, source_area = source
    _, point_weights = rule_tables()
    kernel_sum = jnp.zeros(
        (target_centre.shape[0], target_centre.shape[2], source_centre.shape[2]), jnp.float32
    )
    for point_index in range(8):
        weight = float(point_weights[point_index])
        distance = target_centre[:, :, :, None] - source_points[:, :, point_index, None, :]
        kernel_sum = kernel_sum + weight * lax.rsqrt(jnp.sum(distance * distance, axis=1) + 0.01)
        distance = target_points[:, :, point_index, :, None] - source_centre[:, :, None, :]
        kernel_sum = kernel_sum + weight * lax.rsqrt(jnp.sum(distance * distance, axis=1) + 0.01)
    return kernel_sum * target_area[:, :, None] * source_area[:, None, :] / (8.0 * math.pi)


def apply_tiles(source_values, tile_stack):
    return jnp.einsum("grq,gpq->grp", source_values, tile_stack, precision=lax.Precision.HIGHEST)


def apply_transposed(source_values, tile_stack):
    return jnp.einsum("grp,gpq->grq", source_values, tile_stack, precision=lax.Precision.HIGHEST)


def prepare(column_order, vertices, panel_vertices, near_pairs, band_rows):
    columns = lax.axis_size("col")
    band_count = lax.axis_size("row")
    band_index = lax.axis_index("row")
    column_index = lax.axis_index("col")
    positions = jnp.arange(columns, dtype=jnp.int32)
    position_of = jnp.sum(
        jnp.where(column_order[:, None] == positions[None, :], positions[:, None], 0), axis=0
    )
    home_column = jnp.sum(jnp.where(positions == column_index, column_order, 0))
    first_row = band_index * band_rows
    own_blocks = (first_row + jnp.arange(band_rows, dtype=jnp.int32)) * columns + home_column
    band_pairs = near_pairs.shape[1] // band_count
    share = band_pairs // columns
    segment = lax.dynamic_slice_in_dim(
        near_pairs, band_index * band_pairs + column_index * share, share, 1
    )
    low_blocks = segment[0]
    high_blocks = segment[1]
    targets = jnp.concatenate([own_blocks, low_blocks])
    sources = jnp.concatenate([own_blocks, high_blocks])
    lattice_cols = columns * QUAD_COLS + 1
    tiles = tile_block(
        block_geometry(vertices, panel_vertices, targets, lattice_cols),
        block_geometry(vertices, panel_vertices, sources, lattice_cols),
    )
    self_tiles = tiles[:band_rows]
    pair_tiles = tiles[band_rows:]
    low_row = low_blocks // columns - first_row
    high_row = high_blocks // columns - first_row
    low_pos = position_of[low_blocks % columns]
    high_pos = position_of[high_blocks % columns]
    slot_table = (low_row, low_pos, high_row, high_pos)
    return (self_tiles, pair_tiles, slot_table)


def near_product(block_values, prepared):
    self_tiles, pair_tiles, slot_table = prepared
    band_rows = block_values.shape[0]
    low_row, low_pos, high_row, high_pos = slot_table
    self_term = apply_tiles(block_values[:, 0], self_tiles)
    later = shifted(block_values[:REACH], "row", -1)
    source_table = lax.all_gather(
        jnp.concatenate([block_values, later], axis=0), "col", axis=1, tiled=True
    )
    to_low = apply_tiles(source_table[high_row, high_pos], pair_tiles)
    to_high = apply_transposed(source_table[low_row, low_pos], pair_tiles)
    partial_value = jnp.zeros(source_table.shape, jnp.float32)
    partial_value = partial_value.at[low_row, low_pos].add(to_low).at[high_row, high_pos].add(to_high)
    summed = lax.psum_scatter(partial_value, "col", scatter_dimension=1, tiled=True)
    carried_down = shifted(summed[band_rows:], "row", 1)
    head = summed[:REACH] + carried_down
    own = jnp.concatenate([head, summed[REACH:band_rows]], axis=0)
    return own + self_term[:, None]


def body(charges, column_order, vertices, panel_vertices, near_pairs):
    prepared = prepare(column_order, vertices, panel_vertices, near_pairs, charges.shape[0])
    potential_one = near_product(charges, prepared)
    potential_two = near_product(potential_one, prepared)
    return (potential_one, potential_two)


def solution(mesh):
    return jax.shard_map(
        body,
        mesh=mesh,
        in_specs=(P("row", "col", None, None), P(), P(), P(), P()),
        out_specs=(P("row", "col", None, None), P("row", "col", None, None)),
        check_vma=False,
    )
```

```python
import math

import jax
import jax.numpy as jnp
import numpy as np
from jax import lax
from jax.experimental import pallas as pl
from jax.experimental.pallas import tpu as pltpu
from jax.sharding import PartitionSpec as P

PANELS = 256
REACH = 4
QUAD_ROWS = 8
QUAD_COLS = 16


def shifted(value, axis, by):
    length = lax.axis_size(axis)
    pairs = [(i, i + by) for i in range(length) if 0 <= i + by < length]
    return lax.ppermute(value, axis, pairs)


def rule_tables():
    gauss_two = np.array([-1.0, 1.0]) / math.sqrt(3.0)
    gauss_four = np.array(
        [-0.8611363115940526, -0.3399810435848563, 0.3399810435848563, 0.8611363115940526]
    )
    weight_four = np.array(
        [0.3478548451374538, 0.6521451548625461, 0.6521451548625461, 0.3478548451374538]
    )
    corner_weights = []
    point_weights = []
    for first_index in range(2):
        for second_index in range(4):
            along = 0.5 * (1.0 + gauss_two[first_index])
            across = 0.5 * (1.0 + gauss_four[second_index])
            corner_weights.append([along, (1.0 - along) * across, (1.0 - along) * (1.0 - across)])
            point_weights.append(2.0 * 0.5 * 0.5 * weight_four[second_index] * (1.0 - along))
    return (np.array(corner_weights), np.array(point_weights))


def block_corners(vertices, panel_vertices, block_ids, lattice_cols):
    patch_rows, patch_cols = QUAD_ROWS + 1, QUAD_COLS + 1
    panels = panel_vertices.reshape(3, -1, PANELS)[:, block_ids]
    lattice_row = panels // lattice_cols
    lattice_col = panels % lattice_cols
    base_row = jnp.min(lattice_row, axis=(0, 2))
    base_col = jnp.min(lattice_col, axis=(0, 2))
    local = (lattice_row - base_row[None, :, None]) * patch_cols + (
        lattice_col - base_col[None, :, None]
    )
    grid = jnp.transpose(vertices.reshape(3, -1, lattice_cols), (1, 0, 2))
    row_pick = (
        (base_row[:, None] + jnp.arange(patch_rows, dtype=jnp.int32))[:, :, None]
        == jnp.arange(grid.shape[0], dtype=jnp.int32)
    ).astype(jnp.float32)
    col_pick = (
        jnp.arange(lattice_cols, dtype=jnp.int32)[None, :, None]
        == (base_col[:, None] + jnp.arange(patch_cols, dtype=jnp.int32))[:, None, :]
    ).astype(jnp.float32)
    band = jnp.einsum("grR,Rxc->grxc", row_pick, grid, precision=lax.Precision.HIGHEST)
    patch = jnp.einsum("grxc,gcj->gxrj", band, col_pick, precision=lax.Precision.HIGHEST)
    patch = patch.reshape(block_ids.shape[0], 3, patch_rows * patch_cols)
    pick = (
        local[:, :, :, None] == jnp.arange(patch_rows * patch_cols, dtype=jnp.int32)
    ).astype(jnp.float32)
    return jnp.einsum("gxl,cgpl->gcxp", patch, pick, precision=lax.Precision.HIGHEST)


def block_geometry(vertices, panel_vertices, block_ids, lattice_cols):
    corners = block_corners(vertices, panel_vertices, block_ids, lattice_cols)
    centre = (corners[:, 0] + corners[:, 1] + corners[:, 2]) / 3.0
    first_edge = corners[:, 1] - corners[:, 0]
    second_edge = corners[:, 2] - corners[:, 0]
    normal_x = first_edge[:, 1] * second_edge[:, 2] - first_edge[:, 2] * second_edge[:, 1]
    normal_y = first_edge[:, 2] * second_edge[:, 0] - first_edge[:, 0] * second_edge[:, 2]
    normal_z = first_edge[:, 0] * second_edge[:, 1] - first_edge[:, 1] * second_edge[:, 0]
    panel_area = 0.5 * jnp.sqrt(normal_x * normal_x + normal_y * normal_y + normal_z * normal_z)
    corner_weights, _ = rule_tables()
    points = jnp.einsum(
        "kc,gcxp->gxkp",
        jnp.asarray(corner_weights, corners.dtype),
        corners,
        precision=lax.Precision.HIGHEST,
    )
    return (centre, points, panel_area)


def tile_block(target, source):
    target_centre, target_points, target_area = target
    source_centre, source_points, source_area = source
    _, point_weights = rule_tables()
    kernel_sum = jnp.zeros(
        (target_centre.shape[0], target_centre.shape[2], source_centre.shape[2]), jnp.float32
    )
    for point_index in range(8):
        weight = float(point_weights[point_index])
        distance = target_centre[:, :, :, None] - source_points[:, :, point_index, None, :]
        kernel_sum = kernel_sum + weight * lax.rsqrt(jnp.sum(distance * distance, axis=1) + 0.01)
        distance = target_points[:, :, point_index, :, None] - source_centre[:, :, None, :]
        kernel_sum = kernel_sum + weight * lax.rsqrt(jnp.sum(distance * distance, axis=1) + 0.01)
    return kernel_sum * target_area[:, :, None] * source_area[:, None, :] / (8.0 * math.pi)


def apply_tiles(source_values, tile_stack):
    return jnp.einsum("grq,gpq->grp", source_values, tile_stack, precision=lax.Precision.HIGHEST)


def apply_transposed(source_values, tile_stack):
    return jnp.einsum("grp,gpq->grq", source_values, tile_stack, precision=lax.Precision.HIGHEST)


def prepare(column_order, vertices, panel_vertices, near_pairs, band_rows):
    columns = lax.axis_size("col")
    band_count = lax.axis_size("row")
    band_index = lax.axis_index("row")
    column_index = lax.axis_index("col")
    positions = jnp.arange(columns, dtype=jnp.int32)
    position_of = jnp.sum(
        jnp.where(column_order[:, None] == positions[None, :], positions[:, None], 0), axis=0
    )
    home_column = jnp.sum(jnp.where(positions == column_index, column_order, 0))
    first_row = band_index * band_rows
    own_blocks = (first_row + jnp.arange(band_rows, dtype=jnp.int32)) * columns + home_column
    band_pairs = near_pairs.shape[1] // band_count
    share = band_pairs // columns
    segment = lax.dynamic_slice_in_dim(
        near_pairs, band_index * band_pairs + column_index * share, share, 1
    )
    low_blocks = segment[0]
    high_blocks = segment[1]
    targets = jnp.concatenate([own_blocks, low_blocks])
    sources = jnp.concatenate([own_blocks, high_blocks])
    lattice_cols = columns * QUAD_COLS + 1
    tiles = tile_block(
        block_geometry(vertices, panel_vertices, targets, lattice_cols),
        block_geometry(vertices, panel_vertices, sources, lattice_cols),
    )
    self_tiles = tiles[:band_rows]
    pair_tiles = tiles[band_rows:]
    low_row = low_blocks // columns - first_row
    high_row = high_blocks // columns - first_row
    low_pos = position_of[low_blocks % columns]
    high_pos = position_of[high_blocks % columns]
    slot_table = (low_row, low_pos, high_row, high_pos)
    return (self_tiles, pair_tiles, slot_table)


def near_product(block_values, prepared):
    self_tiles, pair_tiles, slot_table = prepared
    band_rows = block_values.shape[0]
    low_row, low_pos, high_row, high_pos = slot_table
    self_term = apply_tiles(block_values[:, 0], self_tiles)
    later = shifted(block_values[:REACH], "row", -1)
    source_table = lax.all_gather(
        jnp.concatenate([block_values, later], axis=0), "col", axis=1, tiled=True
    )
    to_low = apply_tiles(source_table[high_row, high_pos], pair_tiles)
    to_high = apply_transposed(source_table[low_row, low_pos], pair_tiles)
    partial_value = jnp.zeros(source_table.shape, jnp.float32)
    partial_value = partial_value.at[low_row, low_pos].add(to_low).at[high_row, high_pos].add(to_high)
    summed = lax.psum_scatter(partial_value, "col", scatter_dimension=1, tiled=True)
    carried_down = shifted(summed[band_rows:], "row", 1)
    head = summed[:REACH] + carried_down
    own = jnp.concatenate([head, summed[REACH:band_rows]], axis=0)
    return own + self_term[:, None]


def body(charges, column_order, vertices, panel_vertices, near_pairs):
    prepared = prepare(column_order, vertices, panel_vertices, near_pairs, charges.shape[0])
    potential_one = near_product(charges, prepared)
    potential_two = near_product(potential_one, prepared)
    return (potential_one, potential_two)


def solution(mesh):
    return jax.shard_map(
        body,
        mesh=mesh,
        in_specs=(P("row", "col", None, None), P(), P(), P(), P()),
        out_specs=(P("row", "col", None, None), P("row", "col", None, None)),
        check_vma=False,
    )
```

```python
import math

import jax
import jax.numpy as jnp
import numpy as np
from jax import lax
from jax.experimental import pallas as pl
from jax.experimental.pallas import tpu as pltpu
from jax.sharding import PartitionSpec as P

PANELS = 256
REACH = 4
QUAD_ROWS = 8
QUAD_COLS = 16
FEATURES = 32


def shifted(value, axis, by):
    length = lax.axis_size(axis)
    pairs = [(i, i + by) for i in range(length) if 0 <= i + by < length]
    return lax.ppermute(value, axis, pairs)


def rule_tables():
    gauss_two = np.array([-1.0, 1.0]) / math.sqrt(3.0)
    gauss_four = np.array(
        [-0.8611363115940526, -0.3399810435848563, 0.3399810435848563, 0.8611363115940526]
    )
    weight_four = np.array(
        [0.3478548451374538, 0.6521451548625461, 0.6521451548625461, 0.3478548451374538]
    )
    corner_weights = []
    point_weights = []
    for first_index in range(2):
        for second_index in range(4):
            along = 0.5 * (1.0 + gauss_two[first_index])
            across = 0.5 * (1.0 + gauss_four[second_index])
            corner_weights.append([along, (1.0 - along) * across, (1.0 - along) * (1.0 - across)])
            point_weights.append(2.0 * 0.5 * 0.5 * weight_four[second_index] * (1.0 - along))
    return (np.array(corner_weights), np.array(point_weights))


def block_corners(vertices, panel_vertices, block_ids, lattice_cols):
    patch_rows, patch_cols = QUAD_ROWS + 1, QUAD_COLS + 1
    panels = panel_vertices.reshape(3, -1, PANELS)[:, block_ids]
    lattice_row = panels // lattice_cols
    lattice_col = panels % lattice_cols
    base_row = jnp.min(lattice_row, axis=(0, 2))
    base_col = jnp.min(lattice_col, axis=(0, 2))
    local = (lattice_row - base_row[None, :, None]) * patch_cols + (
        lattice_col - base_col[None, :, None]
    )
    grid = jnp.transpose(vertices.reshape(3, -1, lattice_cols), (1, 0, 2))
    row_pick = (
        (base_row[:, None] + jnp.arange(patch_rows, dtype=jnp.int32))[:, :, None]
        == jnp.arange(grid.shape[0], dtype=jnp.int32)
    ).astype(jnp.float32)
    col_pick = (
        jnp.arange(lattice_cols, dtype=jnp.int32)[None, :, None]
        == (base_col[:, None] + jnp.arange(patch_cols, dtype=jnp.int32))[:, None, :]
    ).astype(jnp.float32)
    band = jnp.einsum("grR,Rxc->grxc", row_pick, grid, precision=lax.Precision.HIGHEST)
    patch = jnp.einsum("grxc,gcj->gxrj", band, col_pick, precision=lax.Precision.HIGHEST)
    patch = patch.reshape(block_ids.shape[0], 3, patch_rows * patch_cols)
    pick = (
        local[:, :, :, None] == jnp.arange(patch_rows * patch_cols, dtype=jnp.int32)
    ).astype(jnp.float32)
    return jnp.einsum("gxl,cgpl->gcxp", patch, pick, precision=lax.Precision.HIGHEST)


def block_geometry(vertices, panel_vertices, block_ids, lattice_cols):
    corners = block_corners(vertices, panel_vertices, block_ids, lattice_cols)
    centre = (corners[:, 0] + corners[:, 1] + corners[:, 2]) / 3.0
    first_edge = corners[:, 1] - corners[:, 0]
    second_edge = corners[:, 2] - corners[:, 0]
    normal_x = first_edge[:, 1] * second_edge[:, 2] - first_edge[:, 2] * second_edge[:, 1]
    normal_y = first_edge[:, 2] * second_edge[:, 0] - first_edge[:, 0] * second_edge[:, 2]
    normal_z = first_edge[:, 0] * second_edge[:, 1] - first_edge[:, 1] * second_edge[:, 0]
    panel_area = 0.5 * jnp.sqrt(normal_x * normal_x + normal_y * normal_y + normal_z * normal_z)
    corner_weights, _ = rule_tables()
    points = jnp.einsum(
        "kc,gcxp->gxkp",
        jnp.asarray(corner_weights, corners.dtype),
        corners,
        precision=lax.Precision.HIGHEST,
    )
    return (centre, points, panel_area)


def feature_rows(geometry):
    centre, points, area = geometry
    count = centre.shape[0]
    flat_points = jnp.transpose(points, (0, 2, 1, 3)).reshape(count, -1, PANELS)
    pad = jnp.zeros((count, FEATURES - 4 - flat_points.shape[1], PANELS), jnp.float32)
    return jnp.concatenate([centre, flat_points, area[:, None], pad], axis=1)


def tile_block(target, source):
    _, point_weights = rule_tables()
    target_rows = jnp.transpose(feature_rows(target), (0, 2, 1))
    source_rows = feature_rows(source)
    count = target_rows.shape[0]
    area_at = 3 + 3 * len(point_weights)
    chunk = 8

    def kernel(target_ref, source_ref, out_ref):
        def body(step, carry):
            rows = pl.ds(pl.multiple_of(step * chunk, chunk), chunk)
            held = target_ref[0, rows, :]
            total = jnp.zeros((chunk, PANELS), jnp.float32)
            for point_index, weight in enumerate(point_weights):
                at = 3 + 3 * point_index
                squared = 0.01
                for axis in range(3):
                    gap = held[:, axis : axis + 1] - source_ref[0, at + axis : at + axis + 1, :]
                    squared = squared + gap * gap
                total = total + float(weight) * lax.rsqrt(squared)
                squared = 0.01
                for axis in range(3):
                    gap = held[:, at + axis : at + axis + 1] - source_ref[0, axis : axis + 1, :]
                    squared = squared + gap * gap
                total = total + float(weight) * lax.rsqrt(squared)
            scale = held[:, area_at : area_at + 1] * source_ref[0, area_at : area_at + 1, :]
            out_ref[0, rows, :] = total * scale * (1.0 / (8.0 * math.pi))
            return carry

        lax.fori_loop(0, PANELS // chunk, body, 0)

    return pl.pallas_call(
        kernel,
        out_shape=jax.ShapeDtypeStruct((count, PANELS, PANELS), jnp.float32),
        grid=(count,),
        in_specs=[
            pl.BlockSpec((1, PANELS, FEATURES), lambda i: (i, 0, 0)),
            pl.BlockSpec((1, FEATURES, PANELS), lambda i: (i, 0, 0)),
        ],
        out_specs=pl.BlockSpec((1, PANELS, PANELS), lambda i: (i, 0, 0)),
        cost_estimate=pl.CostEstimate(
            flops=count * PANELS * PANELS * 16 * 11,
            transcendentals=count * PANELS * PANELS * 16,
            bytes_accessed=count * PANELS * (PANELS + 2 * FEATURES) * 4,
        ),
    )(target_rows, source_rows)


def apply_tiles(source_values, tile_stack):
    return jnp.einsum("grq,gpq->grp", source_values, tile_stack, precision=lax.Precision.HIGHEST)


def apply_transposed(source_values, tile_stack):
    return jnp.einsum("grp,gpq->grq", source_values, tile_stack, precision=lax.Precision.HIGHEST)


def prepare(column_order, vertices, panel_vertices, near_pairs, band_rows):
    columns = lax.axis_size("col")
    band_count = lax.axis_size("row")
    band_index = lax.axis_index("row")
    column_index = lax.axis_index("col")
    positions = jnp.arange(columns, dtype=jnp.int32)
    position_of = jnp.sum(
        jnp.where(column_order[:, None] == positions[None, :], positions[:, None], 0), axis=0
    )
    home_column = jnp.sum(jnp.where(positions == column_index, column_order, 0))
    first_row = band_index * band_rows
    own_blocks = (first_row + jnp.arange(band_rows, dtype=jnp.int32)) * columns + home_column
    band_pairs = near_pairs.shape[1] // band_count
    share = band_pairs // columns
    segment = lax.dynamic_slice_in_dim(
        near_pairs, band_index * band_pairs + column_index * share, share, 1
    )
    low_blocks = segment[0]
    high_blocks = segment[1]
    targets = jnp.concatenate([own_blocks, low_blocks])
    sources = jnp.concatenate([own_blocks, high_blocks])
    lattice_cols = columns * QUAD_COLS + 1
    tiles = tile_block(
        block_geometry(vertices, panel_vertices, targets, lattice_cols),
        block_geometry(vertices, panel_vertices, sources, lattice_cols),
    )
    self_tiles = tiles[:band_rows]
    pair_tiles = tiles[band_rows:]
    low_row = low_blocks // columns - first_row
    high_row = high_blocks // columns - first_row
    low_pos = position_of[low_blocks % columns]
    high_pos = position_of[high_blocks % columns]
    slot_table = (low_row, low_pos, high_row, high_pos)
    return (self_tiles, pair_tiles, slot_table)


def near_product(block_values, prepared):
    self_tiles, pair_tiles, slot_table = prepared
    band_rows = block_values.shape[0]
    low_row, low_pos, high_row, high_pos = slot_table
    self_term = apply_tiles(block_values[:, 0], self_tiles)
    later = shifted(block_values[:REACH], "row", -1)
    source_table = lax.all_gather(
        jnp.concatenate([block_values, later], axis=0), "col", axis=1, tiled=True
    )
    to_low = apply_tiles(source_table[high_row, high_pos], pair_tiles)
    to_high = apply_transposed(source_table[low_row, low_pos], pair_tiles)
    partial_value = jnp.zeros(source_table.shape, jnp.float32)
    partial_value = partial_value.at[low_row, low_pos].add(to_low).at[high_row, high_pos].add(to_high)
    summed = lax.psum_scatter(partial_value, "col", scatter_dimension=1, tiled=True)
    carried_down = shifted(summed[band_rows:], "row", 1)
    head = summed[:REACH] + carried_down
    own = jnp.concatenate([head, summed[REACH:band_rows]], axis=0)
    return own + self_term[:, None]


def body(charges, column_order, vertices, panel_vertices, near_pairs):
    prepared = prepare(column_order, vertices, panel_vertices, near_pairs, charges.shape[0])
    potential_one = near_product(charges, prepared)
    potential_two = near_product(potential_one, prepared)
    return (potential_one, potential_two)


def solution(mesh):
    return jax.shard_map(
        body,
        mesh=mesh,
        in_specs=(P("row", "col", None, None), P(), P(), P(), P()),
        out_specs=(P("row", "col", None, None), P("row", "col", None, None)),
        check_vma=False,
    )
```

```python
import math

import jax
import jax.numpy as jnp
import numpy as np
from jax import lax
from jax.experimental import pallas as pl
from jax.experimental.pallas import tpu as pltpu
from jax.sharding import PartitionSpec as P

PANELS = 256
REACH = 4
QUAD_ROWS = 8
QUAD_COLS = 16


def shifted(value, axis, by):
    length = lax.axis_size(axis)
    pairs = [(i, i + by) for i in range(length) if 0 <= i + by < length]
    return lax.ppermute(value, axis, pairs)


def rule_tables():
    gauss_two = np.array([-1.0, 1.0]) / math.sqrt(3.0)
    gauss_four = np.array(
        [-0.8611363115940526, -0.3399810435848563, 0.3399810435848563, 0.8611363115940526]
    )
    weight_four = np.array(
        [0.3478548451374538, 0.6521451548625461, 0.6521451548625461, 0.3478548451374538]
    )
    corner_weights = []
    point_weights = []
    for first_index in range(2):
        for second_index in range(4):
            along = 0.5 * (1.0 + gauss_two[first_index])
            across = 0.5 * (1.0 + gauss_four[second_index])
            corner_weights.append([along, (1.0 - along) * across, (1.0 - along) * (1.0 - across)])
            point_weights.append(2.0 * 0.5 * 0.5 * weight_four[second_index] * (1.0 - along))
    return (np.array(corner_weights), np.array(point_weights))


def block_corners(vertices, panel_vertices, block_ids, lattice_cols):
    patch_rows, patch_cols = QUAD_ROWS + 1, QUAD_COLS + 1
    panels = panel_vertices.reshape(3, -1, PANELS)[:, block_ids]
    lattice_row = panels // lattice_cols
    lattice_col = panels % lattice_cols
    base_row = jnp.min(lattice_row, axis=(0, 2))
    base_col = jnp.min(lattice_col, axis=(0, 2))
    local = (lattice_row - base_row[None, :, None]) * patch_cols + (
        lattice_col - base_col[None, :, None]
    )
    grid = jnp.transpose(vertices.reshape(3, -1, lattice_cols), (1, 0, 2))
    row_pick = (
        (base_row[:, None] + jnp.arange(patch_rows, dtype=jnp.int32))[:, :, None]
        == jnp.arange(grid.shape[0], dtype=jnp.int32)
    ).astype(jnp.float32)
    col_pick = (
        jnp.arange(lattice_cols, dtype=jnp.int32)[None, :, None]
        == (base_col[:, None] + jnp.arange(patch_cols, dtype=jnp.int32))[:, None, :]
    ).astype(jnp.float32)
    band = jnp.einsum("grR,Rxc->grxc", row_pick, grid, precision=lax.Precision.HIGHEST)
    patch = jnp.einsum("grxc,gcj->gxrj", band, col_pick, precision=lax.Precision.HIGHEST)
    patch = patch.reshape(block_ids.shape[0], 3, patch_rows * patch_cols)
    pick = (
        local[:, :, :, None] == jnp.arange(patch_rows * patch_cols, dtype=jnp.int32)
    ).astype(jnp.float32)
    return jnp.einsum("gxl,cgpl->gcxp", patch, pick, precision=lax.Precision.HIGHEST)


def block_geometry(vertices, panel_vertices, block_ids, lattice_cols):
    corners = block_corners(vertices, panel_vertices, block_ids, lattice_cols)
    centre = (corners[:, 0] + corners[:, 1] + corners[:, 2]) / 3.0
    first_edge = corners[:, 1] - corners[:, 0]
    second_edge = corners[:, 2] - corners[:, 0]
    normal_x = first_edge[:, 1] * second_edge[:, 2] - first_edge[:, 2] * second_edge[:, 1]
    normal_y = first_edge[:, 2] * second_edge[:, 0] - first_edge[:, 0] * second_edge[:, 2]
    normal_z = first_edge[:, 0] * second_edge[:, 1] - first_edge[:, 1] * second_edge[:, 0]
    panel_area = 0.5 * jnp.sqrt(normal_x * normal_x + normal_y * normal_y + normal_z * normal_z)
    corner_weights, _ = rule_tables()
    points = jnp.einsum(
        "kc,gcxp->gxkp",
        jnp.asarray(corner_weights, corners.dtype),
        corners,
        precision=lax.Precision.HIGHEST,
    )
    return (centre, points, panel_area)


def tile_block(target, source):
    target_centre, target_points, target_area = target
    source_centre, source_points, source_area = source
    _, point_weights = rule_tables()
    kernel_sum = jnp.zeros(
        (target_centre.shape[0], target_centre.shape[2], source_centre.shape[2]), jnp.float32
    )
    for point_index in range(8):
        weight = float(point_weights[point_index])
        distance = target_centre[:, :, :, None] - source_points[:, :, point_index, None, :]
        kernel_sum = kernel_sum + weight * lax.rsqrt(jnp.sum(distance * distance, axis=1) + 0.01)
        distance = target_points[:, :, point_index, :, None] - source_centre[:, :, None, :]
        kernel_sum = kernel_sum + weight * lax.rsqrt(jnp.sum(distance * distance, axis=1) + 0.01)
    return kernel_sum * target_area[:, :, None] * source_area[:, None, :] / (8.0 * math.pi)


def apply_tiles(source_values, tile_stack):
    return jnp.einsum("grq,gpq->grp", source_values, tile_stack, precision=lax.Precision.HIGHEST)


def apply_transposed(source_values, tile_stack):
    return jnp.einsum("grp,gpq->grq", source_values, tile_stack, precision=lax.Precision.HIGHEST)


def prepare(column_order, vertices, panel_vertices, near_pairs, band_rows):
    columns = lax.axis_size("col")
    band_count = lax.axis_size("row")
    band_index = lax.axis_index("row")
    column_index = lax.axis_index("col")
    positions = jnp.arange(columns, dtype=jnp.int32)
    position_of = jnp.sum(
        jnp.where(column_order[:, None] == positions[None, :], positions[:, None], 0), axis=0
    )
    home_column = jnp.sum(jnp.where(positions == column_index, column_order, 0))
    first_row = band_index * band_rows
    own_blocks = (first_row + jnp.arange(band_rows, dtype=jnp.int32)) * columns + home_column
    band_pairs = near_pairs.shape[1] // band_count
    share = band_pairs // columns
    segment = lax.dynamic_slice_in_dim(
        near_pairs, band_index * band_pairs + column_index * share, share, 1
    )
    low_blocks = segment[0]
    high_blocks = segment[1]
    targets = jnp.concatenate([own_blocks, low_blocks])
    sources = jnp.concatenate([own_blocks, high_blocks])
    lattice_cols = columns * QUAD_COLS + 1
    tiles = tile_block(
        block_geometry(vertices, panel_vertices, targets, lattice_cols),
        block_geometry(vertices, panel_vertices, sources, lattice_cols),
    )
    self_tiles = tiles[:band_rows]
    pair_tiles = tiles[band_rows:]
    low_row = low_blocks // columns - first_row
    high_row = high_blocks // columns - first_row
    low_pos = position_of[low_blocks % columns]
    high_pos = position_of[high_blocks % columns]
    slot_table = (low_row, low_pos, high_row, high_pos)
    return (self_tiles, pair_tiles, slot_table)


def near_product(block_values, prepared):
    self_tiles, pair_tiles, slot_table = prepared
    band_rows = block_values.shape[0]
    low_row, low_pos, high_row, high_pos = slot_table
    self_term = apply_tiles(block_values[:, 0], self_tiles)
    later = shifted(block_values[:REACH], "row", -1)
    source_table = lax.all_gather(
        jnp.concatenate([block_values, later], axis=0), "col", axis=1, tiled=True
    )
    to_low = apply_tiles(source_table[high_row, high_pos], pair_tiles)
    to_high = apply_transposed(source_table[low_row, low_pos], pair_tiles)
    partial_value = jnp.zeros(source_table.shape, jnp.float32)
    partial_value = partial_value.at[low_row, low_pos].add(to_low).at[high_row, high_pos].add(to_high)
    summed = jnp.sum(lax.all_to_all(partial_value, "col", 1, 1, tiled=True), axis=1)
    carried_down = shifted(summed[band_rows:], "row", 1)
    head = summed[:REACH] + carried_down
    own = jnp.concatenate([head, summed[REACH:band_rows]], axis=0)
    return (own + self_term)[:, None]


def body(charges, column_order, vertices, panel_vertices, near_pairs):
    prepared = prepare(column_order, vertices, panel_vertices, near_pairs, charges.shape[0])
    potential_one = near_product(charges, prepared)
    potential_two = near_product(potential_one, prepared)
    return (potential_one, potential_two)


def solution(mesh):
    return jax.shard_map(
        body,
        mesh=mesh,
        in_specs=(P("row", "col", None, None), P(), P(), P(), P()),
        out_specs=(P("row", "col", None, None), P("row", "col", None, None)),
        check_vma=False,
    )
```

```python
import math

import jax
import jax.numpy as jnp
import numpy as np
from jax import lax
from jax.experimental import pallas as pl
from jax.experimental.pallas import tpu as pltpu
from jax.sharding import PartitionSpec as P

PANELS = 256
REACH = 3
QUAD_ROWS = 8
QUAD_COLS = 16


def shifted(value, axis, by):
    length = lax.axis_size(axis)
    pairs = [(i, i + by) for i in range(length) if 0 <= i + by < length]
    return lax.ppermute(value, axis, pairs)


def rule_tables():
    gauss_two = np.array([-1.0, 1.0]) / math.sqrt(3.0)
    gauss_four = np.array(
        [-0.8611363115940526, -0.3399810435848563, 0.3399810435848563, 0.8611363115940526]
    )
    weight_four = np.array(
        [0.3478548451374538, 0.6521451548625461, 0.6521451548625461, 0.3478548451374538]
    )
    corner_weights = []
    point_weights = []
    for first_index in range(2):
        for second_index in range(4):
            along = 0.5 * (1.0 + gauss_two[first_index])
            across = 0.5 * (1.0 + gauss_four[second_index])
            corner_weights.append([along, (1.0 - along) * across, (1.0 - along) * (1.0 - across)])
            point_weights.append(2.0 * 0.5 * 0.5 * weight_four[second_index] * (1.0 - along))
    return (np.array(corner_weights), np.array(point_weights))


def block_corners(vertices, panel_vertices, block_ids, lattice_cols):
    patch_rows, patch_cols = QUAD_ROWS + 1, QUAD_COLS + 1
    panels = panel_vertices.reshape(3, -1, PANELS)[:, block_ids]
    lattice_row = panels // lattice_cols
    lattice_col = panels % lattice_cols
    base_row = jnp.min(lattice_row, axis=(0, 2))
    base_col = jnp.min(lattice_col, axis=(0, 2))
    local = (lattice_row - base_row[None, :, None]) * patch_cols + (
        lattice_col - base_col[None, :, None]
    )
    grid = jnp.transpose(vertices.reshape(3, -1, lattice_cols), (1, 0, 2))
    row_pick = (
        (base_row[:, None] + jnp.arange(patch_rows, dtype=jnp.int32))[:, :, None]
        == jnp.arange(grid.shape[0], dtype=jnp.int32)
    ).astype(jnp.float32)
    col_pick = (
        jnp.arange(lattice_cols, dtype=jnp.int32)[None, :, None]
        == (base_col[:, None] + jnp.arange(patch_cols, dtype=jnp.int32))[:, None, :]
    ).astype(jnp.float32)
    band = jnp.einsum("grR,Rxc->grxc", row_pick, grid, precision=lax.Precision.HIGHEST)
    patch = jnp.einsum("grxc,gcj->gxrj", band, col_pick, precision=lax.Precision.HIGHEST)
    patch = patch.reshape(block_ids.shape[0], 3, patch_rows * patch_cols)
    pick = (
        local[:, :, :, None] == jnp.arange(patch_rows * patch_cols, dtype=jnp.int32)
    ).astype(jnp.float32)
    return jnp.einsum("gxl,cgpl->gcxp", patch, pick, precision=lax.Precision.HIGHEST)


def block_geometry(vertices, panel_vertices, block_ids, lattice_cols):
    corners = block_corners(vertices, panel_vertices, block_ids, lattice_cols)
    centre = (corners[:, 0] + corners[:, 1] + corners[:, 2]) / 3.0
    first_edge = corners[:, 1] - corners[:, 0]
    second_edge = corners[:, 2] - corners[:, 0]
    normal_x = first_edge[:, 1] * second_edge[:, 2] - first_edge[:, 2] * second_edge[:, 1]
    normal_y = first_edge[:, 2] * second_edge[:, 0] - first_edge[:, 0] * second_edge[:, 2]
    normal_z = first_edge[:, 0] * second_edge[:, 1] - first_edge[:, 1] * second_edge[:, 0]
    panel_area = 0.5 * jnp.sqrt(normal_x * normal_x + normal_y * normal_y + normal_z * normal_z)
    corner_weights, _ = rule_tables()
    points = jnp.einsum(
        "kc,gcxp->gxkp",
        jnp.asarray(corner_weights, corners.dtype),
        corners,
        precision=lax.Precision.HIGHEST,
    )
    return (centre, points, panel_area)


def tile_block(target, source):
    target_centre, target_points, target_area = target
    source_centre, source_points, source_area = source
    _, point_weights = rule_tables()
    kernel_sum = jnp.zeros(
        (target_centre.shape[0], target_centre.shape[2], source_centre.shape[2]), jnp.float32
    )
    for point_index in range(8):
        weight = float(point_weights[point_index])
        distance = target_centre[:, :, :, None] - source_points[:, :, point_index, None, :]
        kernel_sum = kernel_sum + weight * lax.rsqrt(jnp.sum(distance * distance, axis=1) + 0.01)
        distance = target_points[:, :, point_index, :, None] - source_centre[:, :, None, :]
        kernel_sum = kernel_sum + weight * lax.rsqrt(jnp.sum(distance * distance, axis=1) + 0.01)
    return kernel_sum * target_area[:, :, None] * source_area[:, None, :] / (8.0 * math.pi)


def apply_tiles(source_values, tile_stack):
    return jnp.einsum("grq,gpq->grp", source_values, tile_stack, precision=lax.Precision.HIGHEST)


def apply_transposed(source_values, tile_stack):
    return jnp.einsum("grp,gpq->grq", source_values, tile_stack, precision=lax.Precision.HIGHEST)


def prepare(column_order, vertices, panel_vertices, near_pairs, band_rows):
    columns = lax.axis_size("col")
    band_count = lax.axis_size("row")
    band_index = lax.axis_index("row")
    column_index = lax.axis_index("col")
    positions = jnp.arange(columns, dtype=jnp.int32)
    position_of = jnp.sum(
        jnp.where(column_order[:, None] == positions[None, :], positions[:, None], 0), axis=0
    )
    home_column = jnp.sum(jnp.where(positions == column_index, column_order, 0))
    first_row = band_index * band_rows
    own_blocks = (first_row + jnp.arange(band_rows, dtype=jnp.int32)) * columns + home_column
    band_pairs = near_pairs.shape[1] // band_count
    share = band_pairs // columns
    segment = lax.dynamic_slice_in_dim(
        near_pairs, band_index * band_pairs + column_index * share, share, 1
    )
    low_blocks = segment[0]
    high_blocks = segment[1]
    targets = jnp.concatenate([own_blocks, low_blocks])
    sources = jnp.concatenate([own_blocks, high_blocks])
    lattice_cols = columns * QUAD_COLS + 1
    tiles = tile_block(
        block_geometry(vertices, panel_vertices, targets, lattice_cols),
        block_geometry(vertices, panel_vertices, sources, lattice_cols),
    )
    self_tiles = tiles[:band_rows]
    pair_tiles = tiles[band_rows:]
    low_row = low_blocks // columns - first_row
    high_row = high_blocks // columns - first_row
    low_pos = position_of[low_blocks % columns]
    high_pos = position_of[high_blocks % columns]
    slot_table = (low_row, low_pos, high_row, high_pos)
    return (self_tiles, pair_tiles, slot_table)


def near_product(block_values, prepared):
    self_tiles, pair_tiles, slot_table = prepared
    band_rows = block_values.shape[0]
    low_row, low_pos, high_row, high_pos = slot_table
    self_term = apply_tiles(block_values[:, 0], self_tiles)
    later = shifted(block_values[:REACH], "row", -1)
    source_table = lax.all_gather(
        jnp.concatenate([block_values, later], axis=0), "col", axis=1, tiled=True
    )
    to_low = apply_tiles(source_table[high_row, high_pos], pair_tiles)
    to_high = apply_transposed(source_table[low_row, low_pos], pair_tiles)
    partial_value = jnp.zeros(source_table.shape, jnp.float32)
    partial_value = partial_value.at[low_row, low_pos].add(to_low).at[high_row, high_pos].add(to_high)
    summed = jnp.sum(lax.all_to_all(partial_value, "col", 1, 1, tiled=True), axis=1)
    carried_down = shifted(summed[band_rows:], "row", 1)
    head = summed[:REACH] + carried_down
    own = jnp.concatenate([head, summed[REACH:band_rows]], axis=0)
    return (own + self_term)[:, None]


def body(charges, column_order, vertices, panel_vertices, near_pairs):
    prepared = prepare(column_order, vertices, panel_vertices, near_pairs, charges.shape[0])
    potential_one = near_product(charges, prepared)
    potential_two = near_product(potential_one, prepared)
    return (potential_one, potential_two)


def solution(mesh):
    return jax.shard_map(
        body,
        mesh=mesh,
        in_specs=(P("row", "col", None, None), P(), P(), P(), P()),
        out_specs=(P("row", "col", None, None), P("row", "col", None, None)),
        check_vma=False,
    )
```

```python
import math

import jax
import jax.numpy as jnp
import numpy as np
from jax import lax
from jax.experimental import pallas as pl
from jax.experimental.pallas import tpu as pltpu
from jax.sharding import PartitionSpec as P

PANELS = 256
REACH = 3
QUAD_ROWS = 8
QUAD_COLS = 16


def shifted(value, axis, by):
    length = lax.axis_size(axis)
    pairs = [(i, i + by) for i in range(length) if 0 <= i + by < length]
    return lax.ppermute(value, axis, pairs)


def rule_tables():
    gauss_two = np.array([-1.0, 1.0]) / math.sqrt(3.0)
    gauss_four = np.array(
        [-0.8611363115940526, -0.3399810435848563, 0.3399810435848563, 0.8611363115940526]
    )
    weight_four = np.array(
        [0.3478548451374538, 0.6521451548625461, 0.6521451548625461, 0.3478548451374538]
    )
    corner_weights = []
    point_weights = []
    for first_index in range(2):
        for second_index in range(4):
            along = 0.5 * (1.0 + gauss_two[first_index])
            across = 0.5 * (1.0 + gauss_four[second_index])
            corner_weights.append([along, (1.0 - along) * across, (1.0 - along) * (1.0 - across)])
            point_weights.append(2.0 * 0.5 * 0.5 * weight_four[second_index] * (1.0 - along))
    return (np.array(corner_weights), np.array(point_weights))


def block_corners(vertices, panel_vertices, block_ids, lattice_cols):
    patch_rows, patch_cols = QUAD_ROWS + 1, QUAD_COLS + 1
    panels = panel_vertices.reshape(3, -1, PANELS)[:, block_ids]
    lattice_row = panels // lattice_cols
    lattice_col = panels % lattice_cols
    base_row = jnp.min(lattice_row, axis=(0, 2))
    base_col = jnp.min(lattice_col, axis=(0, 2))
    local = (lattice_row - base_row[None, :, None]) * patch_cols + (
        lattice_col - base_col[None, :, None]
    )
    grid = jnp.transpose(vertices.reshape(3, -1, lattice_cols), (1, 0, 2))
    row_pick = (
        (base_row[:, None] + jnp.arange(patch_rows, dtype=jnp.int32))[:, :, None]
        == jnp.arange(grid.shape[0], dtype=jnp.int32)
    ).astype(jnp.float32)
    col_pick = (
        jnp.arange(lattice_cols, dtype=jnp.int32)[None, :, None]
        == (base_col[:, None] + jnp.arange(patch_cols, dtype=jnp.int32))[:, None, :]
    ).astype(jnp.float32)
    band = jnp.einsum("grR,Rxc->grxc", row_pick, grid, precision=lax.Precision.HIGHEST)
    patch = jnp.einsum("grxc,gcj->gxrj", band, col_pick, precision=lax.Precision.HIGHEST)
    patch = patch.reshape(block_ids.shape[0], 3, patch_rows * patch_cols)
    pick = (
        local[:, :, :, None] == jnp.arange(patch_rows * patch_cols, dtype=jnp.int32)
    ).astype(jnp.float32)
    return jnp.einsum("gxl,cgpl->gcxp", patch, pick, precision=lax.Precision.HIGHEST)


def block_geometry(vertices, panel_vertices, block_ids, lattice_cols):
    corners = block_corners(vertices, panel_vertices, block_ids, lattice_cols)
    centre = (corners[:, 0] + corners[:, 1] + corners[:, 2]) / 3.0
    first_edge = corners[:, 1] - corners[:, 0]
    second_edge = corners[:, 2] - corners[:, 0]
    normal_x = first_edge[:, 1] * second_edge[:, 2] - first_edge[:, 2] * second_edge[:, 1]
    normal_y = first_edge[:, 2] * second_edge[:, 0] - first_edge[:, 0] * second_edge[:, 2]
    normal_z = first_edge[:, 0] * second_edge[:, 1] - first_edge[:, 1] * second_edge[:, 0]
    panel_area = 0.5 * jnp.sqrt(normal_x * normal_x + normal_y * normal_y + normal_z * normal_z)
    corner_weights, _ = rule_tables()
    points = jnp.einsum(
        "kc,gcxp->gxkp",
        jnp.asarray(corner_weights, corners.dtype),
        corners,
        precision=lax.Precision.HIGHEST,
    )
    return (centre, points, panel_area)


def tile_block(target, source):
    target_centre, target_points, target_area = target
    source_centre, source_points, source_area = source
    _, point_weights = rule_tables()
    kernel_sum = jnp.zeros(
        (target_centre.shape[0], target_centre.shape[2], source_centre.shape[2]), jnp.float32
    )
    for point_index in range(8):
        weight = float(point_weights[point_index])
        distance = target_centre[:, :, :, None] - source_points[:, :, point_index, None, :]
        kernel_sum = kernel_sum + weight * lax.rsqrt(jnp.sum(distance * distance, axis=1) + 0.01)
        distance = target_points[:, :, point_index, :, None] - source_centre[:, :, None, :]
        kernel_sum = kernel_sum + weight * lax.rsqrt(jnp.sum(distance * distance, axis=1) + 0.01)
    return kernel_sum * target_area[:, :, None] * source_area[:, None, :] / (8.0 * math.pi)


def apply_tiles(source_values, tile_stack):
    return jnp.einsum("grq,gpq->grp", source_values, tile_stack, precision=lax.Precision.HIGHEST)


def apply_transposed(source_values, tile_stack):
    return jnp.einsum("grp,gpq->grq", source_values, tile_stack, precision=lax.Precision.HIGHEST)


def prepare(column_order, vertices, panel_vertices, near_pairs, band_rows):
    columns = lax.axis_size("col")
    band_count = lax.axis_size("row")
    band_index = lax.axis_index("row")
    column_index = lax.axis_index("col")
    positions = jnp.arange(columns, dtype=jnp.int32)
    position_of = jnp.sum(
        jnp.where(column_order[:, None] == positions[None, :], positions[:, None], 0), axis=0
    )
    home_column = jnp.sum(jnp.where(positions == column_index, column_order, 0))
    first_row = band_index * band_rows
    own_blocks = (first_row + jnp.arange(band_rows, dtype=jnp.int32)) * columns + home_column
    band_pairs = near_pairs.shape[1] // band_count
    share = band_pairs // columns
    segment = lax.dynamic_slice_in_dim(
        near_pairs, band_index * band_pairs + column_index * share, share, 1
    )
    low_blocks = segment[0]
    high_blocks = segment[1]
    targets = jnp.concatenate([own_blocks, low_blocks])
    sources = jnp.concatenate([own_blocks, high_blocks])
    lattice_cols = columns * QUAD_COLS + 1
    tiles = tile_block(
        block_geometry(vertices, panel_vertices, targets, lattice_cols),
        block_geometry(vertices, panel_vertices, sources, lattice_cols),
    )
    self_tiles = tiles[:band_rows]
    pair_tiles = tiles[band_rows:]
    low_row = low_blocks // columns - first_row
    high_row = high_blocks // columns - first_row
    low_pos = position_of[low_blocks % columns]
    high_pos = position_of[high_blocks % columns]
    slot_table = (low_row, low_pos, high_row, high_pos)
    return (self_tiles, pair_tiles, slot_table)


def exchange(block, gather, tag):
    columns = lax.axis_size("col")
    slot_shape = block.shape if gather else block.shape[1:]

    def kernel(block_ref, out_ref, send_sems, recv_sems, local_sem):
        band = lax.axis_index("row")
        me = lax.axis_index("col")
        barrier = pltpu.get_barrier_semaphore()
        for offset in range(1, columns):
            peer = lax.rem(me + offset, columns)
            pl.semaphore_signal(
                barrier, 1, device_id=(band, peer), device_id_type=pl.DeviceIdType.MESH
            )
        pl.semaphore_wait(barrier, columns - 1)
        copies = []
        for offset in range(1, columns):
            peer = lax.rem(me + offset, columns)
            copy = pltpu.make_async_remote_copy(
                src_ref=block_ref if gather else block_ref.at[peer],
                dst_ref=out_ref.at[me],
                send_sem=send_sems.at[offset],
                recv_sem=recv_sems.at[offset],
                device_id=(band, peer),
                device_id_type=pl.DeviceIdType.MESH,
            )
            copy.start()
            copies.append(copy)
        local = pltpu.make_async_copy(
            block_ref if gather else block_ref.at[me], out_ref.at[me], local_sem
        )
        local.start()
        for copy in copies:
            copy.wait_send()
        for copy in copies:
            copy.wait_recv()
        local.wait()

    return pl.pallas_call(
        kernel,
        out_shape=jax.ShapeDtypeStruct((columns,) + slot_shape, block.dtype),
        in_specs=[pl.BlockSpec(memory_space=pl.ANY)],
        out_specs=pl.BlockSpec(memory_space=pl.ANY),
        scratch_shapes=[
            pltpu.SemaphoreType.DMA((columns,)),
            pltpu.SemaphoreType.DMA((columns,)),
            pltpu.SemaphoreType.DMA(()),
        ],
        compiler_params=pltpu.CompilerParams(collective_id=tag, has_side_effects=True),
    )(block)


def near_product(block_values, prepared, gathered):
    self_tiles, pair_tiles, slot_table = prepared
    band_rows = block_values.shape[0]
    low_row, low_pos, high_row, high_pos = slot_table
    self_term = apply_tiles(block_values[:, 0], self_tiles)
    later = shifted(block_values[:REACH], "row", -1)
    table = jnp.concatenate([block_values, later], axis=0)[:, 0]
    if gathered:
        source_table = exchange(table, True, 0)
    else:
        source_table = jnp.moveaxis(lax.all_gather(table, "col", axis=1), 1, 0)
    to_low = apply_tiles(source_table[high_pos, high_row], pair_tiles)
    to_high = apply_transposed(source_table[low_pos, low_row], pair_tiles)
    partial_value = jnp.zeros(source_table.shape, jnp.float32)
    partial_value = partial_value.at[low_pos, low_row].add(to_low).at[high_pos, high_row].add(to_high)
    summed = jnp.sum(exchange(partial_value, False, 1), axis=0)
    carried_down = shifted(summed[band_rows:], "row", 1)
    head = summed[:REACH] + carried_down
    own = jnp.concatenate([head, summed[REACH:band_rows]], axis=0)
    return (own + self_term)[:, None]


def body(charges, column_order, vertices, panel_vertices, near_pairs):
    prepared = prepare(column_order, vertices, panel_vertices, near_pairs, charges.shape[0])
    potential_one = near_product(charges, prepared, False)
    potential_two = near_product(potential_one, prepared, True)
    return (potential_one, potential_two)


def solution(mesh):
    return jax.shard_map(
        body,
        mesh=mesh,
        in_specs=(P("row", "col", None, None), P(), P(), P(), P()),
        out_specs=(P("row", "col", None, None), P("row", "col", None, None)),
        check_vma=False,
    )
```

```python
import math

import jax
import jax.numpy as jnp
import numpy as np
from jax import lax
from jax.experimental import pallas as pl
from jax.experimental.pallas import tpu as pltpu
from jax.sharding import PartitionSpec as P

PANELS = 256
REACH = 3
QUAD_ROWS = 8
QUAD_COLS = 16


def shifted(value, axis, by):
    length = lax.axis_size(axis)
    pairs = [(i, i + by) for i in range(length) if 0 <= i + by < length]
    return lax.ppermute(value, axis, pairs)


def rule_tables():
    gauss_two = np.array([-1.0, 1.0]) / math.sqrt(3.0)
    gauss_four = np.array(
        [-0.8611363115940526, -0.3399810435848563, 0.3399810435848563, 0.8611363115940526]
    )
    weight_four = np.array(
        [0.3478548451374538, 0.6521451548625461, 0.6521451548625461, 0.3478548451374538]
    )
    corner_weights = []
    point_weights = []
    for first_index in range(2):
        for second_index in range(4):
            along = 0.5 * (1.0 + gauss_two[first_index])
            across = 0.5 * (1.0 + gauss_four[second_index])
            corner_weights.append([along, (1.0 - along) * across, (1.0 - along) * (1.0 - across)])
            point_weights.append(2.0 * 0.5 * 0.5 * weight_four[second_index] * (1.0 - along))
    return (np.array(corner_weights), np.array(point_weights))


def block_corners(vertices, panel_vertices, block_ids, lattice_cols):
    patch_rows, patch_cols = QUAD_ROWS + 1, QUAD_COLS + 1
    panels = panel_vertices.reshape(3, -1, PANELS)[:, block_ids]
    lattice_row = panels // lattice_cols
    lattice_col = panels % lattice_cols
    base_row = jnp.min(lattice_row, axis=(0, 2))
    base_col = jnp.min(lattice_col, axis=(0, 2))
    local = (lattice_row - base_row[None, :, None]) * patch_cols + (
        lattice_col - base_col[None, :, None]
    )
    grid = jnp.transpose(vertices.reshape(3, -1, lattice_cols), (1, 0, 2))
    row_pick = (
        (base_row[:, None] + jnp.arange(patch_rows, dtype=jnp.int32))[:, :, None]
        == jnp.arange(grid.shape[0], dtype=jnp.int32)
    ).astype(jnp.float32)
    col_pick = (
        jnp.arange(lattice_cols, dtype=jnp.int32)[None, :, None]
        == (base_col[:, None] + jnp.arange(patch_cols, dtype=jnp.int32))[:, None, :]
    ).astype(jnp.float32)
    band = jnp.einsum("grR,Rxc->grxc", row_pick, grid, precision=lax.Precision.HIGHEST)
    patch = jnp.einsum("grxc,gcj->gxrj", band, col_pick, precision=lax.Precision.HIGHEST)
    patch = patch.reshape(block_ids.shape[0], 3, patch_rows * patch_cols)
    pick = (
        local[:, :, :, None] == jnp.arange(patch_rows * patch_cols, dtype=jnp.int32)
    ).astype(jnp.float32)
    return jnp.einsum("gxl,cgpl->gcxp", patch, pick, precision=lax.Precision.HIGHEST)


def block_geometry(vertices, panel_vertices, block_ids, lattice_cols):
    corners = block_corners(vertices, panel_vertices, block_ids, lattice_cols)
    centre = (corners[:, 0] + corners[:, 1] + corners[:, 2]) / 3.0
    first_edge = corners[:, 1] - corners[:, 0]
    second_edge = corners[:, 2] - corners[:, 0]
    normal_x = first_edge[:, 1] * second_edge[:, 2] - first_edge[:, 2] * second_edge[:, 1]
    normal_y = first_edge[:, 2] * second_edge[:, 0] - first_edge[:, 0] * second_edge[:, 2]
    normal_z = first_edge[:, 0] * second_edge[:, 1] - first_edge[:, 1] * second_edge[:, 0]
    panel_area = 0.5 * jnp.sqrt(normal_x * normal_x + normal_y * normal_y + normal_z * normal_z)
    corner_weights, _ = rule_tables()
    points = jnp.einsum(
        "kc,gcxp->gxkp",
        jnp.asarray(corner_weights, corners.dtype),
        corners,
        precision=lax.Precision.HIGHEST,
    )
    return (centre, points, panel_area)


def tile_block(target, source):
    target_centre, target_points, target_area = target
    source_centre, source_points, source_area = source
    _, point_weights = rule_tables()
    kernel_sum = jnp.zeros(
        (target_centre.shape[0], target_centre.shape[2], source_centre.shape[2]), jnp.float32
    )
    for point_index in range(8):
        weight = float(point_weights[point_index])
        distance = target_centre[:, :, :, None] - source_points[:, :, point_index, None, :]
        kernel_sum = kernel_sum + weight * lax.rsqrt(jnp.sum(distance * distance, axis=1) + 0.01)
        distance = target_points[:, :, point_index, :, None] - source_centre[:, :, None, :]
        kernel_sum = kernel_sum + weight * lax.rsqrt(jnp.sum(distance * distance, axis=1) + 0.01)
    return kernel_sum * target_area[:, :, None] * source_area[:, None, :] / (8.0 * math.pi)


def apply_tiles(source_values, tile_stack):
    return jnp.einsum("grq,gpq->grp", source_values, tile_stack, precision=lax.Precision.HIGHEST)


def apply_transposed(source_values, tile_stack):
    return jnp.einsum("grp,gpq->grq", source_values, tile_stack, precision=lax.Precision.HIGHEST)


def prepare(column_order, vertices, panel_vertices, near_pairs, band_rows):
    columns = lax.axis_size("col")
    band_count = lax.axis_size("row")
    band_index = lax.axis_index("row")
    column_index = lax.axis_index("col")
    positions = jnp.arange(columns, dtype=jnp.int32)
    position_of = jnp.sum(
        jnp.where(column_order[:, None] == positions[None, :], positions[:, None], 0), axis=0
    )
    home_column = jnp.sum(jnp.where(positions == column_index, column_order, 0))
    first_row = band_index * band_rows
    own_blocks = (first_row + jnp.arange(band_rows, dtype=jnp.int32)) * columns + home_column
    band_pairs = near_pairs.shape[1] // band_count
    share = band_pairs // columns
    segment = lax.dynamic_slice_in_dim(
        near_pairs, band_index * band_pairs + column_index * share, share, 1
    )
    low_blocks = segment[0]
    high_blocks = segment[1]
    targets = jnp.concatenate([own_blocks, low_blocks])
    sources = jnp.concatenate([own_blocks, high_blocks])
    lattice_cols = columns * QUAD_COLS + 1
    tiles = tile_block(
        block_geometry(vertices, panel_vertices, targets, lattice_cols),
        block_geometry(vertices, panel_vertices, sources, lattice_cols),
    )
    self_tiles = tiles[:band_rows]
    pair_tiles = tiles[band_rows:]
    low_row = low_blocks // columns - first_row
    high_row = high_blocks // columns - first_row
    low_pos = position_of[low_blocks % columns]
    high_pos = position_of[high_blocks % columns]
    slot_table = (low_row, low_pos, high_row, high_pos)
    return (self_tiles, pair_tiles, slot_table)


def exchange(block, gather, tag):
    columns = lax.axis_size("col")
    slot_shape = block.shape if gather else block.shape[1:]

    def kernel(block_ref, out_ref, send_sems, recv_sems, local_sem):
        band = lax.axis_index("row")
        me = lax.axis_index("col")
        barrier = pltpu.get_barrier_semaphore()
        for offset in range(1, columns):
            peer = lax.rem(me + offset, columns)
            pl.semaphore_signal(
                barrier, 1, device_id=(band, peer), device_id_type=pl.DeviceIdType.MESH
            )
        pl.semaphore_wait(barrier, columns - 1)
        copies = []
        for offset in range(1, columns):
            peer = lax.rem(me + offset, columns)
            copy = pltpu.make_async_remote_copy(
                src_ref=block_ref if gather else block_ref.at[peer],
                dst_ref=out_ref.at[me],
                send_sem=send_sems.at[offset],
                recv_sem=recv_sems.at[offset],
                device_id=(band, peer),
                device_id_type=pl.DeviceIdType.MESH,
            )
            copy.start()
            copies.append(copy)
        local = pltpu.make_async_copy(
            block_ref if gather else block_ref.at[me], out_ref.at[me], local_sem
        )
        local.start()
        for copy in copies:
            copy.wait_send()
        for copy in copies:
            copy.wait_recv()
        local.wait()

    return pl.pallas_call(
        kernel,
        out_shape=jax.ShapeDtypeStruct((columns,) + slot_shape, block.dtype),
        in_specs=[pl.BlockSpec(memory_space=pltpu.VMEM)],
        out_specs=pl.BlockSpec(memory_space=pltpu.VMEM),
        scratch_shapes=[
            pltpu.SemaphoreType.DMA((columns,)),
            pltpu.SemaphoreType.DMA((columns,)),
            pltpu.SemaphoreType.DMA(()),
        ],
        compiler_params=pltpu.CompilerParams(collective_id=tag, has_side_effects=True),
    )(block)


def near_product(block_values, prepared, gathered):
    self_tiles, pair_tiles, slot_table = prepared
    band_rows = block_values.shape[0]
    low_row, low_pos, high_row, high_pos = slot_table
    self_term = apply_tiles(block_values[:, 0], self_tiles)
    later = shifted(block_values[:REACH], "row", -1)
    table = jnp.concatenate([block_values, later], axis=0)[:, 0]
    if gathered:
        source_table = exchange(table, True, 0)
    else:
        source_table = jnp.moveaxis(lax.all_gather(table, "col", axis=1), 1, 0)
    to_low = apply_tiles(source_table[high_pos, high_row], pair_tiles)
    to_high = apply_transposed(source_table[low_pos, low_row], pair_tiles)
    partial_value = jnp.zeros(source_table.shape, jnp.float32)
    partial_value = partial_value.at[low_pos, low_row].add(to_low).at[high_pos, high_row].add(to_high)
    summed = jnp.sum(exchange(partial_value, False, 1), axis=0)
    carried_down = shifted(summed[band_rows:], "row", 1)
    head = summed[:REACH] + carried_down
    own = jnp.concatenate([head, summed[REACH:band_rows]], axis=0)
    return (own + self_term)[:, None]


def body(charges, column_order, vertices, panel_vertices, near_pairs):
    prepared = prepare(column_order, vertices, panel_vertices, near_pairs, charges.shape[0])
    potential_one = near_product(charges, prepared, False)
    potential_two = near_product(potential_one, prepared, True)
    return (potential_one, potential_two)


def solution(mesh):
    return jax.shard_map(
        body,
        mesh=mesh,
        in_specs=(P("row", "col", None, None), P(), P(), P(), P()),
        out_specs=(P("row", "col", None, None), P("row", "col", None, None)),
        check_vma=False,
    )
```

```python
import math

import jax
import jax.numpy as jnp
import numpy as np
from jax import lax
from jax.experimental import pallas as pl
from jax.experimental.pallas import tpu as pltpu
from jax.sharding import PartitionSpec as P

PANELS = 256
REACH = 3
QUAD_ROWS = 8
QUAD_COLS = 16


def shifted(value, axis, by):
    length = lax.axis_size(axis)
    pairs = [(i, i + by) for i in range(length) if 0 <= i + by < length]
    return lax.ppermute(value, axis, pairs)


def rule_tables():
    gauss_two = np.array([-1.0, 1.0]) / math.sqrt(3.0)
    gauss_four = np.array(
        [-0.8611363115940526, -0.3399810435848563, 0.3399810435848563, 0.8611363115940526]
    )
    weight_four = np.array(
        [0.3478548451374538, 0.6521451548625461, 0.6521451548625461, 0.3478548451374538]
    )
    corner_weights = []
    point_weights = []
    for first_index in range(2):
        for second_index in range(4):
            along = 0.5 * (1.0 + gauss_two[first_index])
            across = 0.5 * (1.0 + gauss_four[second_index])
            corner_weights.append([along, (1.0 - along) * across, (1.0 - along) * (1.0 - across)])
            point_weights.append(2.0 * 0.5 * 0.5 * weight_four[second_index] * (1.0 - along))
    return (np.array(corner_weights), np.array(point_weights))


def block_corners(vertices, panel_vertices, block_ids, lattice_cols):
    patch_rows, patch_cols = QUAD_ROWS + 1, QUAD_COLS + 1
    panels = panel_vertices.reshape(3, -1, PANELS)[:, block_ids]
    lattice_row = panels // lattice_cols
    lattice_col = panels % lattice_cols
    base_row = jnp.min(lattice_row, axis=(0, 2))
    base_col = jnp.min(lattice_col, axis=(0, 2))
    local = (lattice_row - base_row[None, :, None]) * patch_cols + (
        lattice_col - base_col[None, :, None]
    )
    grid = jnp.transpose(vertices.reshape(3, -1, lattice_cols), (1, 0, 2))
    row_pick = (
        (base_row[:, None] + jnp.arange(patch_rows, dtype=jnp.int32))[:, :, None]
        == jnp.arange(grid.shape[0], dtype=jnp.int32)
    ).astype(jnp.float32)
    col_pick = (
        jnp.arange(lattice_cols, dtype=jnp.int32)[None, :, None]
        == (base_col[:, None] + jnp.arange(patch_cols, dtype=jnp.int32))[:, None, :]
    ).astype(jnp.float32)
    band = jnp.einsum("grR,Rxc->grxc", row_pick, grid, precision=lax.Precision.HIGHEST)
    patch = jnp.einsum("grxc,gcj->gxrj", band, col_pick, precision=lax.Precision.HIGHEST)
    patch = patch.reshape(block_ids.shape[0], 3, patch_rows * patch_cols)
    pick = (
        local[:, :, :, None] == jnp.arange(patch_rows * patch_cols, dtype=jnp.int32)
    ).astype(jnp.float32)
    return jnp.einsum("gxl,cgpl->gcxp", patch, pick, precision=lax.Precision.HIGHEST)


def block_geometry(vertices, panel_vertices, block_ids, lattice_cols):
    corners = block_corners(vertices, panel_vertices, block_ids, lattice_cols)
    centre = (corners[:, 0] + corners[:, 1] + corners[:, 2]) / 3.0
    first_edge = corners[:, 1] - corners[:, 0]
    second_edge = corners[:, 2] - corners[:, 0]
    normal_x = first_edge[:, 1] * second_edge[:, 2] - first_edge[:, 2] * second_edge[:, 1]
    normal_y = first_edge[:, 2] * second_edge[:, 0] - first_edge[:, 0] * second_edge[:, 2]
    normal_z = first_edge[:, 0] * second_edge[:, 1] - first_edge[:, 1] * second_edge[:, 0]
    panel_area = 0.5 * jnp.sqrt(normal_x * normal_x + normal_y * normal_y + normal_z * normal_z)
    corner_weights, _ = rule_tables()
    points = jnp.einsum(
        "kc,gcxp->gxkp",
        jnp.asarray(corner_weights, corners.dtype),
        corners,
        precision=lax.Precision.HIGHEST,
    )
    return (centre, points, panel_area)


def tile_block(target, source):
    target_centre, target_points, target_area = target
    source_centre, source_points, source_area = source
    _, point_weights = rule_tables()
    kernel_sum = jnp.zeros(
        (target_centre.shape[0], target_centre.shape[2], source_centre.shape[2]), jnp.float32
    )
    for point_index in range(8):
        weight = float(point_weights[point_index])
        distance = target_centre[:, :, :, None] - source_points[:, :, point_index, None, :]
        kernel_sum = kernel_sum + weight * lax.rsqrt(jnp.sum(distance * distance, axis=1) + 0.01)
        distance = target_points[:, :, point_index, :, None] - source_centre[:, :, None, :]
        kernel_sum = kernel_sum + weight * lax.rsqrt(jnp.sum(distance * distance, axis=1) + 0.01)
    return kernel_sum * target_area[:, :, None] * source_area[:, None, :] / (8.0 * math.pi)


def self_tile_block(geometry):
    centre, points, area = geometry
    _, point_weights = rule_tables()
    half_sum = jnp.zeros((centre.shape[0], centre.shape[2], centre.shape[2]), jnp.float32)
    for point_index in range(8):
        weight = float(point_weights[point_index])
        distance = centre[:, :, :, None] - points[:, :, point_index, None, :]
        half_sum = half_sum + weight * lax.rsqrt(jnp.sum(distance * distance, axis=1) + 0.01)
    kernel_sum = half_sum + jnp.swapaxes(half_sum, 1, 2)
    return kernel_sum * area[:, :, None] * area[:, None, :] / (8.0 * math.pi)


def apply_tiles(source_values, tile_stack):
    return jnp.einsum("grq,gpq->grp", source_values, tile_stack, precision=lax.Precision.HIGHEST)


def apply_transposed(source_values, tile_stack):
    return jnp.einsum("grp,gpq->grq", source_values, tile_stack, precision=lax.Precision.HIGHEST)


def prepare(column_order, vertices, panel_vertices, near_pairs, band_rows):
    columns = lax.axis_size("col")
    band_count = lax.axis_size("row")
    band_index = lax.axis_index("row")
    column_index = lax.axis_index("col")
    positions = jnp.arange(columns, dtype=jnp.int32)
    position_of = jnp.sum(
        jnp.where(column_order[:, None] == positions[None, :], positions[:, None], 0), axis=0
    )
    home_column = jnp.sum(jnp.where(positions == column_index, column_order, 0))
    first_row = band_index * band_rows
    own_blocks = (first_row + jnp.arange(band_rows, dtype=jnp.int32)) * columns + home_column
    band_pairs = near_pairs.shape[1] // band_count
    share = band_pairs // columns
    segment = lax.dynamic_slice_in_dim(
        near_pairs, band_index * band_pairs + column_index * share, share, 1
    )
    low_blocks = segment[0]
    high_blocks = segment[1]
    targets = jnp.concatenate([own_blocks, low_blocks])
    lattice_cols = columns * QUAD_COLS + 1
    target_geometry = block_geometry(vertices, panel_vertices, targets, lattice_cols)
    source_geometry = block_geometry(vertices, panel_vertices, high_blocks, lattice_cols)
    self_tiles = self_tile_block([part[:band_rows] for part in target_geometry])
    pair_tiles = tile_block([part[band_rows:] for part in target_geometry], source_geometry)
    low_row = low_blocks // columns - first_row
    high_row = high_blocks // columns - first_row
    low_pos = position_of[low_blocks % columns]
    high_pos = position_of[high_blocks % columns]
    slot_table = (low_row, low_pos, high_row, high_pos)
    return (self_tiles, pair_tiles, slot_table)


def near_product(block_values, prepared, split):
    self_tiles, pair_tiles, slot_table = prepared
    band_rows = block_values.shape[0]
    low_row, low_pos, high_row, high_pos = slot_table
    self_term = apply_tiles(block_values[:, 0], self_tiles)
    columns = lax.axis_size("col")
    later = shifted(block_values[:REACH, 0], "row", -1)
    if split:
        own_table = jnp.moveaxis(lax.all_gather(block_values[:, 0], "col", axis=1), 1, 0)
        spread = jnp.broadcast_to(later[None], (columns,) + later.shape)
        later_table = lax.all_to_all(spread, "col", 0, 0, tiled=True)
        source_table = jnp.concatenate([own_table, later_table], axis=1)
    else:
        table = jnp.concatenate([block_values[:, 0], later], axis=0)
        source_table = jnp.moveaxis(lax.all_gather(table, "col", axis=1), 1, 0)
    to_low = apply_tiles(source_table[high_pos, high_row], pair_tiles)
    to_high = apply_transposed(source_table[low_pos, low_row], pair_tiles)
    partial_value = jnp.zeros(source_table.shape, jnp.float32)
    partial_value = partial_value.at[low_pos, low_row].add(to_low).at[high_pos, high_row].add(to_high)
    own_sum = lax.psum_scatter(
        partial_value[:, :band_rows], "col", scatter_dimension=0, tiled=True
    )[0]
    later_sum = jnp.sum(
        lax.all_to_all(partial_value[:, band_rows:], "col", 0, 0, tiled=True), axis=0
    )
    carried_down = shifted(later_sum, "row", 1)
    head = own_sum[:REACH] + carried_down
    own = jnp.concatenate([head, own_sum[REACH:band_rows]], axis=0)
    return (own + self_term)[:, None]


def body(charges, column_order, vertices, panel_vertices, near_pairs):
    prepared = prepare(column_order, vertices, panel_vertices, near_pairs, charges.shape[0])
    potential_one = near_product(charges, prepared, False)
    potential_two = near_product(potential_one, prepared, True)
    return (potential_one, potential_two)


def solution(mesh):
    return jax.shard_map(
        body,
        mesh=mesh,
        in_specs=(P("row", "col", None, None), P(), P(), P(), P()),
        out_specs=(P("row", "col", None, None), P("row", "col", None, None)),
        check_vma=False,
    )
```

```python
import math

import jax
import jax.numpy as jnp
import numpy as np
from jax import lax
from jax.experimental import pallas as pl
from jax.experimental.pallas import tpu as pltpu
from jax.sharding import PartitionSpec as P

PANELS = 256
REACH = 3
QUAD_ROWS = 8
QUAD_COLS = 16


def shifted(value, axis, by):
    length = lax.axis_size(axis)
    pairs = [(i, i + by) for i in range(length) if 0 <= i + by < length]
    return lax.ppermute(value, axis, pairs)


def rule_tables():
    gauss_two = np.array([-1.0, 1.0]) / math.sqrt(3.0)
    gauss_four = np.array(
        [-0.8611363115940526, -0.3399810435848563, 0.3399810435848563, 0.8611363115940526]
    )
    weight_four = np.array(
        [0.3478548451374538, 0.6521451548625461, 0.6521451548625461, 0.3478548451374538]
    )
    corner_weights = []
    point_weights = []
    for first_index in range(2):
        for second_index in range(4):
            along = 0.5 * (1.0 + gauss_two[first_index])
            across = 0.5 * (1.0 + gauss_four[second_index])
            corner_weights.append([along, (1.0 - along) * across, (1.0 - along) * (1.0 - across)])
            point_weights.append(2.0 * 0.5 * 0.5 * weight_four[second_index] * (1.0 - along))
    return (np.array(corner_weights), np.array(point_weights))


def block_corners(vertices, panel_vertices, block_ids, lattice_cols):
    patch_rows, patch_cols = QUAD_ROWS + 1, QUAD_COLS + 1
    panels = panel_vertices.reshape(3, -1, PANELS)[:, block_ids]
    lattice_row = panels // lattice_cols
    lattice_col = panels % lattice_cols
    base_row = jnp.min(lattice_row, axis=(0, 2))
    base_col = jnp.min(lattice_col, axis=(0, 2))
    local = (lattice_row - base_row[None, :, None]) * patch_cols + (
        lattice_col - base_col[None, :, None]
    )
    grid = jnp.transpose(vertices.reshape(3, -1, lattice_cols), (1, 0, 2))
    row_pick = (
        (base_row[:, None] + jnp.arange(patch_rows, dtype=jnp.int32))[:, :, None]
        == jnp.arange(grid.shape[0], dtype=jnp.int32)
    ).astype(jnp.float32)
    col_pick = (
        jnp.arange(lattice_cols, dtype=jnp.int32)[None, :, None]
        == (base_col[:, None] + jnp.arange(patch_cols, dtype=jnp.int32))[:, None, :]
    ).astype(jnp.float32)
    band = jnp.einsum("grR,Rxc->grxc", row_pick, grid, precision=lax.Precision.HIGHEST)
    patch = jnp.einsum("grxc,gcj->gxrj", band, col_pick, precision=lax.Precision.HIGHEST)
    patch = patch.reshape(block_ids.shape[0], 3, patch_rows * patch_cols)
    pick = (
        local[:, :, :, None] == jnp.arange(patch_rows * patch_cols, dtype=jnp.int32)
    ).astype(jnp.float32)
    return jnp.einsum("gxl,cgpl->gcxp", patch, pick, precision=lax.Precision.HIGHEST)


def block_geometry(vertices, panel_vertices, block_ids, lattice_cols):
    corners = block_corners(vertices, panel_vertices, block_ids, lattice_cols)
    centre = (corners[:, 0] + corners[:, 1] + corners[:, 2]) / 3.0
    first_edge = corners[:, 1] - corners[:, 0]
    second_edge = corners[:, 2] - corners[:, 0]
    normal_x = first_edge[:, 1] * second_edge[:, 2] - first_edge[:, 2] * second_edge[:, 1]
    normal_y = first_edge[:, 2] * second_edge[:, 0] - first_edge[:, 0] * second_edge[:, 2]
    normal_z = first_edge[:, 0] * second_edge[:, 1] - first_edge[:, 1] * second_edge[:, 0]
    panel_area = 0.5 * jnp.sqrt(normal_x * normal_x + normal_y * normal_y + normal_z * normal_z)
    corner_weights, _ = rule_tables()
    points = jnp.einsum(
        "kc,gcxp->gxkp",
        jnp.asarray(corner_weights, corners.dtype),
        corners,
        precision=lax.Precision.HIGHEST,
    )
    return (centre, points, panel_area)


def tile_block(target, source):
    target_centre, target_points, target_area = target
    source_centre, source_points, source_area = source
    _, point_weights = rule_tables()
    kernel_sum = jnp.zeros(
        (target_centre.shape[0], target_centre.shape[2], source_centre.shape[2]), jnp.float32
    )
    for point_index in range(8):
        weight = float(point_weights[point_index])
        distance = target_centre[:, :, :, None] - source_points[:, :, point_index, None, :]
        kernel_sum = kernel_sum + weight * lax.rsqrt(jnp.sum(distance * distance, axis=1) + 0.01)
        distance = target_points[:, :, point_index, :, None] - source_centre[:, :, None, :]
        kernel_sum = kernel_sum + weight * lax.rsqrt(jnp.sum(distance * distance, axis=1) + 0.01)
    return kernel_sum * target_area[:, :, None] * source_area[:, None, :] / (8.0 * math.pi)


def self_tile_block(geometry):
    centre, points, area = geometry
    _, point_weights = rule_tables()
    half_sum = jnp.zeros((centre.shape[0], centre.shape[2], centre.shape[2]), jnp.float32)
    for point_index in range(8):
        weight = float(point_weights[point_index])
        distance = centre[:, :, :, None] - points[:, :, point_index, None, :]
        half_sum = half_sum + weight * lax.rsqrt(jnp.sum(distance * distance, axis=1) + 0.01)
    kernel_sum = half_sum + jnp.swapaxes(half_sum, 1, 2)
    return kernel_sum * area[:, :, None] * area[:, None, :] / (8.0 * math.pi)


def apply_tiles(source_values, tile_stack):
    return jnp.einsum("grq,gpq->grp", source_values, tile_stack, precision=lax.Precision.HIGHEST)


def apply_transposed(source_values, tile_stack):
    return jnp.einsum("grp,gpq->grq", source_values, tile_stack, precision=lax.Precision.HIGHEST)


def prepare(column_order, vertices, panel_vertices, near_pairs, band_rows):
    columns = lax.axis_size("col")
    band_count = lax.axis_size("row")
    band_index = lax.axis_index("row")
    column_index = lax.axis_index("col")
    positions = jnp.arange(columns, dtype=jnp.int32)
    position_of = jnp.sum(
        jnp.where(column_order[:, None] == positions[None, :], positions[:, None], 0), axis=0
    )
    home_column = jnp.sum(jnp.where(positions == column_index, column_order, 0))
    first_row = band_index * band_rows
    own_blocks = (first_row + jnp.arange(band_rows, dtype=jnp.int32)) * columns + home_column
    band_pairs = near_pairs.shape[1] // band_count
    share = band_pairs // columns
    segment = lax.dynamic_slice_in_dim(
        near_pairs, band_index * band_pairs + column_index * share, share, 1
    )
    low_blocks = segment[0]
    high_blocks = segment[1]
    targets = jnp.concatenate([own_blocks, low_blocks])
    lattice_cols = columns * QUAD_COLS + 1
    target_geometry = block_geometry(vertices, panel_vertices, targets, lattice_cols)
    source_geometry = block_geometry(vertices, panel_vertices, high_blocks, lattice_cols)
    self_tiles = self_tile_block([part[:band_rows] for part in target_geometry])
    pair_tiles = tile_block([part[band_rows:] for part in target_geometry], source_geometry)
    low_row = low_blocks // columns - first_row
    high_row = high_blocks // columns - first_row
    low_pos = position_of[low_blocks % columns]
    high_pos = position_of[high_blocks % columns]
    slot_table = (low_row, low_pos, high_row, high_pos)
    return (self_tiles, pair_tiles, slot_table)


def near_product(block_values, prepared):
    self_tiles, pair_tiles, slot_table = prepared
    band_rows = block_values.shape[0]
    low_row, low_pos, high_row, high_pos = slot_table
    self_term = apply_tiles(block_values[:, 0], self_tiles)
    later = shifted(block_values[:REACH], "row", -1)
    source_table = lax.all_gather(
        jnp.concatenate([block_values, later], axis=0), "col", axis=1, tiled=True
    )
    to_low = apply_tiles(source_table[high_row, high_pos], pair_tiles)
    to_high = apply_transposed(source_table[low_row, low_pos], pair_tiles)
    partial_value = jnp.zeros(source_table.shape, jnp.float32)
    partial_value = partial_value.at[low_row, low_pos].add(to_low).at[high_row, high_pos].add(to_high)
    summed = jnp.sum(lax.all_to_all(partial_value, "col", 1, 1, tiled=True), axis=1)
    carried_down = shifted(summed[band_rows:], "row", 1)
    head = summed[:REACH] + carried_down
    own = jnp.concatenate([head, summed[REACH:band_rows]], axis=0)
    return (own + self_term)[:, None]


def body(charges, column_order, vertices, panel_vertices, near_pairs):
    prepared = prepare(column_order, vertices, panel_vertices, near_pairs, charges.shape[0])
    potential_one = near_product(charges, prepared)
    potential_two = near_product(potential_one, prepared)
    return (potential_one, potential_two)


def solution(mesh):
    return jax.shard_map(
        body,
        mesh=mesh,
        in_specs=(P("row", "col", None, None), P(), P(), P(), P()),
        out_specs=(P("row", "col", None, None), P("row", "col", None, None)),
        check_vma=False,
    )
```

```python
import math

import jax
import jax.numpy as jnp
import numpy as np
from jax import lax
from jax.experimental import pallas as pl
from jax.experimental.pallas import tpu as pltpu
from jax.sharding import PartitionSpec as P

PANELS = 256
REACH = 3
QUAD_ROWS = 8
QUAD_COLS = 16


def shifted(value, axis, by):
    length = lax.axis_size(axis)
    pairs = [(i, i + by) for i in range(length) if 0 <= i + by < length]
    return lax.ppermute(value, axis, pairs)


def rule_tables():
    gauss_two = np.array([-1.0, 1.0]) / math.sqrt(3.0)
    gauss_four = np.array(
        [-0.8611363115940526, -0.3399810435848563, 0.3399810435848563, 0.8611363115940526]
    )
    weight_four = np.array(
        [0.3478548451374538, 0.6521451548625461, 0.6521451548625461, 0.3478548451374538]
    )
    corner_weights = []
    point_weights = []
    for first_index in range(2):
        for second_index in range(4):
            along = 0.5 * (1.0 + gauss_two[first_index])
            across = 0.5 * (1.0 + gauss_four[second_index])
            corner_weights.append([along, (1.0 - along) * across, (1.0 - along) * (1.0 - across)])
            point_weights.append(2.0 * 0.5 * 0.5 * weight_four[second_index] * (1.0 - along))
    return (np.array(corner_weights), np.array(point_weights))


def block_corners(vertices, panel_vertices, block_ids, lattice_cols):
    patch_rows, patch_cols = QUAD_ROWS + 1, QUAD_COLS + 1
    panels = panel_vertices.reshape(3, -1, PANELS)[:, block_ids]
    lattice_row = panels // lattice_cols
    lattice_col = panels % lattice_cols
    base_row = jnp.min(lattice_row, axis=(0, 2))
    base_col = jnp.min(lattice_col, axis=(0, 2))
    local = (lattice_row - base_row[None, :, None]) * patch_cols + (
        lattice_col - base_col[None, :, None]
    )
    grid = jnp.transpose(vertices.reshape(3, -1, lattice_cols), (1, 0, 2))
    row_pick = (
        (base_row[:, None] + jnp.arange(patch_rows, dtype=jnp.int32))[:, :, None]
        == jnp.arange(grid.shape[0], dtype=jnp.int32)
    ).astype(jnp.float32)
    col_pick = (
        jnp.arange(lattice_cols, dtype=jnp.int32)[None, :, None]
        == (base_col[:, None] + jnp.arange(patch_cols, dtype=jnp.int32))[:, None, :]
    ).astype(jnp.float32)
    band = jnp.einsum("grR,Rxc->grxc", row_pick, grid, precision=lax.Precision.HIGHEST)
    patch = jnp.einsum("grxc,gcj->gxrj", band, col_pick, precision=lax.Precision.HIGHEST)
    patch = patch.reshape(block_ids.shape[0], 3, patch_rows * patch_cols)
    pick = (
        local[:, :, :, None] == jnp.arange(patch_rows * patch_cols, dtype=jnp.int32)
    ).astype(jnp.float32)
    return jnp.einsum("gxl,cgpl->gcxp", patch, pick, precision=lax.Precision.HIGHEST)


def block_geometry(vertices, panel_vertices, block_ids, lattice_cols):
    corners = block_corners(vertices, panel_vertices, block_ids, lattice_cols)
    centre = (corners[:, 0] + corners[:, 1] + corners[:, 2]) / 3.0
    first_edge = corners[:, 1] - corners[:, 0]
    second_edge = corners[:, 2] - corners[:, 0]
    normal_x = first_edge[:, 1] * second_edge[:, 2] - first_edge[:, 2] * second_edge[:, 1]
    normal_y = first_edge[:, 2] * second_edge[:, 0] - first_edge[:, 0] * second_edge[:, 2]
    normal_z = first_edge[:, 0] * second_edge[:, 1] - first_edge[:, 1] * second_edge[:, 0]
    panel_area = 0.5 * jnp.sqrt(normal_x * normal_x + normal_y * normal_y + normal_z * normal_z)
    corner_weights, _ = rule_tables()
    points = jnp.einsum(
        "kc,gcxp->gxkp",
        jnp.asarray(corner_weights, corners.dtype),
        corners,
        precision=lax.Precision.HIGHEST,
    )
    return (centre, points, panel_area)


def tile_block(target, source):
    target_centre, target_points, target_area = target
    source_centre, source_points, source_area = source
    _, point_weights = rule_tables()
    kernel_sum = jnp.zeros(
        (target_centre.shape[0], target_centre.shape[2], source_centre.shape[2]), jnp.float32
    )
    for point_index in range(8):
        weight = float(point_weights[point_index])
        distance = target_centre[:, :, :, None] - source_points[:, :, point_index, None, :]
        kernel_sum = kernel_sum + weight * lax.rsqrt(jnp.sum(distance * distance, axis=1) + 0.01)
        distance = target_points[:, :, point_index, :, None] - source_centre[:, :, None, :]
        kernel_sum = kernel_sum + weight * lax.rsqrt(jnp.sum(distance * distance, axis=1) + 0.01)
    return kernel_sum * target_area[:, :, None] * source_area[:, None, :] / (8.0 * math.pi)


def self_tile_block(geometry):
    centre, points, area = geometry
    _, point_weights = rule_tables()
    half_sum = jnp.zeros((centre.shape[0], centre.shape[2], centre.shape[2]), jnp.float32)
    for point_index in range(8):
        weight = float(point_weights[point_index])
        distance = centre[:, :, :, None] - points[:, :, point_index, None, :]
        half_sum = half_sum + weight * lax.rsqrt(jnp.sum(distance * distance, axis=1) + 0.01)
    kernel_sum = half_sum + jnp.swapaxes(half_sum, 1, 2)
    return kernel_sum * area[:, :, None] * area[:, None, :] / (8.0 * math.pi)


def apply_tiles(source_values, tile_stack):
    return jnp.einsum("grq,gpq->grp", source_values, tile_stack, precision=lax.Precision.HIGHEST)


def apply_transposed(source_values, tile_stack):
    return jnp.einsum("grp,gpq->grq", source_values, tile_stack, precision=lax.Precision.HIGHEST)


def prepare(column_order, vertices, panel_vertices, near_pairs, band_rows):
    columns = lax.axis_size("col")
    band_count = lax.axis_size("row")
    band_index = lax.axis_index("row")
    column_index = lax.axis_index("col")
    positions = jnp.arange(columns, dtype=jnp.int32)
    position_of = jnp.sum(
        jnp.where(column_order[:, None] == positions[None, :], positions[:, None], 0), axis=0
    )
    home_column = jnp.sum(jnp.where(positions == column_index, column_order, 0))
    first_row = band_index * band_rows
    own_blocks = (first_row + jnp.arange(band_rows, dtype=jnp.int32)) * columns + home_column
    band_pairs = near_pairs.shape[1] // band_count
    share = band_pairs // columns
    segment = lax.dynamic_slice_in_dim(
        near_pairs, band_index * band_pairs + column_index * share, share, 1
    )
    low_blocks = segment[0]
    high_blocks = segment[1]
    targets = jnp.concatenate([own_blocks, low_blocks])
    lattice_cols = columns * QUAD_COLS + 1
    target_geometry = block_geometry(vertices, panel_vertices, targets, lattice_cols)
    source_geometry = block_geometry(vertices, panel_vertices, high_blocks, lattice_cols)
    self_tiles = self_tile_block([part[:band_rows] for part in target_geometry])
    pair_tiles = tile_block([part[band_rows:] for part in target_geometry], source_geometry)
    low_row = low_blocks // columns - first_row
    high_row = high_blocks // columns - first_row
    low_pos = position_of[low_blocks % columns]
    high_pos = position_of[high_blocks % columns]
    slot_table = (low_row, low_pos, high_row, high_pos)
    return (self_tiles, pair_tiles, slot_table)


def near_product(block_values, prepared):
    self_tiles, pair_tiles, slot_table = prepared
    band_rows = block_values.shape[0]
    low_row, low_pos, high_row, high_pos = slot_table
    self_term = apply_tiles(block_values[:, 0], self_tiles)
    later = shifted(block_values[:REACH], "row", -1)
    source_table = lax.all_gather(
        jnp.concatenate([block_values, later], axis=0), "col", axis=1, tiled=True
    )
    table_rows, columns = source_table.shape[:2]
    flat_table = source_table.reshape(table_rows * columns, -1)
    slots = jnp.arange(table_rows * columns, dtype=jnp.int32)
    low_pick = (slots[None, :] == (low_row * columns + low_pos)[:, None]).astype(jnp.float32)
    high_pick = (slots[None, :] == (high_row * columns + high_pos)[:, None]).astype(jnp.float32)
    shape = (low_row.shape[0],) + source_table.shape[2:]
    high_values = jnp.dot(high_pick, flat_table, precision=lax.Precision.HIGHEST).reshape(shape)
    low_values = jnp.dot(low_pick, flat_table, precision=lax.Precision.HIGHEST).reshape(shape)
    to_low = apply_tiles(high_values, pair_tiles).reshape(low_row.shape[0], -1)
    to_high = apply_transposed(low_values, pair_tiles).reshape(low_row.shape[0], -1)
    partial_value = jnp.dot(
        jnp.concatenate([low_pick, high_pick]).T,
        jnp.concatenate([to_low, to_high]),
        precision=lax.Precision.HIGHEST,
    ).reshape(source_table.shape)
    summed = jnp.sum(lax.all_to_all(partial_value, "col", 1, 1, tiled=True), axis=1)
    carried_down = shifted(summed[band_rows:], "row", 1)
    head = summed[:REACH] + carried_down
    own = jnp.concatenate([head, summed[REACH:band_rows]], axis=0)
    return (own + self_term)[:, None]


def body(charges, column_order, vertices, panel_vertices, near_pairs):
    prepared = prepare(column_order, vertices, panel_vertices, near_pairs, charges.shape[0])
    potential_one = near_product(charges, prepared)
    potential_two = near_product(potential_one, prepared)
    return (potential_one, potential_two)


def solution(mesh):
    return jax.shard_map(
        body,
        mesh=mesh,
        in_specs=(P("row", "col", None, None), P(), P(), P(), P()),
        out_specs=(P("row", "col", None, None), P("row", "col", None, None)),
        check_vma=False,
    )
```

```python
import math

import jax
import jax.numpy as jnp
import numpy as np
from jax import lax
from jax.experimental import pallas as pl
from jax.experimental.pallas import tpu as pltpu
from jax.sharding import PartitionSpec as P

PANELS = 256
REACH = 3
QUAD_ROWS = 8
QUAD_COLS = 16


def shifted(value, axis, by):
    length = lax.axis_size(axis)
    pairs = [(i, i + by) for i in range(length) if 0 <= i + by < length]
    return lax.ppermute(value, axis, pairs)


def rule_tables():
    gauss_two = np.array([-1.0, 1.0]) / math.sqrt(3.0)
    gauss_four = np.array(
        [-0.8611363115940526, -0.3399810435848563, 0.3399810435848563, 0.8611363115940526]
    )
    weight_four = np.array(
        [0.3478548451374538, 0.6521451548625461, 0.6521451548625461, 0.3478548451374538]
    )
    corner_weights = []
    point_weights = []
    for first_index in range(2):
        for second_index in range(4):
            along = 0.5 * (1.0 + gauss_two[first_index])
            across = 0.5 * (1.0 + gauss_four[second_index])
            corner_weights.append([along, (1.0 - along) * across, (1.0 - along) * (1.0 - across)])
            point_weights.append(2.0 * 0.5 * 0.5 * weight_four[second_index] * (1.0 - along))
    return (np.array(corner_weights), np.array(point_weights))


def block_corners(vertices, panel_vertices, block_ids, lattice_cols):
    patch_rows, patch_cols = QUAD_ROWS + 1, QUAD_COLS + 1
    panels = panel_vertices.reshape(3, -1, PANELS)[:, block_ids]
    lattice_row = panels // lattice_cols
    lattice_col = panels % lattice_cols
    base_row = jnp.min(lattice_row, axis=(0, 2))
    base_col = jnp.min(lattice_col, axis=(0, 2))
    local = (lattice_row - base_row[None, :, None]) * patch_cols + (
        lattice_col - base_col[None, :, None]
    )
    grid = jnp.transpose(vertices.reshape(3, -1, lattice_cols), (1, 0, 2))
    row_pick = (
        (base_row[:, None] + jnp.arange(patch_rows, dtype=jnp.int32))[:, :, None]
        == jnp.arange(grid.shape[0], dtype=jnp.int32)
    ).astype(jnp.float32)
    col_pick = (
        jnp.arange(lattice_cols, dtype=jnp.int32)[None, :, None]
        == (base_col[:, None] + jnp.arange(patch_cols, dtype=jnp.int32))[:, None, :]
    ).astype(jnp.float32)
    band = jnp.einsum("grR,Rxc->grxc", row_pick, grid, precision=lax.Precision.HIGHEST)
    patch = jnp.einsum("grxc,gcj->gxrj", band, col_pick, precision=lax.Precision.HIGHEST)
    patch = patch.reshape(block_ids.shape[0], 3, patch_rows * patch_cols)
    pick = (
        local[:, :, :, None] == jnp.arange(patch_rows * patch_cols, dtype=jnp.int32)
    ).astype(jnp.float32)
    return jnp.einsum("gxl,cgpl->gcxp", patch, pick, precision=lax.Precision.HIGHEST)


def block_geometry(vertices, panel_vertices, block_ids, lattice_cols):
    corners = block_corners(vertices, panel_vertices, block_ids, lattice_cols)
    centre = (corners[:, 0] + corners[:, 1] + corners[:, 2]) / 3.0
    first_edge = corners[:, 1] - corners[:, 0]
    second_edge = corners[:, 2] - corners[:, 0]
    normal_x = first_edge[:, 1] * second_edge[:, 2] - first_edge[:, 2] * second_edge[:, 1]
    normal_y = first_edge[:, 2] * second_edge[:, 0] - first_edge[:, 0] * second_edge[:, 2]
    normal_z = first_edge[:, 0] * second_edge[:, 1] - first_edge[:, 1] * second_edge[:, 0]
    panel_area = 0.5 * jnp.sqrt(normal_x * normal_x + normal_y * normal_y + normal_z * normal_z)
    corner_weights, _ = rule_tables()
    points = jnp.einsum(
        "kc,gcxp->gxkp",
        jnp.asarray(corner_weights, corners.dtype),
        corners,
        precision=lax.Precision.HIGHEST,
    )
    return (centre, points, panel_area)


def tile_block(target, source):
    target_centre, target_points, target_area = target
    source_centre, source_points, source_area = source
    _, point_weights = rule_tables()
    kernel_sum = jnp.zeros(
        (target_centre.shape[0], target_centre.shape[2], source_centre.shape[2]), jnp.float32
    )
    for point_index in range(8):
        weight = float(point_weights[point_index])
        distance = target_centre[:, :, :, None] - source_points[:, :, point_index, None, :]
        kernel_sum = kernel_sum + weight * lax.rsqrt(jnp.sum(distance * distance, axis=1) + 0.01)
        distance = target_points[:, :, point_index, :, None] - source_centre[:, :, None, :]
        kernel_sum = kernel_sum + weight * lax.rsqrt(jnp.sum(distance * distance, axis=1) + 0.01)
    return kernel_sum * target_area[:, :, None] * source_area[:, None, :] / (8.0 * math.pi)


def self_tile_block(geometry):
    centre, points, area = geometry
    _, point_weights = rule_tables()
    half_sum = jnp.zeros((centre.shape[0], centre.shape[2], centre.shape[2]), jnp.float32)
    for point_index in range(8):
        weight = float(point_weights[point_index])
        distance = centre[:, :, :, None] - points[:, :, point_index, None, :]
        half_sum = half_sum + weight * lax.rsqrt(jnp.sum(distance * distance, axis=1) + 0.01)
    kernel_sum = half_sum + jnp.swapaxes(half_sum, 1, 2)
    return kernel_sum * area[:, :, None] * area[:, None, :] / (8.0 * math.pi)


def apply_tiles(source_values, tile_stack):
    return jnp.einsum("grq,gpq->grp", source_values, tile_stack, precision=lax.Precision.HIGHEST)


def apply_transposed(source_values, tile_stack):
    return jnp.einsum("grp,gpq->grq", source_values, tile_stack, precision=lax.Precision.HIGHEST)


def prepare(column_order, vertices, panel_vertices, near_pairs, band_rows):
    columns = lax.axis_size("col")
    band_count = lax.axis_size("row")
    band_index = lax.axis_index("row")
    column_index = lax.axis_index("col")
    positions = jnp.arange(columns, dtype=jnp.int32)
    position_of = jnp.sum(
        jnp.where(column_order[:, None] == positions[None, :], positions[:, None], 0), axis=0
    )
    home_column = jnp.sum(jnp.where(positions == column_index, column_order, 0))
    first_row = band_index * band_rows
    own_blocks = (first_row + jnp.arange(band_rows, dtype=jnp.int32)) * columns + home_column
    band_pairs = near_pairs.shape[1] // band_count
    share = band_pairs // columns
    segment = lax.dynamic_slice_in_dim(
        near_pairs, band_index * band_pairs + column_index * share, share, 1
    )
    low_blocks = segment[0]
    high_blocks = segment[1]
    targets = jnp.concatenate([own_blocks, low_blocks])
    lattice_cols = columns * QUAD_COLS + 1
    geometry = block_geometry(
        vertices, panel_vertices, jnp.concatenate([targets, high_blocks]), lattice_cols
    )
    target_geometry = [part[: targets.shape[0]] for part in geometry]
    source_geometry = [part[targets.shape[0] :] for part in geometry]
    self_tiles = self_tile_block([part[:band_rows] for part in target_geometry])
    pair_tiles = tile_block([part[band_rows:] for part in target_geometry], source_geometry)
    low_row = low_blocks // columns - first_row
    high_row = high_blocks // columns - first_row
    low_pos = position_of[low_blocks % columns]
    high_pos = position_of[high_blocks % columns]
    slot_table = (low_row, low_pos, high_row, high_pos)
    return (self_tiles, pair_tiles, slot_table)


def near_product(block_values, prepared):
    self_tiles, pair_tiles, slot_table = prepared
    band_rows = block_values.shape[0]
    low_row, low_pos, high_row, high_pos = slot_table
    self_term = apply_tiles(block_values[:, 0], self_tiles)
    later = shifted(block_values[:REACH], "row", -1)
    source_table = lax.all_gather(
        jnp.concatenate([block_values, later], axis=0), "col", axis=1, tiled=True
    )
    table_rows, columns = source_table.shape[:2]
    flat_table = source_table.reshape(table_rows * columns, -1)
    slots = jnp.arange(table_rows * columns, dtype=jnp.int32)
    low_pick = (slots[None, :] == (low_row * columns + low_pos)[:, None]).astype(jnp.float32)
    high_pick = (slots[None, :] == (high_row * columns + high_pos)[:, None]).astype(jnp.float32)
    shape = (low_row.shape[0],) + source_table.shape[2:]
    high_values = jnp.dot(high_pick, flat_table, precision=lax.Precision.HIGHEST).reshape(shape)
    low_values = jnp.dot(low_pick, flat_table, precision=lax.Precision.HIGHEST).reshape(shape)
    to_low = apply_tiles(high_values, pair_tiles).reshape(low_row.shape[0], -1)
    to_high = apply_transposed(low_values, pair_tiles).reshape(low_row.shape[0], -1)
    partial_value = jnp.dot(
        jnp.concatenate([low_pick, high_pick]).T,
        jnp.concatenate([to_low, to_high]),
        precision=lax.Precision.HIGHEST,
    ).reshape(source_table.shape)
    summed = jnp.sum(lax.all_to_all(partial_value, "col", 1, 1, tiled=True), axis=1)
    carried_down = shifted(summed[band_rows:], "row", 1)
    head = summed[:REACH] + carried_down
    own = jnp.concatenate([head, summed[REACH:band_rows]], axis=0)
    return (own + self_term)[:, None]


def body(charges, column_order, vertices, panel_vertices, near_pairs):
    prepared = prepare(column_order, vertices, panel_vertices, near_pairs, charges.shape[0])
    potential_one = near_product(charges, prepared)
    potential_two = near_product(potential_one, prepared)
    return (potential_one, potential_two)


def solution(mesh):
    return jax.shard_map(
        body,
        mesh=mesh,
        in_specs=(P("row", "col", None, None), P(), P(), P(), P()),
        out_specs=(P("row", "col", None, None), P("row", "col", None, None)),
        check_vma=False,
    )
```

```python
import math

import jax
import jax.numpy as jnp
import numpy as np
from jax import lax
from jax.experimental import pallas as pl
from jax.experimental.pallas import tpu as pltpu
from jax.sharding import PartitionSpec as P

PANELS = 256
REACH = 3
QUAD_ROWS = 8
QUAD_COLS = 16


def shifted(value, axis, by):
    length = lax.axis_size(axis)
    pairs = [(i, i + by) for i in range(length) if 0 <= i + by < length]
    return lax.ppermute(value, axis, pairs)


def rule_tables():
    gauss_two = np.array([-1.0, 1.0]) / math.sqrt(3.0)
    gauss_four = np.array(
        [-0.8611363115940526, -0.3399810435848563, 0.3399810435848563, 0.8611363115940526]
    )
    weight_four = np.array(
        [0.3478548451374538, 0.6521451548625461, 0.6521451548625461, 0.3478548451374538]
    )
    corner_weights = []
    point_weights = []
    for first_index in range(2):
        for second_index in range(4):
            along = 0.5 * (1.0 + gauss_two[first_index])
            across = 0.5 * (1.0 + gauss_four[second_index])
            corner_weights.append([along, (1.0 - along) * across, (1.0 - along) * (1.0 - across)])
            point_weights.append(2.0 * 0.5 * 0.5 * weight_four[second_index] * (1.0 - along))
    return (np.array(corner_weights), np.array(point_weights))


def block_corners(vertices, panel_vertices, block_ids, lattice_cols):
    patch_rows, patch_cols = QUAD_ROWS + 1, QUAD_COLS + 1
    panels = panel_vertices.reshape(3, -1, PANELS)[:, block_ids]
    lattice_row = panels // lattice_cols
    lattice_col = panels % lattice_cols
    base_row = jnp.min(lattice_row, axis=(0, 2))
    base_col = jnp.min(lattice_col, axis=(0, 2))
    local = (lattice_row - base_row[None, :, None]) * patch_cols + (
        lattice_col - base_col[None, :, None]
    )
    grid = jnp.transpose(vertices.reshape(3, -1, lattice_cols), (1, 0, 2))
    row_pick = (
        (base_row[:, None] + jnp.arange(patch_rows, dtype=jnp.int32))[:, :, None]
        == jnp.arange(grid.shape[0], dtype=jnp.int32)
    ).astype(jnp.float32)
    col_pick = (
        jnp.arange(lattice_cols, dtype=jnp.int32)[None, :, None]
        == (base_col[:, None] + jnp.arange(patch_cols, dtype=jnp.int32))[:, None, :]
    ).astype(jnp.float32)
    band = jnp.einsum("grR,Rxc->grxc", row_pick, grid, precision=lax.Precision.HIGHEST)
    patch = jnp.einsum("grxc,gcj->gxrj", band, col_pick, precision=lax.Precision.HIGHEST)
    patch = patch.reshape(block_ids.shape[0], 3, patch_rows * patch_cols)
    pick = (
        local[:, :, :, None] == jnp.arange(patch_rows * patch_cols, dtype=jnp.int32)
    ).astype(jnp.float32)
    return jnp.einsum("gxl,cgpl->gcxp", patch, pick, precision=lax.Precision.HIGHEST)


def block_geometry(vertices, panel_vertices, block_ids, lattice_cols):
    corners = block_corners(vertices, panel_vertices, block_ids, lattice_cols)
    centre = (corners[:, 0] + corners[:, 1] + corners[:, 2]) / 3.0
    first_edge = corners[:, 1] - corners[:, 0]
    second_edge = corners[:, 2] - corners[:, 0]
    normal_x = first_edge[:, 1] * second_edge[:, 2] - first_edge[:, 2] * second_edge[:, 1]
    normal_y = first_edge[:, 2] * second_edge[:, 0] - first_edge[:, 0] * second_edge[:, 2]
    normal_z = first_edge[:, 0] * second_edge[:, 1] - first_edge[:, 1] * second_edge[:, 0]
    panel_area = 0.5 * jnp.sqrt(normal_x * normal_x + normal_y * normal_y + normal_z * normal_z)
    corner_weights, _ = rule_tables()
    points = jnp.einsum(
        "kc,gcxp->gxkp",
        jnp.asarray(corner_weights, corners.dtype),
        corners,
        precision=lax.Precision.HIGHEST,
    )
    return (centre, points, panel_area)


def tile_block(target, source):
    target_centre, target_points, target_area = target
    source_centre, source_points, source_area = source
    _, point_weights = rule_tables()
    scales = [1.0 / float(weight) for weight in point_weights]
    scaled = lax.optimization_barrier(
        (
            jnp.stack([target_centre * scale for scale in scales], axis=2),
            source_points * jnp.asarray(scales, jnp.float32)[None, None, :, None],
            target_points * jnp.asarray(scales, jnp.float32)[None, None, :, None],
            jnp.stack([source_centre * scale for scale in scales], axis=2),
        )
    )
    centre_near, points_far, points_near, centre_far = scaled
    kernel_sum = jnp.zeros(
        (target_centre.shape[0], target_centre.shape[2], source_centre.shape[2]), jnp.float32
    )
    for point_index, scale in enumerate(scales):
        floor = 0.01 * scale * scale
        distance = centre_near[:, :, point_index, :, None] - points_far[:, :, point_index, None, :]
        kernel_sum = kernel_sum + lax.rsqrt(jnp.sum(distance * distance, axis=1) + floor)
        distance = points_near[:, :, point_index, :, None] - centre_far[:, :, point_index, None, :]
        kernel_sum = kernel_sum + lax.rsqrt(jnp.sum(distance * distance, axis=1) + floor)
    return kernel_sum * target_area[:, :, None] * source_area[:, None, :] / (8.0 * math.pi)


def self_tile_block(geometry):
    centre, points, area = geometry
    _, point_weights = rule_tables()
    scales = [1.0 / float(weight) for weight in point_weights]
    centre_near, points_far = lax.optimization_barrier(
        (
            jnp.stack([centre * scale for scale in scales], axis=2),
            points * jnp.asarray(scales, jnp.float32)[None, None, :, None],
        )
    )
    half_sum = jnp.zeros((centre.shape[0], centre.shape[2], centre.shape[2]), jnp.float32)
    for point_index, scale in enumerate(scales):
        floor = 0.01 * scale * scale
        distance = centre_near[:, :, point_index, :, None] - points_far[:, :, point_index, None, :]
        half_sum = half_sum + lax.rsqrt(jnp.sum(distance * distance, axis=1) + floor)
    kernel_sum = half_sum + jnp.swapaxes(half_sum, 1, 2)
    return kernel_sum * area[:, :, None] * area[:, None, :] / (8.0 * math.pi)


def apply_tiles(source_values, tile_stack):
    return jnp.einsum("grq,gpq->grp", source_values, tile_stack, precision=lax.Precision.HIGHEST)


def apply_transposed(source_values, tile_stack):
    return jnp.einsum("grp,gpq->grq", source_values, tile_stack, precision=lax.Precision.HIGHEST)


def prepare(column_order, vertices, panel_vertices, near_pairs, band_rows):
    columns = lax.axis_size("col")
    band_count = lax.axis_size("row")
    band_index = lax.axis_index("row")
    column_index = lax.axis_index("col")
    positions = jnp.arange(columns, dtype=jnp.int32)
    position_of = jnp.sum(
        jnp.where(column_order[:, None] == positions[None, :], positions[:, None], 0), axis=0
    )
    home_column = jnp.sum(jnp.where(positions == column_index, column_order, 0))
    first_row = band_index * band_rows
    own_blocks = (first_row + jnp.arange(band_rows, dtype=jnp.int32)) * columns + home_column
    band_pairs = near_pairs.shape[1] // band_count
    share = band_pairs // columns
    segment = lax.dynamic_slice_in_dim(
        near_pairs, band_index * band_pairs + column_index * share, share, 1
    )
    low_blocks = segment[0]
    high_blocks = segment[1]
    targets = jnp.concatenate([own_blocks, low_blocks])
    lattice_cols = columns * QUAD_COLS + 1
    geometry = block_geometry(
        vertices, panel_vertices, jnp.concatenate([targets, high_blocks]), lattice_cols
    )
    target_geometry = [part[: targets.shape[0]] for part in geometry]
    source_geometry = [part[targets.shape[0] :] for part in geometry]
    self_tiles = self_tile_block([part[:band_rows] for part in target_geometry])
    pair_tiles = tile_block([part[band_rows:] for part in target_geometry], source_geometry)
    low_row = low_blocks // columns - first_row
    high_row = high_blocks // columns - first_row
    low_pos = position_of[low_blocks % columns]
    high_pos = position_of[high_blocks % columns]
    slot_table = (low_row, low_pos, high_row, high_pos)
    return (self_tiles, pair_tiles, slot_table)


def near_product(block_values, prepared):
    self_tiles, pair_tiles, slot_table = prepared
    band_rows = block_values.shape[0]
    low_row, low_pos, high_row, high_pos = slot_table
    self_term = apply_tiles(block_values[:, 0], self_tiles)
    later = shifted(block_values[:REACH], "row", -1)
    source_table = lax.all_gather(
        jnp.concatenate([block_values, later], axis=0), "col", axis=1, tiled=True
    )
    table_rows, columns = source_table.shape[:2]
    flat_table = source_table.reshape(table_rows * columns, -1)
    slots = jnp.arange(table_rows * columns, dtype=jnp.int32)
    low_pick = (slots[None, :] == (low_row * columns + low_pos)[:, None]).astype(jnp.float32)
    high_pick = (slots[None, :] == (high_row * columns + high_pos)[:, None]).astype(jnp.float32)
    shape = (low_row.shape[0],) + source_table.shape[2:]
    high_values = jnp.dot(high_pick, flat_table, precision=lax.Precision.HIGHEST).reshape(shape)
    low_values = jnp.dot(low_pick, flat_table, precision=lax.Precision.HIGHEST).reshape(shape)
    to_low = apply_tiles(high_values, pair_tiles).reshape(low_row.shape[0], -1)
    to_high = apply_transposed(low_values, pair_tiles).reshape(low_row.shape[0], -1)
    partial_value = jnp.dot(
        jnp.concatenate([low_pick, high_pick]).T,
        jnp.concatenate([to_low, to_high]),
        precision=lax.Precision.HIGHEST,
    ).reshape(source_table.shape)
    summed = jnp.sum(lax.all_to_all(partial_value, "col", 1, 1, tiled=True), axis=1)
    carried_down = shifted(summed[band_rows:], "row", 1)
    head = summed[:REACH] + carried_down
    own = jnp.concatenate([head, summed[REACH:band_rows]], axis=0)
    return (own + self_term)[:, None]


def body(charges, column_order, vertices, panel_vertices, near_pairs):
    prepared = prepare(column_order, vertices, panel_vertices, near_pairs, charges.shape[0])
    potential_one = near_product(charges, prepared)
    potential_two = near_product(potential_one, prepared)
    return (potential_one, potential_two)


def solution(mesh):
    return jax.shard_map(
        body,
        mesh=mesh,
        in_specs=(P("row", "col", None, None), P(), P(), P(), P()),
        out_specs=(P("row", "col", None, None), P("row", "col", None, None)),
        check_vma=False,
    )
```

```python
import math

import jax
import jax.numpy as jnp
import numpy as np
from jax import lax
from jax.experimental import pallas as pl
from jax.experimental.pallas import tpu as pltpu
from jax.sharding import PartitionSpec as P

PANELS = 256
REACH = 3
QUAD_ROWS = 8
QUAD_COLS = 16
FEATURES = 32


def shifted(value, axis, by):
    length = lax.axis_size(axis)
    pairs = [(i, i + by) for i in range(length) if 0 <= i + by < length]
    return lax.ppermute(value, axis, pairs)


def rule_tables():
    gauss_two = np.array([-1.0, 1.0]) / math.sqrt(3.0)
    gauss_four = np.array(
        [-0.8611363115940526, -0.3399810435848563, 0.3399810435848563, 0.8611363115940526]
    )
    weight_four = np.array(
        [0.3478548451374538, 0.6521451548625461, 0.6521451548625461, 0.3478548451374538]
    )
    corner_weights = []
    point_weights = []
    for first_index in range(2):
        for second_index in range(4):
            along = 0.5 * (1.0 + gauss_two[first_index])
            across = 0.5 * (1.0 + gauss_four[second_index])
            corner_weights.append([along, (1.0 - along) * across, (1.0 - along) * (1.0 - across)])
            point_weights.append(2.0 * 0.5 * 0.5 * weight_four[second_index] * (1.0 - along))
    return (np.array(corner_weights), np.array(point_weights))


def block_corners(vertices, panel_vertices, block_ids, lattice_cols):
    patch_rows, patch_cols = QUAD_ROWS + 1, QUAD_COLS + 1
    panels = panel_vertices.reshape(3, -1, PANELS)[:, block_ids]
    lattice_row = panels // lattice_cols
    lattice_col = panels % lattice_cols
    base_row = jnp.min(lattice_row, axis=(0, 2))
    base_col = jnp.min(lattice_col, axis=(0, 2))
    local = (lattice_row - base_row[None, :, None]) * patch_cols + (
        lattice_col - base_col[None, :, None]
    )
    grid = jnp.transpose(vertices.reshape(3, -1, lattice_cols), (1, 0, 2))
    row_pick = (
        (base_row[:, None] + jnp.arange(patch_rows, dtype=jnp.int32))[:, :, None]
        == jnp.arange(grid.shape[0], dtype=jnp.int32)
    ).astype(jnp.float32)
    col_pick = (
        jnp.arange(lattice_cols, dtype=jnp.int32)[None, :, None]
        == (base_col[:, None] + jnp.arange(patch_cols, dtype=jnp.int32))[:, None, :]
    ).astype(jnp.float32)
    band = jnp.einsum("grR,Rxc->grxc", row_pick, grid, precision=lax.Precision.HIGHEST)
    patch = jnp.einsum("grxc,gcj->gxrj", band, col_pick, precision=lax.Precision.HIGHEST)
    patch = patch.reshape(block_ids.shape[0], 3, patch_rows * patch_cols)
    pick = (
        local[:, :, :, None] == jnp.arange(patch_rows * patch_cols, dtype=jnp.int32)
    ).astype(jnp.float32)
    return jnp.einsum("gxl,cgpl->gcxp", patch, pick, precision=lax.Precision.HIGHEST)


def block_geometry(vertices, panel_vertices, block_ids, lattice_cols):
    corners = block_corners(vertices, panel_vertices, block_ids, lattice_cols)
    centre = (corners[:, 0] + corners[:, 1] + corners[:, 2]) / 3.0
    first_edge = corners[:, 1] - corners[:, 0]
    second_edge = corners[:, 2] - corners[:, 0]
    normal_x = first_edge[:, 1] * second_edge[:, 2] - first_edge[:, 2] * second_edge[:, 1]
    normal_y = first_edge[:, 2] * second_edge[:, 0] - first_edge[:, 0] * second_edge[:, 2]
    normal_z = first_edge[:, 0] * second_edge[:, 1] - first_edge[:, 1] * second_edge[:, 0]
    panel_area = 0.5 * jnp.sqrt(normal_x * normal_x + normal_y * normal_y + normal_z * normal_z)
    corner_weights, _ = rule_tables()
    points = jnp.einsum(
        "kc,gcxp->gxkp",
        jnp.asarray(corner_weights, corners.dtype),
        corners,
        precision=lax.Precision.HIGHEST,
    )
    return (centre, points, panel_area)


def tile_block(target, source):
    target_centre, target_points, target_area = target
    source_centre, source_points, source_area = source
    _, point_weights = rule_tables()
    kernel_sum = jnp.zeros(
        (target_centre.shape[0], target_centre.shape[2], source_centre.shape[2]), jnp.float32
    )
    for point_index in range(8):
        weight = float(point_weights[point_index])
        distance = target_centre[:, :, :, None] - source_points[:, :, point_index, None, :]
        kernel_sum = kernel_sum + weight * lax.rsqrt(jnp.sum(distance * distance, axis=1) + 0.01)
        distance = target_points[:, :, point_index, :, None] - source_centre[:, :, None, :]
        kernel_sum = kernel_sum + weight * lax.rsqrt(jnp.sum(distance * distance, axis=1) + 0.01)
    return kernel_sum * target_area[:, :, None] * source_area[:, None, :] / (8.0 * math.pi)


def feature_rows(geometry):
    centre, points, area = geometry
    count = centre.shape[0]
    flat_points = jnp.transpose(points, (0, 2, 1, 3)).reshape(count, -1, PANELS)
    pad = jnp.zeros((count, FEATURES - 4 - flat_points.shape[1], PANELS), jnp.float32)
    return jnp.concatenate([centre, flat_points, area[:, None], pad], axis=1)


def pair_tile_block(target, source):
    _, point_weights = rule_tables()
    target_rows = jnp.transpose(feature_rows(target), (0, 2, 1))
    source_rows = feature_rows(source)
    count = target_rows.shape[0]
    area_at = 3 + 3 * len(point_weights)
    chunk = 16

    def kernel(target_ref, source_ref, out_ref):
        source_centre = [
            jnp.broadcast_to(source_ref[0, axis : axis + 1, :], (chunk, PANELS))
            for axis in range(3)
        ]
        source_area = source_ref[0, area_at : area_at + 1, :]

        def body(step, carry):
            rows = pl.ds(pl.multiple_of(step * chunk, chunk), chunk)
            held = target_ref[0, rows, :]
            target_centre = [
                jnp.broadcast_to(held[:, axis : axis + 1], (chunk, PANELS)) for axis in range(3)
            ]
            total = jnp.zeros((chunk, PANELS), jnp.float32)
            for point_index, weight in enumerate(point_weights):
                at = 3 + 3 * point_index
                squared = 0.01
                for axis in range(3):
                    gap = target_centre[axis] - source_ref[0, at + axis : at + axis + 1, :]
                    squared = squared + gap * gap
                total = total + float(weight) * lax.rsqrt(squared)
                squared = 0.01
                for axis in range(3):
                    gap = held[:, at + axis : at + axis + 1] - source_centre[axis]
                    squared = squared + gap * gap
                total = total + float(weight) * lax.rsqrt(squared)
            scale = held[:, area_at : area_at + 1] * source_area
            out_ref[0, rows, :] = total * scale * (1.0 / (8.0 * math.pi))
            return carry

        lax.fori_loop(0, PANELS // chunk, body, 0)

    return pl.pallas_call(
        kernel,
        out_shape=jax.ShapeDtypeStruct((count, PANELS, PANELS), jnp.float32),
        grid=(count,),
        in_specs=[
            pl.BlockSpec((1, PANELS, FEATURES), lambda i: (i, 0, 0)),
            pl.BlockSpec((1, FEATURES, PANELS), lambda i: (i, 0, 0)),
        ],
        out_specs=pl.BlockSpec((1, PANELS, PANELS), lambda i: (i, 0, 0)),
        cost_estimate=pl.CostEstimate(
            flops=count * PANELS * PANELS * 16 * 11,
            transcendentals=count * PANELS * PANELS * 16,
            bytes_accessed=count * PANELS * (PANELS + 2 * FEATURES) * 4,
        ),
    )(target_rows, source_rows)


def self_tile_block(geometry):
    centre, points, area = geometry
    _, point_weights = rule_tables()
    half_sum = jnp.zeros((centre.shape[0], centre.shape[2], centre.shape[2]), jnp.float32)
    for point_index in range(8):
        weight = float(point_weights[point_index])
        distance = centre[:, :, :, None] - points[:, :, point_index, None, :]
        half_sum = half_sum + weight * lax.rsqrt(jnp.sum(distance * distance, axis=1) + 0.01)
    kernel_sum = half_sum + jnp.swapaxes(half_sum, 1, 2)
    return kernel_sum * area[:, :, None] * area[:, None, :] / (8.0 * math.pi)


def apply_tiles(source_values, tile_stack):
    return jnp.einsum("grq,gpq->grp", source_values, tile_stack, precision=lax.Precision.HIGHEST)


def apply_transposed(source_values, tile_stack):
    return jnp.einsum("grp,gpq->grq", source_values, tile_stack, precision=lax.Precision.HIGHEST)


def prepare(column_order, vertices, panel_vertices, near_pairs, band_rows):
    columns = lax.axis_size("col")
    band_count = lax.axis_size("row")
    band_index = lax.axis_index("row")
    column_index = lax.axis_index("col")
    positions = jnp.arange(columns, dtype=jnp.int32)
    position_of = jnp.sum(
        jnp.where(column_order[:, None] == positions[None, :], positions[:, None], 0), axis=0
    )
    home_column = jnp.sum(jnp.where(positions == column_index, column_order, 0))
    first_row = band_index * band_rows
    own_blocks = (first_row + jnp.arange(band_rows, dtype=jnp.int32)) * columns + home_column
    band_pairs = near_pairs.shape[1] // band_count
    share = band_pairs // columns
    segment = lax.dynamic_slice_in_dim(
        near_pairs, band_index * band_pairs + column_index * share, share, 1
    )
    low_blocks = segment[0]
    high_blocks = segment[1]
    targets = jnp.concatenate([own_blocks, low_blocks])
    lattice_cols = columns * QUAD_COLS + 1
    geometry = block_geometry(
        vertices, panel_vertices, jnp.concatenate([targets, high_blocks]), lattice_cols
    )
    target_geometry = [part[: targets.shape[0]] for part in geometry]
    source_geometry = [part[targets.shape[0] :] for part in geometry]
    self_tiles = self_tile_block([part[:band_rows] for part in target_geometry])
    pair_tiles = pair_tile_block([part[band_rows:] for part in target_geometry], source_geometry)
    low_row = low_blocks // columns - first_row
    high_row = high_blocks // columns - first_row
    low_pos = position_of[low_blocks % columns]
    high_pos = position_of[high_blocks % columns]
    slot_table = (low_row, low_pos, high_row, high_pos)
    return (self_tiles, pair_tiles, slot_table)


def near_product(block_values, prepared):
    self_tiles, pair_tiles, slot_table = prepared
    band_rows = block_values.shape[0]
    low_row, low_pos, high_row, high_pos = slot_table
    self_term = apply_tiles(block_values[:, 0], self_tiles)
    later = shifted(block_values[:REACH], "row", -1)
    source_table = lax.all_gather(
        jnp.concatenate([block_values, later], axis=0), "col", axis=1, tiled=True
    )
    table_rows, columns = source_table.shape[:2]
    flat_table = source_table.reshape(table_rows * columns, -1)
    slots = jnp.arange(table_rows * columns, dtype=jnp.int32)
    low_pick = (slots[None, :] == (low_row * columns + low_pos)[:, None]).astype(jnp.float32)
    high_pick = (slots[None, :] == (high_row * columns + high_pos)[:, None]).astype(jnp.float32)
    shape = (low_row.shape[0],) + source_table.shape[2:]
    high_values = jnp.dot(high_pick, flat_table, precision=lax.Precision.HIGHEST).reshape(shape)
    low_values = jnp.dot(low_pick, flat_table, precision=lax.Precision.HIGHEST).reshape(shape)
    to_low = apply_tiles(high_values, pair_tiles).reshape(low_row.shape[0], -1)
    to_high = apply_transposed(low_values, pair_tiles).reshape(low_row.shape[0], -1)
    partial_value = jnp.dot(
        jnp.concatenate([low_pick, high_pick]).T,
        jnp.concatenate([to_low, to_high]),
        precision=lax.Precision.HIGHEST,
    ).reshape(source_table.shape)
    summed = jnp.sum(lax.all_to_all(partial_value, "col", 1, 1, tiled=True), axis=1)
    carried_down = shifted(summed[band_rows:], "row", 1)
    head = summed[:REACH] + carried_down
    own = jnp.concatenate([head, summed[REACH:band_rows]], axis=0)
    return (own + self_term)[:, None]


def body(charges, column_order, vertices, panel_vertices, near_pairs):
    prepared = prepare(column_order, vertices, panel_vertices, near_pairs, charges.shape[0])
    potential_one = near_product(charges, prepared)
    potential_two = near_product(potential_one, prepared)
    return (potential_one, potential_two)


def solution(mesh):
    return jax.shard_map(
        body,
        mesh=mesh,
        in_specs=(P("row", "col", None, None), P(), P(), P(), P()),
        out_specs=(P("row", "col", None, None), P("row", "col", None, None)),
        check_vma=False,
    )
```

```python
import math

import jax
import jax.numpy as jnp
import numpy as np
from jax import lax
from jax.experimental import pallas as pl
from jax.experimental.pallas import tpu as pltpu
from jax.sharding import PartitionSpec as P

PANELS = 256
REACH = 3
QUAD_ROWS = 8
QUAD_COLS = 16
FEATURES = 32


def shifted(value, axis, by):
    length = lax.axis_size(axis)
    pairs = [(i, i + by) for i in range(length) if 0 <= i + by < length]
    return lax.ppermute(value, axis, pairs)


def rule_tables():
    gauss_two = np.array([-1.0, 1.0]) / math.sqrt(3.0)
    gauss_four = np.array(
        [-0.8611363115940526, -0.3399810435848563, 0.3399810435848563, 0.8611363115940526]
    )
    weight_four = np.array(
        [0.3478548451374538, 0.6521451548625461, 0.6521451548625461, 0.3478548451374538]
    )
    corner_weights = []
    point_weights = []
    for first_index in range(2):
        for second_index in range(4):
            along = 0.5 * (1.0 + gauss_two[first_index])
            across = 0.5 * (1.0 + gauss_four[second_index])
            corner_weights.append([along, (1.0 - along) * across, (1.0 - along) * (1.0 - across)])
            point_weights.append(2.0 * 0.5 * 0.5 * weight_four[second_index] * (1.0 - along))
    return (np.array(corner_weights), np.array(point_weights))


def block_corners(vertices, panel_vertices, block_ids, lattice_cols):
    patch_rows, patch_cols = QUAD_ROWS + 1, QUAD_COLS + 1
    panels = panel_vertices.reshape(3, -1, PANELS)[:, block_ids]
    lattice_row = panels // lattice_cols
    lattice_col = panels % lattice_cols
    base_row = jnp.min(lattice_row, axis=(0, 2))
    base_col = jnp.min(lattice_col, axis=(0, 2))
    local = (lattice_row - base_row[None, :, None]) * patch_cols + (
        lattice_col - base_col[None, :, None]
    )
    grid = jnp.transpose(vertices.reshape(3, -1, lattice_cols), (1, 0, 2))
    row_pick = (
        (base_row[:, None] + jnp.arange(patch_rows, dtype=jnp.int32))[:, :, None]
        == jnp.arange(grid.shape[0], dtype=jnp.int32)
    ).astype(jnp.float32)
    col_pick = (
        jnp.arange(lattice_cols, dtype=jnp.int32)[None, :, None]
        == (base_col[:, None] + jnp.arange(patch_cols, dtype=jnp.int32))[:, None, :]
    ).astype(jnp.float32)
    band = jnp.einsum("grR,Rxc->grxc", row_pick, grid, precision=lax.Precision.HIGHEST)
    patch = jnp.einsum("grxc,gcj->gxrj", band, col_pick, precision=lax.Precision.HIGHEST)
    patch = patch.reshape(block_ids.shape[0], 3, patch_rows * patch_cols)
    pick = (
        local[:, :, :, None] == jnp.arange(patch_rows * patch_cols, dtype=jnp.int32)
    ).astype(jnp.float32)
    return jnp.einsum("gxl,cgpl->gcxp", patch, pick, precision=lax.Precision.HIGHEST)


def block_geometry(vertices, panel_vertices, block_ids, lattice_cols):
    corners = block_corners(vertices, panel_vertices, block_ids, lattice_cols)
    centre = (corners[:, 0] + corners[:, 1] + corners[:, 2]) / 3.0
    first_edge = corners[:, 1] - corners[:, 0]
    second_edge = corners[:, 2] - corners[:, 0]
    normal_x = first_edge[:, 1] * second_edge[:, 2] - first_edge[:, 2] * second_edge[:, 1]
    normal_y = first_edge[:, 2] * second_edge[:, 0] - first_edge[:, 0] * second_edge[:, 2]
    normal_z = first_edge[:, 0] * second_edge[:, 1] - first_edge[:, 1] * second_edge[:, 0]
    panel_area = 0.5 * jnp.sqrt(normal_x * normal_x + normal_y * normal_y + normal_z * normal_z)
    corner_weights, _ = rule_tables()
    points = jnp.einsum(
        "kc,gcxp->gxkp",
        jnp.asarray(corner_weights, corners.dtype),
        corners,
        precision=lax.Precision.HIGHEST,
    )
    return (centre, points, panel_area)


def tile_block(target, source):
    target_centre, target_points, target_area = target
    source_centre, source_points, source_area = source
    _, point_weights = rule_tables()
    kernel_sum = jnp.zeros(
        (target_centre.shape[0], target_centre.shape[2], source_centre.shape[2]), jnp.float32
    )
    for point_index in range(8):
        weight = float(point_weights[point_index])
        distance = target_centre[:, :, :, None] - source_points[:, :, point_index, None, :]
        kernel_sum = kernel_sum + weight * lax.rsqrt(jnp.sum(distance * distance, axis=1) + 0.01)
        distance = target_points[:, :, point_index, :, None] - source_centre[:, :, None, :]
        kernel_sum = kernel_sum + weight * lax.rsqrt(jnp.sum(distance * distance, axis=1) + 0.01)
    return kernel_sum * target_area[:, :, None] * source_area[:, None, :] / (8.0 * math.pi)


def feature_rows(geometry):
    centre, points, area = geometry
    count = centre.shape[0]
    flat_points = jnp.transpose(points, (0, 2, 1, 3)).reshape(count, -1, PANELS)
    pad = jnp.zeros((count, FEATURES - 4 - flat_points.shape[1], PANELS), jnp.float32)
    return jnp.concatenate([centre, flat_points, area[:, None], pad], axis=1)


def pair_tile_block(target, source):
    _, point_weights = rule_tables()
    target_rows = feature_rows(target)
    source_rows = feature_rows(source)
    count = target_rows.shape[0]
    area_at = 3 + 3 * len(point_weights)
    chunk = 16

    def kernel(target_ref, source_ref, out_ref, turned_ref):
        turned_ref[...] = target_ref[0].T
        source_centre = [
            jnp.broadcast_to(source_ref[0, axis : axis + 1, :], (chunk, PANELS))
            for axis in range(3)
        ]
        source_area = source_ref[0, area_at : area_at + 1, :]

        def body(step, carry):
            rows = pl.ds(pl.multiple_of(step * chunk, chunk), chunk)
            held = turned_ref[rows, :]
            target_centre = [
                jnp.broadcast_to(held[:, axis : axis + 1], (chunk, PANELS)) for axis in range(3)
            ]
            total = jnp.zeros((chunk, PANELS), jnp.float32)
            for point_index, weight in enumerate(point_weights):
                at = 3 + 3 * point_index
                squared = 0.01
                for axis in range(3):
                    gap = target_centre[axis] - source_ref[0, at + axis : at + axis + 1, :]
                    squared = squared + gap * gap
                total = total + float(weight) * lax.rsqrt(squared)
                squared = 0.01
                for axis in range(3):
                    gap = held[:, at + axis : at + axis + 1] - source_centre[axis]
                    squared = squared + gap * gap
                total = total + float(weight) * lax.rsqrt(squared)
            scale = held[:, area_at : area_at + 1] * source_area
            out_ref[0, rows, :] = total * scale * (1.0 / (8.0 * math.pi))
            return carry

        lax.fori_loop(0, PANELS // chunk, body, 0)

    return pl.pallas_call(
        kernel,
        out_shape=jax.ShapeDtypeStruct((count, PANELS, PANELS), jnp.float32),
        grid=(count,),
        in_specs=[
            pl.BlockSpec((1, FEATURES, PANELS), lambda i: (i, 0, 0)),
            pl.BlockSpec((1, FEATURES, PANELS), lambda i: (i, 0, 0)),
        ],
        out_specs=pl.BlockSpec((1, PANELS, PANELS), lambda i: (i, 0, 0)),
        scratch_shapes=[pltpu.VMEM((PANELS, FEATURES), jnp.float32)],
        cost_estimate=pl.CostEstimate(
            flops=count * PANELS * PANELS * 16 * 11,
            transcendentals=count * PANELS * PANELS * 16,
            bytes_accessed=count * PANELS * (PANELS + 2 * FEATURES) * 4,
        ),
    )(target_rows, source_rows)


def self_tile_block(geometry):
    centre, points, area = geometry
    _, point_weights = rule_tables()
    half_sum = jnp.zeros((centre.shape[0], centre.shape[2], centre.shape[2]), jnp.float32)
    for point_index in range(8):
        weight = float(point_weights[point_index])
        distance = centre[:, :, :, None] - points[:, :, point_index, None, :]
        half_sum = half_sum + weight * lax.rsqrt(jnp.sum(distance * distance, axis=1) + 0.01)
    kernel_sum = half_sum + jnp.swapaxes(half_sum, 1, 2)
    return kernel_sum * area[:, :, None] * area[:, None, :] / (8.0 * math.pi)


def apply_tiles(source_values, tile_stack):
    return jnp.einsum("grq,gpq->grp", source_values, tile_stack, precision=lax.Precision.HIGHEST)


def apply_transposed(source_values, tile_stack):
    return jnp.einsum("grp,gpq->grq", source_values, tile_stack, precision=lax.Precision.HIGHEST)


def prepare(column_order, vertices, panel_vertices, near_pairs, band_rows):
    columns = lax.axis_size("col")
    band_count = lax.axis_size("row")
    band_index = lax.axis_index("row")
    column_index = lax.axis_index("col")
    positions = jnp.arange(columns, dtype=jnp.int32)
    position_of = jnp.sum(
        jnp.where(column_order[:, None] == positions[None, :], positions[:, None], 0), axis=0
    )
    home_column = jnp.sum(jnp.where(positions == column_index, column_order, 0))
    first_row = band_index * band_rows
    own_blocks = (first_row + jnp.arange(band_rows, dtype=jnp.int32)) * columns + home_column
    band_pairs = near_pairs.shape[1] // band_count
    share = band_pairs // columns
    segment = lax.dynamic_slice_in_dim(
        near_pairs, band_index * band_pairs + column_index * share, share, 1
    )
    low_blocks = segment[0]
    high_blocks = segment[1]
    targets = jnp.concatenate([own_blocks, low_blocks])
    lattice_cols = columns * QUAD_COLS + 1
    geometry = block_geometry(
        vertices, panel_vertices, jnp.concatenate([targets, high_blocks]), lattice_cols
    )
    target_geometry = [part[: targets.shape[0]] for part in geometry]
    source_geometry = [part[targets.shape[0] :] for part in geometry]
    self_tiles = self_tile_block([part[:band_rows] for part in target_geometry])
    pair_tiles = pair_tile_block([part[band_rows:] for part in target_geometry], source_geometry)
    low_row = low_blocks // columns - first_row
    high_row = high_blocks // columns - first_row
    low_pos = position_of[low_blocks % columns]
    high_pos = position_of[high_blocks % columns]
    slot_table = (low_row, low_pos, high_row, high_pos)
    return (self_tiles, pair_tiles, slot_table)


def near_product(block_values, prepared):
    self_tiles, pair_tiles, slot_table = prepared
    band_rows = block_values.shape[0]
    low_row, low_pos, high_row, high_pos = slot_table
    self_term = apply_tiles(block_values[:, 0], self_tiles)
    later = shifted(block_values[:REACH], "row", -1)
    source_table = lax.all_gather(
        jnp.concatenate([block_values, later], axis=0), "col", axis=1, tiled=True
    )
    table_rows, columns = source_table.shape[:2]
    flat_table = source_table.reshape(table_rows * columns, -1)
    slots = jnp.arange(table_rows * columns, dtype=jnp.int32)
    low_pick = (slots[None, :] == (low_row * columns + low_pos)[:, None]).astype(jnp.float32)
    high_pick = (slots[None, :] == (high_row * columns + high_pos)[:, None]).astype(jnp.float32)
    shape = (low_row.shape[0],) + source_table.shape[2:]
    high_values = jnp.dot(high_pick, flat_table, precision=lax.Precision.HIGHEST).reshape(shape)
    low_values = jnp.dot(low_pick, flat_table, precision=lax.Precision.HIGHEST).reshape(shape)
    to_low = apply_tiles(high_values, pair_tiles).reshape(low_row.shape[0], -1)
    to_high = apply_transposed(low_values, pair_tiles).reshape(low_row.shape[0], -1)
    partial_value = jnp.dot(
        jnp.concatenate([low_pick, high_pick]).T,
        jnp.concatenate([to_low, to_high]),
        precision=lax.Precision.HIGHEST,
    ).reshape(source_table.shape)
    summed = jnp.sum(lax.all_to_all(partial_value, "col", 1, 1, tiled=True), axis=1)
    carried_down = shifted(summed[band_rows:], "row", 1)
    head = summed[:REACH] + carried_down
    own = jnp.concatenate([head, summed[REACH:band_rows]], axis=0)
    return (own + self_term)[:, None]


def body(charges, column_order, vertices, panel_vertices, near_pairs):
    prepared = prepare(column_order, vertices, panel_vertices, near_pairs, charges.shape[0])
    potential_one = near_product(charges, prepared)
    potential_two = near_product(potential_one, prepared)
    return (potential_one, potential_two)


def solution(mesh):
    return jax.shard_map(
        body,
        mesh=mesh,
        in_specs=(P("row", "col", None, None), P(), P(), P(), P()),
        out_specs=(P("row", "col", None, None), P("row", "col", None, None)),
        check_vma=False,
    )
```

```python
import math

import jax
import jax.numpy as jnp
import numpy as np
from jax import lax
from jax.experimental import pallas as pl
from jax.experimental.pallas import tpu as pltpu
from jax.sharding import PartitionSpec as P

PANELS = 256
REACH = 3
QUAD_ROWS = 8
QUAD_COLS = 16
FEATURES = 32


def shifted(value, axis, by):
    length = lax.axis_size(axis)
    pairs = [(i, i + by) for i in range(length) if 0 <= i + by < length]
    return lax.ppermute(value, axis, pairs)


def rule_tables():
    gauss_two = np.array([-1.0, 1.0]) / math.sqrt(3.0)
    gauss_four = np.array(
        [-0.8611363115940526, -0.3399810435848563, 0.3399810435848563, 0.8611363115940526]
    )
    weight_four = np.array(
        [0.3478548451374538, 0.6521451548625461, 0.6521451548625461, 0.3478548451374538]
    )
    corner_weights = []
    point_weights = []
    for first_index in range(2):
        for second_index in range(4):
            along = 0.5 * (1.0 + gauss_two[first_index])
            across = 0.5 * (1.0 + gauss_four[second_index])
            corner_weights.append([along, (1.0 - along) * across, (1.0 - along) * (1.0 - across)])
            point_weights.append(2.0 * 0.5 * 0.5 * weight_four[second_index] * (1.0 - along))
    return (np.array(corner_weights), np.array(point_weights))


def block_corners(vertices, panel_vertices, block_ids, lattice_cols):
    patch_rows, patch_cols = QUAD_ROWS + 1, QUAD_COLS + 1
    panels = panel_vertices.reshape(3, -1, PANELS)[:, block_ids]
    lattice_row = panels // lattice_cols
    lattice_col = panels % lattice_cols
    base_row = jnp.min(lattice_row, axis=(0, 2))
    base_col = jnp.min(lattice_col, axis=(0, 2))
    local = (lattice_row - base_row[None, :, None]) * patch_cols + (
        lattice_col - base_col[None, :, None]
    )
    grid = jnp.transpose(vertices.reshape(3, -1, lattice_cols), (1, 0, 2))
    row_pick = (
        (base_row[:, None] + jnp.arange(patch_rows, dtype=jnp.int32))[:, :, None]
        == jnp.arange(grid.shape[0], dtype=jnp.int32)
    ).astype(jnp.float32)
    col_pick = (
        jnp.arange(lattice_cols, dtype=jnp.int32)[None, :, None]
        == (base_col[:, None] + jnp.arange(patch_cols, dtype=jnp.int32))[:, None, :]
    ).astype(jnp.float32)
    band = jnp.einsum("grR,Rxc->grxc", row_pick, grid, precision=lax.Precision.HIGHEST)
    patch = jnp.einsum("grxc,gcj->gxrj", band, col_pick, precision=lax.Precision.HIGHEST)
    patch = patch.reshape(block_ids.shape[0], 3, patch_rows * patch_cols)
    pick = (
        local[:, :, :, None] == jnp.arange(patch_rows * patch_cols, dtype=jnp.int32)
    ).astype(jnp.float32)
    return jnp.einsum("gxl,cgpl->gcxp", patch, pick, precision=lax.Precision.HIGHEST)


def block_geometry(vertices, panel_vertices, block_ids, lattice_cols):
    corners = block_corners(vertices, panel_vertices, block_ids, lattice_cols)
    centre = (corners[:, 0] + corners[:, 1] + corners[:, 2]) / 3.0
    first_edge = corners[:, 1] - corners[:, 0]
    second_edge = corners[:, 2] - corners[:, 0]
    normal_x = first_edge[:, 1] * second_edge[:, 2] - first_edge[:, 2] * second_edge[:, 1]
    normal_y = first_edge[:, 2] * second_edge[:, 0] - first_edge[:, 0] * second_edge[:, 2]
    normal_z = first_edge[:, 0] * second_edge[:, 1] - first_edge[:, 1] * second_edge[:, 0]
    panel_area = 0.5 * jnp.sqrt(normal_x * normal_x + normal_y * normal_y + normal_z * normal_z)
    corner_weights, _ = rule_tables()
    points = jnp.einsum(
        "kc,gcxp->gxkp",
        jnp.asarray(corner_weights, corners.dtype),
        corners,
        precision=lax.Precision.HIGHEST,
    )
    return (centre, points, panel_area)


def tile_block(target, source):
    target_centre, target_points, target_area = target
    source_centre, source_points, source_area = source
    _, point_weights = rule_tables()
    kernel_sum = jnp.zeros(
        (target_centre.shape[0], target_centre.shape[2], source_centre.shape[2]), jnp.float32
    )
    for point_index in range(8):
        weight = float(point_weights[point_index])
        distance = target_centre[:, :, :, None] - source_points[:, :, point_index, None, :]
        kernel_sum = kernel_sum + weight * lax.rsqrt(jnp.sum(distance * distance, axis=1) + 0.01)
        distance = target_points[:, :, point_index, :, None] - source_centre[:, :, None, :]
        kernel_sum = kernel_sum + weight * lax.rsqrt(jnp.sum(distance * distance, axis=1) + 0.01)
    return kernel_sum * target_area[:, :, None] * source_area[:, None, :] / (8.0 * math.pi)


def feature_rows(geometry):
    centre, points, area = geometry
    count = centre.shape[0]
    flat_points = jnp.transpose(points, (0, 2, 1, 3)).reshape(count, -1, PANELS)
    pad = jnp.zeros((count, FEATURES - 4 - flat_points.shape[1], PANELS), jnp.float32)
    return jnp.concatenate([centre, flat_points, area[:, None], pad], axis=1)


def pair_tile_block(target, source):
    _, point_weights = rule_tables()
    target_rows = feature_rows(target)
    source_rows = feature_rows(source)
    count = target_rows.shape[0]
    area_at = 3 + 3 * len(point_weights)
    chunk = 16

    def kernel(target_ref, source_ref, out_ref, turned_ref):
        turned_ref[...] = target_ref[0].T
        source_centre = [
            jnp.broadcast_to(source_ref[0, axis : axis + 1, :], (chunk, PANELS))
            for axis in range(3)
        ]
        source_area = source_ref[0, area_at : area_at + 1, :]

        def body(step, carry):
            rows = pl.ds(pl.multiple_of(step * chunk, chunk), chunk)
            held = turned_ref[rows, :]
            target_centre = [
                jnp.broadcast_to(held[:, axis : axis + 1], (chunk, PANELS)) for axis in range(3)
            ]
            total = jnp.zeros((chunk, PANELS), jnp.float32)
            for point_index, weight in enumerate(point_weights):
                at = 3 + 3 * point_index
                squared = 0.01
                for axis in range(3):
                    gap = target_centre[axis] - source_ref[0, at + axis : at + axis + 1, :]
                    squared = squared + gap * gap
                total = total + float(weight) * lax.rsqrt(squared)
                squared = 0.01
                for axis in range(3):
                    gap = held[:, at + axis : at + axis + 1] - source_centre[axis]
                    squared = squared + gap * gap
                total = total + float(weight) * lax.rsqrt(squared)
            scale = held[:, area_at : area_at + 1] * source_area
            out_ref[0, rows, :] = total * scale * (1.0 / (8.0 * math.pi))
            return carry

        lax.fori_loop(0, PANELS // chunk, body, 0)

    return pl.pallas_call(
        kernel,
        out_shape=jax.ShapeDtypeStruct((count, PANELS, PANELS), jnp.float32),
        grid=(count,),
        in_specs=[
            pl.BlockSpec((1, FEATURES, PANELS), lambda i: (i, 0, 0)),
            pl.BlockSpec((1, FEATURES, PANELS), lambda i: (i, 0, 0)),
        ],
        out_specs=pl.BlockSpec((1, PANELS, PANELS), lambda i: (i, 0, 0)),
        scratch_shapes=[pltpu.VMEM((PANELS, FEATURES), jnp.float32)],
        cost_estimate=pl.CostEstimate(
            flops=count * PANELS * PANELS * 16 * 11,
            transcendentals=count * PANELS * PANELS * 16,
            bytes_accessed=count * PANELS * (PANELS + 2 * FEATURES) * 4,
        ),
    )(target_rows, source_rows)


def self_tile_block(geometry):
    centre, points, area = geometry
    _, point_weights = rule_tables()
    half_sum = jnp.zeros((centre.shape[0], centre.shape[2], centre.shape[2]), jnp.float32)
    for point_index in range(8):
        weight = float(point_weights[point_index])
        distance = centre[:, :, :, None] - points[:, :, point_index, None, :]
        half_sum = half_sum + weight * lax.rsqrt(jnp.sum(distance * distance, axis=1) + 0.01)
    kernel_sum = half_sum + jnp.swapaxes(half_sum, 1, 2)
    return kernel_sum * area[:, :, None] * area[:, None, :] / (8.0 * math.pi)


def apply_tiles(source_values, tile_stack):
    return jnp.einsum("grq,gpq->grp", source_values, tile_stack, precision=lax.Precision.HIGHEST)


def apply_transposed(source_values, tile_stack):
    return jnp.einsum("grp,gpq->grq", source_values, tile_stack, precision=lax.Precision.HIGHEST)


def prepare(column_order, vertices, panel_vertices, near_pairs, band_rows):
    columns = lax.axis_size("col")
    band_count = lax.axis_size("row")
    band_index = lax.axis_index("row")
    column_index = lax.axis_index("col")
    positions = jnp.arange(columns, dtype=jnp.int32)
    position_of = jnp.sum(
        jnp.where(column_order[:, None] == positions[None, :], positions[:, None], 0), axis=0
    )
    home_column = jnp.sum(jnp.where(positions == column_index, column_order, 0))
    first_row = band_index * band_rows
    own_blocks = (first_row + jnp.arange(band_rows, dtype=jnp.int32)) * columns + home_column
    band_pairs = near_pairs.shape[1] // band_count
    share = band_pairs // columns
    segment = lax.dynamic_slice_in_dim(
        near_pairs, band_index * band_pairs + column_index * share, share, 1
    )
    low_blocks = segment[0]
    high_blocks = segment[1]
    targets = jnp.concatenate([own_blocks, low_blocks])
    lattice_cols = columns * QUAD_COLS + 1
    geometry = block_geometry(
        vertices, panel_vertices, jnp.concatenate([targets, high_blocks]), lattice_cols
    )
    target_geometry = [part[: targets.shape[0]] for part in geometry]
    source_geometry = [part[targets.shape[0] :] for part in geometry]
    self_tiles = self_tile_block([part[:band_rows] for part in target_geometry])
    pair_tiles = pair_tile_block([part[band_rows:] for part in target_geometry], source_geometry)
    low_row = low_blocks // columns - first_row
    high_row = high_blocks // columns - first_row
    low_pos = position_of[low_blocks % columns]
    high_pos = position_of[high_blocks % columns]
    slot_table = (low_row, low_pos, high_row, high_pos)
    return (self_tiles, pair_tiles, slot_table)


def near_product(block_values, later, prepared):
    self_tiles, pair_tiles, slot_table = prepared
    band_rows = block_values.shape[0]
    low_row, low_pos, high_row, high_pos = slot_table
    self_term = apply_tiles(block_values[:, 0], self_tiles)
    source_table = lax.all_gather(
        jnp.concatenate([block_values, later], axis=0), "col", axis=1, tiled=True
    )
    table_rows, columns = source_table.shape[:2]
    flat_table = source_table.reshape(table_rows * columns, -1)
    slots = jnp.arange(table_rows * columns, dtype=jnp.int32)
    low_pick = (slots[None, :] == (low_row * columns + low_pos)[:, None]).astype(jnp.float32)
    high_pick = (slots[None, :] == (high_row * columns + high_pos)[:, None]).astype(jnp.float32)
    shape = (low_row.shape[0],) + source_table.shape[2:]
    high_values = jnp.dot(high_pick, flat_table, precision=lax.Precision.HIGHEST).reshape(shape)
    low_values = jnp.dot(low_pick, flat_table, precision=lax.Precision.HIGHEST).reshape(shape)
    to_low = apply_tiles(high_values, pair_tiles).reshape(low_row.shape[0], -1)
    to_high = apply_transposed(low_values, pair_tiles).reshape(low_row.shape[0], -1)
    partial_value = jnp.dot(
        jnp.concatenate([low_pick, high_pick]).T,
        jnp.concatenate([to_low, to_high]),
        precision=lax.Precision.HIGHEST,
    ).reshape(source_table.shape)
    summed = jnp.sum(lax.all_to_all(partial_value, "col", 1, 1, tiled=True), axis=1)
    own_partial = summed[:band_rows] + self_term
    reaching = summed[band_rows:]
    carried_down = shifted(reaching, "row", 1)
    sent_up = shifted(own_partial[:REACH], "row", -1)
    head = own_partial[:REACH] + carried_down
    own = jnp.concatenate([head, own_partial[REACH:]], axis=0)[:, None]
    return own, (sent_up + reaching)[:, None]


def body(charges, column_order, vertices, panel_vertices, near_pairs):
    prepared = prepare(column_order, vertices, panel_vertices, near_pairs, charges.shape[0])
    later = shifted(charges[:REACH], "row", -1)
    potential_one, later_one = near_product(charges, later, prepared)
    potential_two, _ = near_product(potential_one, later_one, prepared)
    return (potential_one, potential_two)


def solution(mesh):
    return jax.shard_map(
        body,
        mesh=mesh,
        in_specs=(P("row", "col", None, None), P(), P(), P(), P()),
        out_specs=(P("row", "col", None, None), P("row", "col", None, None)),
        check_vma=False,
    )
```

```python
import math

import jax
import jax.numpy as jnp
import numpy as np
from jax import lax
from jax.experimental import pallas as pl
from jax.experimental.pallas import tpu as pltpu
from jax.sharding import PartitionSpec as P

PANELS = 256
REACH = 3
QUAD_ROWS = 8
QUAD_COLS = 16
FEATURES = 32


def shifted(value, axis, by):
    length = lax.axis_size(axis)
    pairs = [(i, i + by) for i in range(length) if 0 <= i + by < length]
    return lax.ppermute(value, axis, pairs)


def rule_tables():
    gauss_two = np.array([-1.0, 1.0]) / math.sqrt(3.0)
    gauss_four = np.array(
        [-0.8611363115940526, -0.3399810435848563, 0.3399810435848563, 0.8611363115940526]
    )
    weight_four = np.array(
        [0.3478548451374538, 0.6521451548625461, 0.6521451548625461, 0.3478548451374538]
    )
    corner_weights = []
    point_weights = []
    for first_index in range(2):
        for second_index in range(4):
            along = 0.5 * (1.0 + gauss_two[first_index])
            across = 0.5 * (1.0 + gauss_four[second_index])
            corner_weights.append([along, (1.0 - along) * across, (1.0 - along) * (1.0 - across)])
            point_weights.append(2.0 * 0.5 * 0.5 * weight_four[second_index] * (1.0 - along))
    return (np.array(corner_weights), np.array(point_weights))


def block_corners(vertices, panel_vertices, block_ids, lattice_cols):
    patch_rows, patch_cols = QUAD_ROWS + 1, QUAD_COLS + 1
    panels = panel_vertices.reshape(3, -1, PANELS)[:, block_ids]
    lattice_row = panels // lattice_cols
    lattice_col = panels % lattice_cols
    base_row = jnp.min(lattice_row, axis=(0, 2))
    base_col = jnp.min(lattice_col, axis=(0, 2))
    local = (lattice_row - base_row[None, :, None]) * patch_cols + (
        lattice_col - base_col[None, :, None]
    )
    grid = jnp.transpose(vertices.reshape(3, -1, lattice_cols), (1, 0, 2))
    row_pick = (
        (base_row[:, None] + jnp.arange(patch_rows, dtype=jnp.int32))[:, :, None]
        == jnp.arange(grid.shape[0], dtype=jnp.int32)
    ).astype(jnp.float32)
    col_pick = (
        jnp.arange(lattice_cols, dtype=jnp.int32)[None, :, None]
        == (base_col[:, None] + jnp.arange(patch_cols, dtype=jnp.int32))[:, None, :]
    ).astype(jnp.float32)
    band = jnp.einsum("grR,Rxc->grxc", row_pick, grid, precision=lax.Precision.HIGHEST)
    patch = jnp.einsum("grxc,gcj->gxrj", band, col_pick, precision=lax.Precision.HIGHEST)
    patch = patch.reshape(block_ids.shape[0], 3, patch_rows * patch_cols)
    pick = (
        local[:, :, :, None] == jnp.arange(patch_rows * patch_cols, dtype=jnp.int32)
    ).astype(jnp.float32)
    return jnp.einsum("gxl,cgpl->gcxp", patch, pick, precision=lax.Precision.HIGHEST)


def block_geometry(vertices, panel_vertices, block_ids, lattice_cols):
    corners = block_corners(vertices, panel_vertices, block_ids, lattice_cols)
    centre = (corners[:, 0] + corners[:, 1] + corners[:, 2]) / 3.0
    first_edge = corners[:, 1] - corners[:, 0]
    second_edge = corners[:, 2] - corners[:, 0]
    normal_x = first_edge[:, 1] * second_edge[:, 2] - first_edge[:, 2] * second_edge[:, 1]
    normal_y = first_edge[:, 2] * second_edge[:, 0] - first_edge[:, 0] * second_edge[:, 2]
    normal_z = first_edge[:, 0] * second_edge[:, 1] - first_edge[:, 1] * second_edge[:, 0]
    panel_area = 0.5 * jnp.sqrt(normal_x * normal_x + normal_y * normal_y + normal_z * normal_z)
    corner_weights, _ = rule_tables()
    points = jnp.einsum(
        "kc,gcxp->gxkp",
        jnp.asarray(corner_weights, corners.dtype),
        corners,
        precision=lax.Precision.HIGHEST,
    )
    return (centre, points, panel_area)


def tile_block(target, source):
    target_centre, target_points, target_area = target
    source_centre, source_points, source_area = source
    _, point_weights = rule_tables()
    kernel_sum = jnp.zeros(
        (target_centre.shape[0], target_centre.shape[2], source_centre.shape[2]), jnp.float32
    )
    for point_index in range(8):
        weight = float(point_weights[point_index])
        distance = target_centre[:, :, :, None] - source_points[:, :, point_index, None, :]
        kernel_sum = kernel_sum + weight * lax.rsqrt(jnp.sum(distance * distance, axis=1) + 0.01)
        distance = target_points[:, :, point_index, :, None] - source_centre[:, :, None, :]
        kernel_sum = kernel_sum + weight * lax.rsqrt(jnp.sum(distance * distance, axis=1) + 0.01)
    return kernel_sum * target_area[:, :, None] * source_area[:, None, :] / (8.0 * math.pi)


def feature_rows(geometry):
    centre, points, area = geometry
    count = centre.shape[0]
    flat_points = jnp.transpose(points, (0, 2, 1, 3)).reshape(count, -1, PANELS)
    pad = jnp.zeros((count, FEATURES - 4 - flat_points.shape[1], PANELS), jnp.float32)
    return jnp.concatenate([centre, flat_points, area[:, None], pad], axis=1)


def pair_tile_block(target, source):
    _, point_weights = rule_tables()
    target_rows = feature_rows(target)
    source_rows = feature_rows(source)
    count = target_rows.shape[0]
    chunk = 16

    def kernel(target_ref, source_ref, near_ref, far_ref, turned_target, turned_source):
        turned_target[...] = target_ref[0].T
        turned_source[...] = source_ref[0].T

        def body(step, carry):
            rows = pl.ds(pl.multiple_of(step * chunk, chunk), chunk)
            held_target = turned_target[rows, :]
            held_source = turned_source[rows, :]
            target_centre = [
                jnp.broadcast_to(held_target[:, axis : axis + 1], (chunk, PANELS))
                for axis in range(3)
            ]
            source_centre = [
                jnp.broadcast_to(held_source[:, axis : axis + 1], (chunk, PANELS))
                for axis in range(3)
            ]
            near = jnp.zeros((chunk, PANELS), jnp.float32)
            far = jnp.zeros((chunk, PANELS), jnp.float32)
            for point_index, weight in enumerate(point_weights):
                at = 3 + 3 * point_index
                squared = 0.01
                for axis in range(3):
                    gap = target_centre[axis] - source_ref[0, at + axis : at + axis + 1, :]
                    squared = squared + gap * gap
                near = near + float(weight) * lax.rsqrt(squared)
                squared = 0.01
                for axis in range(3):
                    gap = source_centre[axis] - target_ref[0, at + axis : at + axis + 1, :]
                    squared = squared + gap * gap
                far = far + float(weight) * lax.rsqrt(squared)
            near_ref[0, rows, :] = near
            far_ref[0, rows, :] = far
            return carry

        lax.fori_loop(0, PANELS // chunk, body, 0)

    tile_spec = pl.BlockSpec((1, PANELS, PANELS), lambda i: (i, 0, 0))
    near, far = pl.pallas_call(
        kernel,
        out_shape=[jax.ShapeDtypeStruct((count, PANELS, PANELS), jnp.float32)] * 2,
        grid=(count,),
        in_specs=[
            pl.BlockSpec((1, FEATURES, PANELS), lambda i: (i, 0, 0)),
            pl.BlockSpec((1, FEATURES, PANELS), lambda i: (i, 0, 0)),
        ],
        out_specs=[tile_spec, tile_spec],
        scratch_shapes=[
            pltpu.VMEM((PANELS, FEATURES), jnp.float32),
            pltpu.VMEM((PANELS, FEATURES), jnp.float32),
        ],
        cost_estimate=pl.CostEstimate(
            flops=count * PANELS * PANELS * 16 * 11,
            transcendentals=count * PANELS * PANELS * 16,
            bytes_accessed=count * PANELS * (2 * PANELS + 2 * FEATURES) * 4,
        ),
    )(target_rows, source_rows)
    target_area = target[2]
    source_area = source[2]
    kernel_sum = near + jnp.swapaxes(far, 1, 2)
    return kernel_sum * target_area[:, :, None] * source_area[:, None, :] / (8.0 * math.pi)


def self_tile_block(geometry):
    centre, points, area = geometry
    _, point_weights = rule_tables()
    half_sum = jnp.zeros((centre.shape[0], centre.shape[2], centre.shape[2]), jnp.float32)
    for point_index in range(8):
        weight = float(point_weights[point_index])
        distance = centre[:, :, :, None] - points[:, :, point_index, None, :]
        half_sum = half_sum + weight * lax.rsqrt(jnp.sum(distance * distance, axis=1) + 0.01)
    kernel_sum = half_sum + jnp.swapaxes(half_sum, 1, 2)
    return kernel_sum * area[:, :, None] * area[:, None, :] / (8.0 * math.pi)


def apply_tiles(source_values, tile_stack):
    return jnp.einsum("grq,gpq->grp", source_values, tile_stack, precision=lax.Precision.HIGHEST)


def apply_transposed(source_values, tile_stack):
    return jnp.einsum("grp,gpq->grq", source_values, tile_stack, precision=lax.Precision.HIGHEST)


def prepare(column_order, vertices, panel_vertices, near_pairs, band_rows):
    columns = lax.axis_size("col")
    band_count = lax.axis_size("row")
    band_index = lax.axis_index("row")
    column_index = lax.axis_index("col")
    positions = jnp.arange(columns, dtype=jnp.int32)
    position_of = jnp.sum(
        jnp.where(column_order[:, None] == positions[None, :], positions[:, None], 0), axis=0
    )
    home_column = jnp.sum(jnp.where(positions == column_index, column_order, 0))
    first_row = band_index * band_rows
    own_blocks = (first_row + jnp.arange(band_rows, dtype=jnp.int32)) * columns + home_column
    band_pairs = near_pairs.shape[1] // band_count
    share = band_pairs // columns
    segment = lax.dynamic_slice_in_dim(
        near_pairs, band_index * band_pairs + column_index * share, share, 1
    )
    low_blocks = segment[0]
    high_blocks = segment[1]
    targets = jnp.concatenate([own_blocks, low_blocks])
    lattice_cols = columns * QUAD_COLS + 1
    geometry = block_geometry(
        vertices, panel_vertices, jnp.concatenate([targets, high_blocks]), lattice_cols
    )
    target_geometry = [part[: targets.shape[0]] for part in geometry]
    source_geometry = [part[targets.shape[0] :] for part in geometry]
    self_tiles = self_tile_block([part[:band_rows] for part in target_geometry])
    pair_tiles = pair_tile_block([part[band_rows:] for part in target_geometry], source_geometry)
    low_row = low_blocks // columns - first_row
    high_row = high_blocks // columns - first_row
    low_pos = position_of[low_blocks % columns]
    high_pos = position_of[high_blocks % columns]
    slot_table = (low_row, low_pos, high_row, high_pos)
    return (self_tiles, pair_tiles, slot_table)


def near_product(block_values, later, prepared):
    self_tiles, pair_tiles, slot_table = prepared
    band_rows = block_values.shape[0]
    low_row, low_pos, high_row, high_pos = slot_table
    self_term = apply_tiles(block_values[:, 0], self_tiles)
    source_table = lax.all_gather(
        jnp.concatenate([block_values, later], axis=0), "col", axis=1, tiled=True
    )
    table_rows, columns = source_table.shape[:2]
    flat_table = source_table.reshape(table_rows * columns, -1)
    slots = jnp.arange(table_rows * columns, dtype=jnp.int32)
    low_pick = (slots[None, :] == (low_row * columns + low_pos)[:, None]).astype(jnp.float32)
    high_pick = (slots[None, :] == (high_row * columns + high_pos)[:, None]).astype(jnp.float32)
    shape = (low_row.shape[0],) + source_table.shape[2:]
    high_values = jnp.dot(high_pick, flat_table, precision=lax.Precision.HIGHEST).reshape(shape)
    low_values = jnp.dot(low_pick, flat_table, precision=lax.Precision.HIGHEST).reshape(shape)
    to_low = apply_tiles(high_values, pair_tiles).reshape(low_row.shape[0], -1)
    to_high = apply_transposed(low_values, pair_tiles).reshape(low_row.shape[0], -1)
    partial_value = jnp.dot(
        jnp.concatenate([low_pick, high_pick]).T,
        jnp.concatenate([to_low, to_high]),
        precision=lax.Precision.HIGHEST,
    ).reshape(source_table.shape)
    summed = jnp.sum(lax.all_to_all(partial_value, "col", 1, 1, tiled=True), axis=1)
    own_partial = summed[:band_rows] + self_term
    reaching = summed[band_rows:]
    carried_down = shifted(reaching, "row", 1)
    sent_up = shifted(own_partial[:REACH], "row", -1)
    head = own_partial[:REACH] + carried_down
    own = jnp.concatenate([head, own_partial[REACH:]], axis=0)[:, None]
    return own, (sent_up + reaching)[:, None]


def body(charges, column_order, vertices, panel_vertices, near_pairs):
    prepared = prepare(column_order, vertices, panel_vertices, near_pairs, charges.shape[0])
    later = shifted(charges[:REACH], "row", -1)
    potential_one, later_one = near_product(charges, later, prepared)
    potential_two, _ = near_product(potential_one, later_one, prepared)
    return (potential_one, potential_two)


def solution(mesh):
    return jax.shard_map(
        body,
        mesh=mesh,
        in_specs=(P("row", "col", None, None), P(), P(), P(), P()),
        out_specs=(P("row", "col", None, None), P("row", "col", None, None)),
        check_vma=False,
    )
```

```python
import math

import jax
import jax.numpy as jnp
import numpy as np
from jax import lax
from jax.experimental import pallas as pl
from jax.experimental.pallas import tpu as pltpu
from jax.sharding import PartitionSpec as P

PANELS = 256
REACH = 3
QUAD_ROWS = 8
QUAD_COLS = 16
FEATURES = 32


def shifted(value, axis, by):
    length = lax.axis_size(axis)
    pairs = [(i, i + by) for i in range(length) if 0 <= i + by < length]
    return lax.ppermute(value, axis, pairs)


def rule_tables():
    gauss_two = np.array([-1.0, 1.0]) / math.sqrt(3.0)
    gauss_four = np.array(
        [-0.8611363115940526, -0.3399810435848563, 0.3399810435848563, 0.8611363115940526]
    )
    weight_four = np.array(
        [0.3478548451374538, 0.6521451548625461, 0.6521451548625461, 0.3478548451374538]
    )
    corner_weights = []
    point_weights = []
    for first_index in range(2):
        for second_index in range(4):
            along = 0.5 * (1.0 + gauss_two[first_index])
            across = 0.5 * (1.0 + gauss_four[second_index])
            corner_weights.append([along, (1.0 - along) * across, (1.0 - along) * (1.0 - across)])
            point_weights.append(2.0 * 0.5 * 0.5 * weight_four[second_index] * (1.0 - along))
    return (np.array(corner_weights), np.array(point_weights))


def block_corners(vertices, panel_vertices, block_ids, lattice_cols):
    patch_rows, patch_cols = QUAD_ROWS + 1, QUAD_COLS + 1
    panels = panel_vertices.reshape(3, -1, PANELS)[:, block_ids]
    lattice_row = panels // lattice_cols
    lattice_col = panels % lattice_cols
    base_row = jnp.min(lattice_row, axis=(0, 2))
    base_col = jnp.min(lattice_col, axis=(0, 2))
    local = (lattice_row - base_row[None, :, None]) * patch_cols + (
        lattice_col - base_col[None, :, None]
    )
    grid = jnp.transpose(vertices.reshape(3, -1, lattice_cols), (1, 0, 2))
    row_pick = (
        (base_row[:, None] + jnp.arange(patch_rows, dtype=jnp.int32))[:, :, None]
        == jnp.arange(grid.shape[0], dtype=jnp.int32)
    ).astype(jnp.float32)
    col_pick = (
        jnp.arange(lattice_cols, dtype=jnp.int32)[None, :, None]
        == (base_col[:, None] + jnp.arange(patch_cols, dtype=jnp.int32))[:, None, :]
    ).astype(jnp.float32)
    band = jnp.einsum("grR,Rxc->grxc", row_pick, grid, precision=lax.Precision.HIGHEST)
    patch = jnp.einsum("grxc,gcj->gxrj", band, col_pick, precision=lax.Precision.HIGHEST)
    patch = patch.reshape(block_ids.shape[0], 3, patch_rows * patch_cols)
    pick = (
        local[:, :, :, None] == jnp.arange(patch_rows * patch_cols, dtype=jnp.int32)
    ).astype(jnp.float32)
    return jnp.einsum("gxl,cgpl->gcxp", patch, pick, precision=lax.Precision.HIGHEST)


def block_geometry(vertices, panel_vertices, block_ids, lattice_cols):
    corners = block_corners(vertices, panel_vertices, block_ids, lattice_cols)
    centre = (corners[:, 0] + corners[:, 1] + corners[:, 2]) / 3.0
    first_edge = corners[:, 1] - corners[:, 0]
    second_edge = corners[:, 2] - corners[:, 0]
    normal_x = first_edge[:, 1] * second_edge[:, 2] - first_edge[:, 2] * second_edge[:, 1]
    normal_y = first_edge[:, 2] * second_edge[:, 0] - first_edge[:, 0] * second_edge[:, 2]
    normal_z = first_edge[:, 0] * second_edge[:, 1] - first_edge[:, 1] * second_edge[:, 0]
    panel_area = 0.5 * jnp.sqrt(normal_x * normal_x + normal_y * normal_y + normal_z * normal_z)
    corner_weights, _ = rule_tables()
    points = jnp.einsum(
        "kc,gcxp->gxkp",
        jnp.asarray(corner_weights, corners.dtype),
        corners,
        precision=lax.Precision.HIGHEST,
    )
    return (centre, points, panel_area)


def tile_block(target, source):
    target_centre, target_points, target_area = target
    source_centre, source_points, source_area = source
    _, point_weights = rule_tables()
    kernel_sum = jnp.zeros(
        (target_centre.shape[0], target_centre.shape[2], source_centre.shape[2]), jnp.float32
    )
    for point_index in range(8):
        weight = float(point_weights[point_index])
        distance = target_centre[:, :, :, None] - source_points[:, :, point_index, None, :]
        kernel_sum = kernel_sum + weight * lax.rsqrt(jnp.sum(distance * distance, axis=1) + 0.01)
        distance = target_points[:, :, point_index, :, None] - source_centre[:, :, None, :]
        kernel_sum = kernel_sum + weight * lax.rsqrt(jnp.sum(distance * distance, axis=1) + 0.01)
    return kernel_sum * target_area[:, :, None] * source_area[:, None, :] / (8.0 * math.pi)


def feature_rows(geometry):
    centre, points, area = geometry
    count = centre.shape[0]
    flat_points = jnp.transpose(points, (0, 2, 1, 3)).reshape(count, -1, PANELS)
    pad = jnp.zeros((count, FEATURES - 4 - flat_points.shape[1], PANELS), jnp.float32)
    return jnp.concatenate([centre, flat_points, area[:, None], pad], axis=1)


def pair_tile_block(target, source):
    _, point_weights = rule_tables()
    target_rows = feature_rows(target)
    source_rows = feature_rows(source)
    count = target_rows.shape[0]
    area_at = 3 + 3 * len(point_weights)
    chunk = 16
    weight_groups = {}
    for point_index, weight in enumerate(point_weights):
        weight_groups.setdefault(float(weight), []).append(point_index)
    weight_groups = sorted(weight_groups.items())

    def kernel(target_ref, source_ref, out_ref, turned_ref):
        turned_ref[...] = target_ref[0].T
        source_centre = [
            jnp.broadcast_to(source_ref[0, axis : axis + 1, :], (chunk, PANELS))
            for axis in range(3)
        ]
        source_area = source_ref[0, area_at : area_at + 1, :]

        def body(step, carry):
            rows = pl.ds(pl.multiple_of(step * chunk, chunk), chunk)
            held = turned_ref[rows, :]
            target_centre = [
                jnp.broadcast_to(held[:, axis : axis + 1], (chunk, PANELS)) for axis in range(3)
            ]
            total = jnp.zeros((chunk, PANELS), jnp.float32)
            for weight, group in weight_groups:
                grouped = jnp.zeros((chunk, PANELS), jnp.float32)
                for point_index in group:
                    at = 3 + 3 * point_index
                    squared = 0.01
                    for axis in range(3):
                        gap = target_centre[axis] - source_ref[0, at + axis : at + axis + 1, :]
                        squared = squared + gap * gap
                    grouped = grouped + lax.rsqrt(squared)
                    squared = 0.01
                    for axis in range(3):
                        gap = held[:, at + axis : at + axis + 1] - source_centre[axis]
                        squared = squared + gap * gap
                    grouped = grouped + lax.rsqrt(squared)
                total = total + weight * grouped
            scale = held[:, area_at : area_at + 1] * source_area
            out_ref[0, rows, :] = total * scale * (1.0 / (8.0 * math.pi))
            return carry

        lax.fori_loop(0, PANELS // chunk, body, 0)

    return pl.pallas_call(
        kernel,
        out_shape=jax.ShapeDtypeStruct((count, PANELS, PANELS), jnp.float32),
        grid=(count,),
        in_specs=[
            pl.BlockSpec((1, FEATURES, PANELS), lambda i: (i, 0, 0)),
            pl.BlockSpec((1, FEATURES, PANELS), lambda i: (i, 0, 0)),
        ],
        out_specs=pl.BlockSpec((1, PANELS, PANELS), lambda i: (i, 0, 0)),
        scratch_shapes=[pltpu.VMEM((PANELS, FEATURES), jnp.float32)],
        cost_estimate=pl.CostEstimate(
            flops=count * PANELS * PANELS * 16 * 11,
            transcendentals=count * PANELS * PANELS * 16,
            bytes_accessed=count * PANELS * (PANELS + 2 * FEATURES) * 4,
        ),
    )(target_rows, source_rows)


def self_tile_block(geometry):
    centre, points, area = geometry
    _, point_weights = rule_tables()
    half_sum = jnp.zeros((centre.shape[0], centre.shape[2], centre.shape[2]), jnp.float32)
    for point_index in range(8):
        weight = float(point_weights[point_index])
        distance = centre[:, :, :, None] - points[:, :, point_index, None, :]
        half_sum = half_sum + weight * lax.rsqrt(jnp.sum(distance * distance, axis=1) + 0.01)
    kernel_sum = half_sum + jnp.swapaxes(half_sum, 1, 2)
    return kernel_sum * area[:, :, None] * area[:, None, :] / (8.0 * math.pi)


def apply_tiles(source_values, tile_stack):
    return jnp.einsum("grq,gpq->grp", source_values, tile_stack, precision=lax.Precision.HIGHEST)


def apply_transposed(source_values, tile_stack):
    return jnp.einsum("grp,gpq->grq", source_values, tile_stack, precision=lax.Precision.HIGHEST)


def prepare(column_order, vertices, panel_vertices, near_pairs, band_rows):
    columns = lax.axis_size("col")
    band_count = lax.axis_size("row")
    band_index = lax.axis_index("row")
    column_index = lax.axis_index("col")
    positions = jnp.arange(columns, dtype=jnp.int32)
    position_of = jnp.sum(
        jnp.where(column_order[:, None] == positions[None, :], positions[:, None], 0), axis=0
    )
    home_column = jnp.sum(jnp.where(positions == column_index, column_order, 0))
    first_row = band_index * band_rows
    own_blocks = (first_row + jnp.arange(band_rows, dtype=jnp.int32)) * columns + home_column
    band_pairs = near_pairs.shape[1] // band_count
    share = band_pairs // columns
    segment = lax.dynamic_slice_in_dim(
        near_pairs, band_index * band_pairs + column_index * share, share, 1
    )
    low_blocks = segment[0]
    high_blocks = segment[1]
    targets = jnp.concatenate([own_blocks, low_blocks])
    lattice_cols = columns * QUAD_COLS + 1
    geometry = block_geometry(
        vertices, panel_vertices, jnp.concatenate([targets, high_blocks]), lattice_cols
    )
    target_geometry = [part[: targets.shape[0]] for part in geometry]
    source_geometry = [part[targets.shape[0] :] for part in geometry]
    self_tiles = self_tile_block([part[:band_rows] for part in target_geometry])
    pair_tiles = pair_tile_block([part[band_rows:] for part in target_geometry], source_geometry)
    low_row = low_blocks // columns - first_row
    high_row = high_blocks // columns - first_row
    low_pos = position_of[low_blocks % columns]
    high_pos = position_of[high_blocks % columns]
    slot_table = (low_row, low_pos, high_row, high_pos)
    return (self_tiles, pair_tiles, slot_table)


def near_product(block_values, later, prepared):
    self_tiles, pair_tiles, slot_table = prepared
    band_rows = block_values.shape[0]
    low_row, low_pos, high_row, high_pos = slot_table
    self_term = apply_tiles(block_values[:, 0], self_tiles)
    source_table = lax.all_gather(
        jnp.concatenate([block_values, later], axis=0), "col", axis=1, tiled=True
    )
    table_rows, columns = source_table.shape[:2]
    flat_table = source_table.reshape(table_rows * columns, -1)
    slots = jnp.arange(table_rows * columns, dtype=jnp.int32)
    low_pick = (slots[None, :] == (low_row * columns + low_pos)[:, None]).astype(jnp.float32)
    high_pick = (slots[None, :] == (high_row * columns + high_pos)[:, None]).astype(jnp.float32)
    shape = (low_row.shape[0],) + source_table.shape[2:]
    high_values = jnp.dot(high_pick, flat_table, precision=lax.Precision.HIGHEST).reshape(shape)
    low_values = jnp.dot(low_pick, flat_table, precision=lax.Precision.HIGHEST).reshape(shape)
    to_low = apply_tiles(high_values, pair_tiles).reshape(low_row.shape[0], -1)
    to_high = apply_transposed(low_values, pair_tiles).reshape(low_row.shape[0], -1)
    partial_value = jnp.dot(
        jnp.concatenate([low_pick, high_pick]).T,
        jnp.concatenate([to_low, to_high]),
        precision=lax.Precision.HIGHEST,
    ).reshape(source_table.shape)
    summed = jnp.sum(lax.all_to_all(partial_value, "col", 1, 1, tiled=True), axis=1)
    own_partial = summed[:band_rows] + self_term
    reaching = summed[band_rows:]
    carried_down = shifted(reaching, "row", 1)
    sent_up = shifted(own_partial[:REACH], "row", -1)
    head = own_partial[:REACH] + carried_down
    own = jnp.concatenate([head, own_partial[REACH:]], axis=0)[:, None]
    return own, (sent_up + reaching)[:, None]


def body(charges, column_order, vertices, panel_vertices, near_pairs):
    prepared = prepare(column_order, vertices, panel_vertices, near_pairs, charges.shape[0])
    later = shifted(charges[:REACH], "row", -1)
    potential_one, later_one = near_product(charges, later, prepared)
    potential_two, _ = near_product(potential_one, later_one, prepared)
    return (potential_one, potential_two)


def solution(mesh):
    return jax.shard_map(
        body,
        mesh=mesh,
        in_specs=(P("row", "col", None, None), P(), P(), P(), P()),
        out_specs=(P("row", "col", None, None), P("row", "col", None, None)),
        check_vma=False,
    )
```

```python
import math

import jax
import jax.numpy as jnp
import numpy as np
from jax import lax
from jax.experimental import pallas as pl
from jax.experimental.pallas import tpu as pltpu
from jax.sharding import PartitionSpec as P

PANELS = 256
REACH = 3
QUAD_ROWS = 8
QUAD_COLS = 16
FEATURES = 32


def shifted(value, axis, by):
    length = lax.axis_size(axis)
    pairs = [(i, i + by) for i in range(length) if 0 <= i + by < length]
    return lax.ppermute(value, axis, pairs)


def rule_tables():
    gauss_two = np.array([-1.0, 1.0]) / math.sqrt(3.0)
    gauss_four = np.array(
        [-0.8611363115940526, -0.3399810435848563, 0.3399810435848563, 0.8611363115940526]
    )
    weight_four = np.array(
        [0.3478548451374538, 0.6521451548625461, 0.6521451548625461, 0.3478548451374538]
    )
    corner_weights = []
    point_weights = []
    for first_index in range(2):
        for second_index in range(4):
            along = 0.5 * (1.0 + gauss_two[first_index])
            across = 0.5 * (1.0 + gauss_four[second_index])
            corner_weights.append([along, (1.0 - along) * across, (1.0 - along) * (1.0 - across)])
            point_weights.append(2.0 * 0.5 * 0.5 * weight_four[second_index] * (1.0 - along))
    return (np.array(corner_weights), np.array(point_weights))


def block_corners(vertices, panel_vertices, block_ids, lattice_cols):
    patch_rows, patch_cols = QUAD_ROWS + 1, QUAD_COLS + 1
    panels = panel_vertices.reshape(3, -1, PANELS)[:, block_ids]
    lattice_row = panels // lattice_cols
    lattice_col = panels % lattice_cols
    base_row = jnp.min(lattice_row, axis=(0, 2))
    base_col = jnp.min(lattice_col, axis=(0, 2))
    local = (lattice_row - base_row[None, :, None]) * patch_cols + (
        lattice_col - base_col[None, :, None]
    )
    grid = jnp.transpose(vertices.reshape(3, -1, lattice_cols), (1, 0, 2))
    row_pick = (
        (base_row[:, None] + jnp.arange(patch_rows, dtype=jnp.int32))[:, :, None]
        == jnp.arange(grid.shape[0], dtype=jnp.int32)
    ).astype(jnp.float32)
    col_pick = (
        jnp.arange(lattice_cols, dtype=jnp.int32)[None, :, None]
        == (base_col[:, None] + jnp.arange(patch_cols, dtype=jnp.int32))[:, None, :]
    ).astype(jnp.float32)
    band = jnp.einsum("grR,Rxc->grxc", row_pick, grid, precision=lax.Precision.HIGHEST)
    patch = jnp.einsum("grxc,gcj->gxrj", band, col_pick, precision=lax.Precision.HIGHEST)
    patch = patch.reshape(block_ids.shape[0], 3, patch_rows * patch_cols)
    pick = (
        local[:, :, :, None] == jnp.arange(patch_rows * patch_cols, dtype=jnp.int32)
    ).astype(jnp.float32)
    return jnp.einsum("gxl,cgpl->gcxp", patch, pick, precision=lax.Precision.HIGHEST)


def block_geometry(vertices, panel_vertices, block_ids, lattice_cols):
    corners = block_corners(vertices, panel_vertices, block_ids, lattice_cols)
    centre = (corners[:, 0] + corners[:, 1] + corners[:, 2]) / 3.0
    first_edge = corners[:, 1] - corners[:, 0]
    second_edge = corners[:, 2] - corners[:, 0]
    normal_x = first_edge[:, 1] * second_edge[:, 2] - first_edge[:, 2] * second_edge[:, 1]
    normal_y = first_edge[:, 2] * second_edge[:, 0] - first_edge[:, 0] * second_edge[:, 2]
    normal_z = first_edge[:, 0] * second_edge[:, 1] - first_edge[:, 1] * second_edge[:, 0]
    panel_area = 0.5 * jnp.sqrt(normal_x * normal_x + normal_y * normal_y + normal_z * normal_z)
    corner_weights, _ = rule_tables()
    points = jnp.einsum(
        "kc,gcxp->gxkp",
        jnp.asarray(corner_weights, corners.dtype),
        corners,
        precision=lax.Precision.HIGHEST,
    )
    return (centre, points, panel_area)


def tile_block(target, source):
    target_centre, target_points, target_area = target
    source_centre, source_points, source_area = source
    _, point_weights = rule_tables()
    kernel_sum = jnp.zeros(
        (target_centre.shape[0], target_centre.shape[2], source_centre.shape[2]), jnp.float32
    )
    for point_index in range(8):
        weight = float(point_weights[point_index])
        distance = target_centre[:, :, :, None] - source_points[:, :, point_index, None, :]
        kernel_sum = kernel_sum + weight * lax.rsqrt(jnp.sum(distance * distance, axis=1) + 0.01)
        distance = target_points[:, :, point_index, :, None] - source_centre[:, :, None, :]
        kernel_sum = kernel_sum + weight * lax.rsqrt(jnp.sum(distance * distance, axis=1) + 0.01)
    return kernel_sum * target_area[:, :, None] * source_area[:, None, :] / (8.0 * math.pi)


def feature_rows(geometry):
    centre, points, area = geometry
    count = centre.shape[0]
    flat_points = jnp.transpose(points, (0, 2, 1, 3)).reshape(count, -1, PANELS)
    pad = jnp.zeros((count, FEATURES - 4 - flat_points.shape[1], PANELS), jnp.float32)
    return jnp.concatenate([centre, flat_points, area[:, None], pad], axis=1)


def pair_tile_block(target, source):
    _, point_weights = rule_tables()
    target_rows = feature_rows(target)
    source_rows = feature_rows(source)
    count = target_rows.shape[0]
    area_at = 3 + 3 * len(point_weights)
    chunk = 16

    def kernel(target_ref, source_ref, out_ref, turned_ref):
        turned_ref[...] = target_ref[0].T
        source_centre = [
            jnp.broadcast_to(source_ref[0, axis : axis + 1, :], (chunk, PANELS))
            for axis in range(3)
        ]
        source_area = source_ref[0, area_at : area_at + 1, :]

        def body(step, carry):
            rows = pl.ds(pl.multiple_of(step * chunk, chunk), chunk)
            held = turned_ref[rows, :]
            target_centre = [
                jnp.broadcast_to(held[:, axis : axis + 1], (chunk, PANELS)) for axis in range(3)
            ]
            total = jnp.zeros((chunk, PANELS), jnp.float32)
            for point_index, weight in enumerate(point_weights):
                at = 3 + 3 * point_index
                squared = 0.01
                for axis in range(3):
                    gap = target_centre[axis] - source_ref[0, at + axis : at + axis + 1, :]
                    squared = squared + gap * gap
                total = total + float(weight) * lax.rsqrt(squared)
                squared = 0.01
                for axis in range(3):
                    gap = held[:, at + axis : at + axis + 1] - source_centre[axis]
                    squared = squared + gap * gap
                total = total + float(weight) * lax.rsqrt(squared)
            scale = held[:, area_at : area_at + 1] * source_area
            out_ref[0, rows, :] = total * scale * (1.0 / (8.0 * math.pi))
            return carry

        lax.fori_loop(0, PANELS // chunk, body, 0)

    return pl.pallas_call(
        kernel,
        out_shape=jax.ShapeDtypeStruct((count, PANELS, PANELS), jnp.float32),
        grid=(count,),
        in_specs=[
            pl.BlockSpec((1, FEATURES, PANELS), lambda i: (i, 0, 0)),
            pl.BlockSpec((1, FEATURES, PANELS), lambda i: (i, 0, 0)),
        ],
        out_specs=pl.BlockSpec((1, PANELS, PANELS), lambda i: (i, 0, 0)),
        scratch_shapes=[pltpu.VMEM((PANELS, FEATURES), jnp.float32)],
        cost_estimate=pl.CostEstimate(
            flops=count * PANELS * PANELS * 16 * 11,
            transcendentals=count * PANELS * PANELS * 16,
            bytes_accessed=count * PANELS * (PANELS + 2 * FEATURES) * 4,
        ),
    )(target_rows, source_rows)


def self_tile_block(geometry):
    centre, points, area = geometry
    _, point_weights = rule_tables()
    half_sum = jnp.zeros((centre.shape[0], centre.shape[2], centre.shape[2]), jnp.float32)
    for point_index in range(8):
        weight = float(point_weights[point_index])
        distance = centre[:, :, :, None] - points[:, :, point_index, None, :]
        half_sum = half_sum + weight * lax.rsqrt(jnp.sum(distance * distance, axis=1) + 0.01)
    kernel_sum = half_sum + jnp.swapaxes(half_sum, 1, 2)
    return kernel_sum * area[:, :, None] * area[:, None, :] / (8.0 * math.pi)


def apply_tiles(source_values, tile_stack):
    return jnp.einsum("grq,gpq->grp", source_values, tile_stack, precision=lax.Precision.HIGHEST)


def apply_transposed(source_values, tile_stack):
    return jnp.einsum("grp,gpq->grq", source_values, tile_stack, precision=lax.Precision.HIGHEST)


def prepare(column_order, vertices, panel_vertices, near_pairs, band_rows, later):
    columns = lax.axis_size("col")
    band_count = lax.axis_size("row")
    band_index = lax.axis_index("row")
    column_index = lax.axis_index("col")
    positions = jnp.arange(columns, dtype=jnp.int32)
    position_of = jnp.sum(
        jnp.where(column_order[:, None] == positions[None, :], positions[:, None], 0), axis=0
    )
    home_column = jnp.sum(jnp.where(positions == column_index, column_order, 0))
    first_row = band_index * band_rows
    own_blocks = (first_row + jnp.arange(band_rows, dtype=jnp.int32)) * columns + home_column
    band_pairs = near_pairs.shape[1] // band_count
    share = band_pairs // columns
    segment = lax.dynamic_slice_in_dim(
        near_pairs, band_index * band_pairs + column_index * share, share, 1
    )
    low_blocks = segment[0]
    high_blocks = segment[1]
    targets = jnp.concatenate([own_blocks, low_blocks])
    lattice_cols = columns * QUAD_COLS + 1
    geometry = block_geometry(
        vertices, panel_vertices, jnp.concatenate([targets, high_blocks]), lattice_cols
    )
    geometry, later = lax.optimization_barrier((geometry, later))
    target_geometry = [part[: targets.shape[0]] for part in geometry]
    source_geometry = [part[targets.shape[0] :] for part in geometry]
    self_tiles = self_tile_block([part[:band_rows] for part in target_geometry])
    pair_tiles = pair_tile_block([part[band_rows:] for part in target_geometry], source_geometry)
    low_row = low_blocks // columns - first_row
    high_row = high_blocks // columns - first_row
    low_pos = position_of[low_blocks % columns]
    high_pos = position_of[high_blocks % columns]
    slot_table = (low_row, low_pos, high_row, high_pos)
    return (self_tiles, pair_tiles, slot_table), later


def near_product(block_values, later, prepared):
    self_tiles, pair_tiles, slot_table = prepared
    band_rows = block_values.shape[0]
    low_row, low_pos, high_row, high_pos = slot_table
    self_term = apply_tiles(block_values[:, 0], self_tiles)
    source_table = lax.all_gather(
        jnp.concatenate([block_values, later], axis=0), "col", axis=1, tiled=True
    )
    table_rows, columns = source_table.shape[:2]
    flat_table = source_table.reshape(table_rows * columns, -1)
    slots = jnp.arange(table_rows * columns, dtype=jnp.int32)
    low_pick = (slots[None, :] == (low_row * columns + low_pos)[:, None]).astype(jnp.float32)
    high_pick = (slots[None, :] == (high_row * columns + high_pos)[:, None]).astype(jnp.float32)
    shape = (low_row.shape[0],) + source_table.shape[2:]
    high_values = jnp.dot(high_pick, flat_table, precision=lax.Precision.HIGHEST).reshape(shape)
    low_values = jnp.dot(low_pick, flat_table, precision=lax.Precision.HIGHEST).reshape(shape)
    to_low = apply_tiles(high_values, pair_tiles).reshape(low_row.shape[0], -1)
    to_high = apply_transposed(low_values, pair_tiles).reshape(low_row.shape[0], -1)
    partial_value = jnp.dot(
        jnp.concatenate([low_pick, high_pick]).T,
        jnp.concatenate([to_low, to_high]),
        precision=lax.Precision.HIGHEST,
    ).reshape(source_table.shape)
    summed = jnp.sum(lax.all_to_all(partial_value, "col", 1, 1, tiled=True), axis=1)
    own_partial = summed[:band_rows] + self_term
    reaching = summed[band_rows:]
    carried_down = shifted(reaching, "row", 1)
    sent_up = shifted(own_partial[:REACH], "row", -1)
    head = own_partial[:REACH] + carried_down
    own = jnp.concatenate([head, own_partial[REACH:]], axis=0)[:, None]
    return own, (sent_up + reaching)[:, None]


def body(charges, column_order, vertices, panel_vertices, near_pairs):
    later = shifted(charges[:REACH], "row", -1)
    prepared, later = prepare(
        column_order, vertices, panel_vertices, near_pairs, charges.shape[0], later
    )
    potential_one, later_one = near_product(charges, later, prepared)
    potential_two, _ = near_product(potential_one, later_one, prepared)
    return (potential_one, potential_two)


def solution(mesh):
    return jax.shard_map(
        body,
        mesh=mesh,
        in_specs=(P("row", "col", None, None), P(), P(), P(), P()),
        out_specs=(P("row", "col", None, None), P("row", "col", None, None)),
        check_vma=False,
    )
```

```python
import math

import jax
import jax.numpy as jnp
import numpy as np
from jax import lax
from jax.experimental import pallas as pl
from jax.experimental.pallas import tpu as pltpu
from jax.sharding import PartitionSpec as P

PANELS = 256
REACH = 3
QUAD_ROWS = 8
QUAD_COLS = 16
FEATURES = 32


def shifted(value, axis, by):
    length = lax.axis_size(axis)
    pairs = [(i, i + by) for i in range(length) if 0 <= i + by < length]
    return lax.ppermute(value, axis, pairs)


def rule_tables():
    gauss_two = np.array([-1.0, 1.0]) / math.sqrt(3.0)
    gauss_four = np.array(
        [-0.8611363115940526, -0.3399810435848563, 0.3399810435848563, 0.8611363115940526]
    )
    weight_four = np.array(
        [0.3478548451374538, 0.6521451548625461, 0.6521451548625461, 0.3478548451374538]
    )
    corner_weights = []
    point_weights = []
    for first_index in range(2):
        for second_index in range(4):
            along = 0.5 * (1.0 + gauss_two[first_index])
            across = 0.5 * (1.0 + gauss_four[second_index])
            corner_weights.append([along, (1.0 - along) * across, (1.0 - along) * (1.0 - across)])
            point_weights.append(2.0 * 0.5 * 0.5 * weight_four[second_index] * (1.0 - along))
    return (np.array(corner_weights), np.array(point_weights))


def block_corners(vertices, panel_vertices, block_ids, lattice_cols):
    patch_rows, patch_cols = QUAD_ROWS + 1, QUAD_COLS + 1
    panels = panel_vertices.reshape(3, -1, PANELS)[:, block_ids]
    lattice_row = panels // lattice_cols
    lattice_col = panels % lattice_cols
    base_row = jnp.min(lattice_row, axis=(0, 2))
    base_col = jnp.min(lattice_col, axis=(0, 2))
    local = (lattice_row - base_row[None, :, None]) * patch_cols + (
        lattice_col - base_col[None, :, None]
    )
    grid = jnp.transpose(vertices.reshape(3, -1, lattice_cols), (1, 0, 2))
    row_pick = (
        (base_row[:, None] + jnp.arange(patch_rows, dtype=jnp.int32))[:, :, None]
        == jnp.arange(grid.shape[0], dtype=jnp.int32)
    ).astype(jnp.float32)
    col_pick = (
        jnp.arange(lattice_cols, dtype=jnp.int32)[None, :, None]
        == (base_col[:, None] + jnp.arange(patch_cols, dtype=jnp.int32))[:, None, :]
    ).astype(jnp.float32)
    band = jnp.einsum("grR,Rxc->grxc", row_pick, grid, precision=lax.Precision.HIGHEST)
    patch = jnp.einsum("grxc,gcj->gxrj", band, col_pick, precision=lax.Precision.HIGHEST)
    patch = patch.reshape(block_ids.shape[0], 3, patch_rows * patch_cols)
    pick = (
        local[:, :, :, None] == jnp.arange(patch_rows * patch_cols, dtype=jnp.int32)
    ).astype(jnp.float32)
    return jnp.einsum("gxl,cgpl->gcxp", patch, pick, precision=lax.Precision.HIGHEST)


def block_geometry(vertices, panel_vertices, block_ids, lattice_cols):
    corners = block_corners(vertices, panel_vertices, block_ids, lattice_cols)
    centre = (corners[:, 0] + corners[:, 1] + corners[:, 2]) / 3.0
    first_edge = corners[:, 1] - corners[:, 0]
    second_edge = corners[:, 2] - corners[:, 0]
    normal_x = first_edge[:, 1] * second_edge[:, 2] - first_edge[:, 2] * second_edge[:, 1]
    normal_y = first_edge[:, 2] * second_edge[:, 0] - first_edge[:, 0] * second_edge[:, 2]
    normal_z = first_edge[:, 0] * second_edge[:, 1] - first_edge[:, 1] * second_edge[:, 0]
    panel_area = 0.5 * jnp.sqrt(normal_x * normal_x + normal_y * normal_y + normal_z * normal_z)
    corner_weights, _ = rule_tables()
    points = jnp.einsum(
        "kc,gcxp->gxkp",
        jnp.asarray(corner_weights, corners.dtype),
        corners,
        precision=lax.Precision.HIGHEST,
    )
    return (centre, points, panel_area)


def tile_block(target, source):
    target_centre, target_points, target_area = target
    source_centre, source_points, source_area = source
    _, point_weights = rule_tables()
    kernel_sum = jnp.zeros(
        (target_centre.shape[0], target_centre.shape[2], source_centre.shape[2]), jnp.float32
    )
    for point_index in range(8):
        weight = float(point_weights[point_index])
        distance = target_centre[:, :, :, None] - source_points[:, :, point_index, None, :]
        kernel_sum = kernel_sum + weight * lax.rsqrt(jnp.sum(distance * distance, axis=1) + 0.01)
        distance = target_points[:, :, point_index, :, None] - source_centre[:, :, None, :]
        kernel_sum = kernel_sum + weight * lax.rsqrt(jnp.sum(distance * distance, axis=1) + 0.01)
    return kernel_sum * target_area[:, :, None] * source_area[:, None, :] / (8.0 * math.pi)


def feature_rows(geometry):
    centre, points, area = geometry
    count = centre.shape[0]
    flat_points = jnp.transpose(points, (0, 2, 1, 3)).reshape(count, -1, PANELS)
    pad = jnp.zeros((count, FEATURES - 4 - flat_points.shape[1], PANELS), jnp.float32)
    return jnp.concatenate([centre, flat_points, area[:, None], pad], axis=1)


def pair_tile_block(target, source):
    _, point_weights = rule_tables()
    target_rows = feature_rows(target)
    source_rows = feature_rows(source)
    count = target_rows.shape[0]
    area_at = 3 + 3 * len(point_weights)
    chunk = 16

    def kernel(target_ref, source_ref, out_ref, turned_ref):
        turned_ref[...] = target_ref[0].T
        source_centre = [
            jnp.broadcast_to(source_ref[0, axis : axis + 1, :], (chunk, PANELS))
            for axis in range(3)
        ]
        source_area = source_ref[0, area_at : area_at + 1, :]

        def body(step, carry):
            rows = pl.ds(pl.multiple_of(step * chunk, chunk), chunk)
            held = turned_ref[rows, :]
            target_centre = [
                jnp.broadcast_to(held[:, axis : axis + 1], (chunk, PANELS)) for axis in range(3)
            ]
            total = jnp.zeros((chunk, PANELS), jnp.float32)
            for point_index, weight in enumerate(point_weights):
                at = 3 + 3 * point_index
                squared = 0.01
                for axis in range(3):
                    gap = target_centre[axis] - source_ref[0, at + axis : at + axis + 1, :]
                    squared = squared + gap * gap
                total = total + float(weight) * lax.rsqrt(squared)
                squared = 0.01
                for axis in range(3):
                    gap = held[:, at + axis : at + axis + 1] - source_centre[axis]
                    squared = squared + gap * gap
                total = total + float(weight) * lax.rsqrt(squared)
            scale = held[:, area_at : area_at + 1] * source_area
            out_ref[0, rows, :] = total * scale * (1.0 / (8.0 * math.pi))
            return carry

        lax.fori_loop(0, PANELS // chunk, body, 0)

    return pl.pallas_call(
        kernel,
        out_shape=jax.ShapeDtypeStruct((count, PANELS, PANELS), jnp.float32),
        grid=(count,),
        in_specs=[
            pl.BlockSpec((1, FEATURES, PANELS), lambda i: (i, 0, 0)),
            pl.BlockSpec((1, FEATURES, PANELS), lambda i: (i, 0, 0)),
        ],
        out_specs=pl.BlockSpec((1, PANELS, PANELS), lambda i: (i, 0, 0)),
        scratch_shapes=[pltpu.VMEM((PANELS, FEATURES), jnp.float32)],
        cost_estimate=pl.CostEstimate(
            flops=count * PANELS * PANELS * 16 * 11,
            transcendentals=count * PANELS * PANELS * 16,
            bytes_accessed=count * PANELS * (PANELS + 2 * FEATURES) * 4,
        ),
    )(target_rows, source_rows)


def self_tile_block(geometry):
    centre, points, area = geometry
    _, point_weights = rule_tables()
    half_sum = jnp.zeros((centre.shape[0], centre.shape[2], centre.shape[2]), jnp.float32)
    for point_index in range(8):
        weight = float(point_weights[point_index])
        distance = centre[:, :, :, None] - points[:, :, point_index, None, :]
        half_sum = half_sum + weight * lax.rsqrt(jnp.sum(distance * distance, axis=1) + 0.01)
    kernel_sum = half_sum + jnp.swapaxes(half_sum, 1, 2)
    return kernel_sum * area[:, :, None] * area[:, None, :] / (8.0 * math.pi)


def apply_tiles(source_values, tile_stack):
    return jnp.einsum("grq,gpq->grp", source_values, tile_stack, precision=lax.Precision.HIGHEST)


def apply_transposed(source_values, tile_stack):
    return jnp.einsum("grp,gpq->grq", source_values, tile_stack, precision=lax.Precision.HIGHEST)


def prepare(column_order, vertices, panel_vertices, near_pairs, band_rows, later):
    columns = lax.axis_size("col")
    band_count = lax.axis_size("row")
    band_index = lax.axis_index("row")
    column_index = lax.axis_index("col")
    positions = jnp.arange(columns, dtype=jnp.int32)
    position_of = jnp.sum(
        jnp.where(column_order[:, None] == positions[None, :], positions[:, None], 0), axis=0
    )
    home_column = jnp.sum(jnp.where(positions == column_index, column_order, 0))
    first_row = band_index * band_rows
    own_blocks = (first_row + jnp.arange(band_rows, dtype=jnp.int32)) * columns + home_column
    band_pairs = near_pairs.shape[1] // band_count
    share = band_pairs // columns
    segment = lax.dynamic_slice_in_dim(
        near_pairs, band_index * band_pairs + column_index * share, share, 1
    )
    low_blocks = segment[0]
    high_blocks = segment[1]
    targets = jnp.concatenate([own_blocks, low_blocks])
    lattice_cols = columns * QUAD_COLS + 1
    geometry = block_geometry(
        vertices, panel_vertices, jnp.concatenate([targets, high_blocks]), lattice_cols
    )
    geometry, later = lax.optimization_barrier((geometry, later))
    target_geometry = [part[: targets.shape[0]] for part in geometry]
    source_geometry = [part[targets.shape[0] :] for part in geometry]
    self_tiles = self_tile_block([part[:band_rows] for part in target_geometry])
    pair_tiles = pair_tile_block([part[band_rows:] for part in target_geometry], source_geometry)
    low_row = low_blocks // columns - first_row
    high_row = high_blocks // columns - first_row
    low_pos = position_of[low_blocks % columns]
    high_pos = position_of[high_blocks % columns]
    slot_table = (low_row, low_pos, high_row, high_pos)
    return (self_tiles, pair_tiles, slot_table), later


def near_product(block_values, later, prepared):
    self_tiles, pair_tiles, slot_table = prepared
    band_rows = block_values.shape[0]
    low_row, low_pos, high_row, high_pos = slot_table
    self_term = apply_tiles(block_values[:, 0], self_tiles)
    source_table = lax.all_gather(
        jnp.concatenate([block_values, later], axis=0), "col", axis=1, tiled=True
    )
    table_rows, columns = source_table.shape[:2]
    flat_table = source_table.reshape(table_rows * columns, -1)
    slots = jnp.arange(table_rows * columns, dtype=jnp.int32)
    low_pick = (slots[None, :] == (low_row * columns + low_pos)[:, None]).astype(jnp.float32)
    high_pick = (slots[None, :] == (high_row * columns + high_pos)[:, None]).astype(jnp.float32)
    shape = (low_row.shape[0],) + source_table.shape[2:]
    high_values = jnp.dot(high_pick, flat_table, precision=lax.Precision.HIGHEST).reshape(shape)
    low_values = jnp.dot(low_pick, flat_table, precision=lax.Precision.HIGHEST).reshape(shape)
    to_low = apply_tiles(high_values, pair_tiles).reshape(low_row.shape[0], -1)
    to_high = apply_transposed(low_values, pair_tiles).reshape(low_row.shape[0], -1)
    partial_value = jnp.dot(
        jnp.concatenate([low_pick, high_pick]).T,
        jnp.concatenate([to_low, to_high]),
        precision=lax.Precision.HIGHEST,
    ).reshape(source_table.shape)
    summed = jnp.sum(lax.all_to_all(partial_value, "col", 1, 1, tiled=True), axis=1)
    own_partial = summed[:band_rows] + self_term
    reaching = summed[band_rows:]
    bands = lax.axis_size("row")
    band_index = lax.axis_index("row")
    slot = jnp.arange(bands, dtype=jnp.int32)[:, None, None, None]
    outgoing = jnp.where(
        slot == band_index - 1,
        own_partial[None, :REACH],
        jnp.where(slot == band_index + 1, reaching[None], 0.0),
    )
    incoming = lax.all_to_all(outgoing, "row", 0, 0, tiled=True)
    carried_down = jnp.sum(jnp.where(slot == band_index - 1, incoming, 0.0), axis=0)
    sent_up = jnp.sum(jnp.where(slot == band_index + 1, incoming, 0.0), axis=0)
    head = own_partial[:REACH] + carried_down
    own = jnp.concatenate([head, own_partial[REACH:]], axis=0)[:, None]
    return own, (sent_up + reaching)[:, None]


def body(charges, column_order, vertices, panel_vertices, near_pairs):
    later = shifted(charges[:REACH], "row", -1)
    prepared, later = prepare(
        column_order, vertices, panel_vertices, near_pairs, charges.shape[0], later
    )
    potential_one, later_one = near_product(charges, later, prepared)
    potential_two, _ = near_product(potential_one, later_one, prepared)
    return (potential_one, potential_two)


def solution(mesh):
    return jax.shard_map(
        body,
        mesh=mesh,
        in_specs=(P("row", "col", None, None), P(), P(), P(), P()),
        out_specs=(P("row", "col", None, None), P("row", "col", None, None)),
        check_vma=False,
    )
```

```python
import math

import jax
import jax.numpy as jnp
import numpy as np
from jax import lax
from jax.experimental import pallas as pl
from jax.experimental.pallas import tpu as pltpu
from jax.sharding import PartitionSpec as P

PANELS = 256
REACH = 3
QUAD_ROWS = 8
QUAD_COLS = 16
FEATURES = 32


def shifted(value, axis, by):
    length = lax.axis_size(axis)
    pairs = [(i, i + by) for i in range(length) if 0 <= i + by < length]
    return lax.ppermute(value, axis, pairs)


def rule_tables():
    gauss_two = np.array([-1.0, 1.0]) / math.sqrt(3.0)
    gauss_four = np.array(
        [-0.8611363115940526, -0.3399810435848563, 0.3399810435848563, 0.8611363115940526]
    )
    weight_four = np.array(
        [0.3478548451374538, 0.6521451548625461, 0.6521451548625461, 0.3478548451374538]
    )
    corner_weights = []
    point_weights = []
    for first_index in range(2):
        for second_index in range(4):
            along = 0.5 * (1.0 + gauss_two[first_index])
            across = 0.5 * (1.0 + gauss_four[second_index])
            corner_weights.append([along, (1.0 - along) * across, (1.0 - along) * (1.0 - across)])
            point_weights.append(2.0 * 0.5 * 0.5 * weight_four[second_index] * (1.0 - along))
    return (np.array(corner_weights), np.array(point_weights))


def block_corners(vertices, panel_vertices, block_ids, lattice_cols):
    patch_rows, patch_cols = QUAD_ROWS + 1, QUAD_COLS + 1
    panels = panel_vertices.reshape(3, -1, PANELS)[:, block_ids]
    lattice_row = panels // lattice_cols
    lattice_col = panels % lattice_cols
    base_row = jnp.min(lattice_row, axis=(0, 2))
    base_col = jnp.min(lattice_col, axis=(0, 2))
    local = (lattice_row - base_row[None, :, None]) * patch_cols + (
        lattice_col - base_col[None, :, None]
    )
    grid = jnp.transpose(vertices.reshape(3, -1, lattice_cols), (1, 0, 2))
    row_pick = (
        (base_row[:, None] + jnp.arange(patch_rows, dtype=jnp.int32))[:, :, None]
        == jnp.arange(grid.shape[0], dtype=jnp.int32)
    ).astype(jnp.float32)
    col_pick = (
        jnp.arange(lattice_cols, dtype=jnp.int32)[None, :, None]
        == (base_col[:, None] + jnp.arange(patch_cols, dtype=jnp.int32))[:, None, :]
    ).astype(jnp.float32)
    band = jnp.einsum("grR,Rxc->grxc", row_pick, grid, precision=lax.Precision.HIGHEST)
    patch = jnp.einsum("grxc,gcj->gxrj", band, col_pick, precision=lax.Precision.HIGHEST)
    patch = patch.reshape(block_ids.shape[0], 3, patch_rows * patch_cols)
    pick = (
        local[:, :, :, None] == jnp.arange(patch_rows * patch_cols, dtype=jnp.int32)
    ).astype(jnp.float32)
    return jnp.einsum("gxl,cgpl->gcxp", patch, pick, precision=lax.Precision.HIGHEST)


def block_geometry(vertices, panel_vertices, block_ids, lattice_cols):
    corners = block_corners(vertices, panel_vertices, block_ids, lattice_cols)
    centre = (corners[:, 0] + corners[:, 1] + corners[:, 2]) / 3.0
    first_edge = corners[:, 1] - corners[:, 0]
    second_edge = corners[:, 2] - corners[:, 0]
    normal_x = first_edge[:, 1] * second_edge[:, 2] - first_edge[:, 2] * second_edge[:, 1]
    normal_y = first_edge[:, 2] * second_edge[:, 0] - first_edge[:, 0] * second_edge[:, 2]
    normal_z = first_edge[:, 0] * second_edge[:, 1] - first_edge[:, 1] * second_edge[:, 0]
    panel_area = 0.5 * jnp.sqrt(normal_x * normal_x + normal_y * normal_y + normal_z * normal_z)
    corner_weights, _ = rule_tables()
    points = jnp.einsum(
        "kc,gcxp->gxkp",
        jnp.asarray(corner_weights, corners.dtype),
        corners,
        precision=lax.Precision.HIGHEST,
    )
    return (centre, points, panel_area)


def tile_block(target, source):
    target_centre, target_points, target_area = target
    source_centre, source_points, source_area = source
    _, point_weights = rule_tables()
    kernel_sum = jnp.zeros(
        (target_centre.shape[0], target_centre.shape[2], source_centre.shape[2]), jnp.float32
    )
    for point_index in range(8):
        weight = float(point_weights[point_index])
        distance = target_centre[:, :, :, None] - source_points[:, :, point_index, None, :]
        kernel_sum = kernel_sum + weight * lax.rsqrt(jnp.sum(distance * distance, axis=1) + 0.01)
        distance = target_points[:, :, point_index, :, None] - source_centre[:, :, None, :]
        kernel_sum = kernel_sum + weight * lax.rsqrt(jnp.sum(distance * distance, axis=1) + 0.01)
    return kernel_sum * target_area[:, :, None] * source_area[:, None, :] / (8.0 * math.pi)


def feature_rows(geometry):
    centre, points, area = geometry
    count = centre.shape[0]
    flat_points = jnp.transpose(points, (0, 2, 1, 3)).reshape(count, -1, PANELS)
    pad = jnp.zeros((count, FEATURES - 4 - flat_points.shape[1], PANELS), jnp.float32)
    return jnp.concatenate([centre, flat_points, area[:, None], pad], axis=1)


def pair_tile_block(target, source):
    _, point_weights = rule_tables()
    target_rows = feature_rows(target)
    source_rows = feature_rows(source)
    count = target_rows.shape[0]
    area_at = 3 + 3 * len(point_weights)
    chunk = 16

    def kernel(target_ref, source_ref, out_ref, turned_ref):
        turned_ref[...] = target_ref[0].T
        source_centre = [
            jnp.broadcast_to(source_ref[0, axis : axis + 1, :], (chunk, PANELS))
            for axis in range(3)
        ]
        source_area = source_ref[0, area_at : area_at + 1, :]

        def body(step, carry):
            rows = pl.ds(pl.multiple_of(step * chunk, chunk), chunk)
            held = turned_ref[rows, :]
            target_centre = [
                jnp.broadcast_to(held[:, axis : axis + 1], (chunk, PANELS)) for axis in range(3)
            ]
            total = jnp.zeros((chunk, PANELS), jnp.float32)
            for point_index, weight in enumerate(point_weights):
                at = 3 + 3 * point_index
                squared = 0.01
                for axis in range(3):
                    gap = target_centre[axis] - source_ref[0, at + axis : at + axis + 1, :]
                    squared = squared + gap * gap
                total = total + float(weight) * lax.rsqrt(squared)
                squared = 0.01
                for axis in range(3):
                    gap = held[:, at + axis : at + axis + 1] - source_centre[axis]
                    squared = squared + gap * gap
                total = total + float(weight) * lax.rsqrt(squared)
            scale = held[:, area_at : area_at + 1] * source_area
            out_ref[0, rows, :] = total * scale * (1.0 / (8.0 * math.pi))
            return carry

        lax.fori_loop(0, PANELS // chunk, body, 0)

    return pl.pallas_call(
        kernel,
        out_shape=jax.ShapeDtypeStruct((count, PANELS, PANELS), jnp.float32),
        grid=(count,),
        in_specs=[
            pl.BlockSpec((1, FEATURES, PANELS), lambda i: (i, 0, 0)),
            pl.BlockSpec((1, FEATURES, PANELS), lambda i: (i, 0, 0)),
        ],
        out_specs=pl.BlockSpec((1, PANELS, PANELS), lambda i: (i, 0, 0)),
        scratch_shapes=[pltpu.VMEM((PANELS, FEATURES), jnp.float32)],
        cost_estimate=pl.CostEstimate(
            flops=count * PANELS * PANELS * 16 * 11,
            transcendentals=count * PANELS * PANELS * 16,
            bytes_accessed=count * PANELS * (PANELS + 2 * FEATURES) * 4,
        ),
    )(target_rows, source_rows)


def self_tile_block(geometry):
    centre, points, area = geometry
    _, point_weights = rule_tables()
    half_sum = jnp.zeros((centre.shape[0], centre.shape[2], centre.shape[2]), jnp.float32)
    for point_index in range(8):
        weight = float(point_weights[point_index])
        distance = centre[:, :, :, None] - points[:, :, point_index, None, :]
        half_sum = half_sum + weight * lax.rsqrt(jnp.sum(distance * distance, axis=1) + 0.01)
    kernel_sum = half_sum + jnp.swapaxes(half_sum, 1, 2)
    return kernel_sum * area[:, :, None] * area[:, None, :] / (8.0 * math.pi)


def apply_tiles(source_values, tile_stack):
    return jnp.einsum("grq,gpq->grp", source_values, tile_stack, precision=lax.Precision.HIGHEST)


def apply_transposed(source_values, tile_stack):
    return jnp.einsum("grp,gpq->grq", source_values, tile_stack, precision=lax.Precision.HIGHEST)


def prepare(column_order, vertices, panel_vertices, near_pairs, band_rows, later):
    columns = lax.axis_size("col")
    band_count = lax.axis_size("row")
    band_index = lax.axis_index("row")
    column_index = lax.axis_index("col")
    positions = jnp.arange(columns, dtype=jnp.int32)
    position_of = jnp.sum(
        jnp.where(column_order[:, None] == positions[None, :], positions[:, None], 0), axis=0
    )
    home_column = jnp.sum(jnp.where(positions == column_index, column_order, 0))
    first_row = band_index * band_rows
    own_blocks = (first_row + jnp.arange(band_rows, dtype=jnp.int32)) * columns + home_column
    band_pairs = near_pairs.shape[1] // band_count
    share = band_pairs // columns
    segment = lax.dynamic_slice_in_dim(
        near_pairs, band_index * band_pairs + column_index * share, share, 1
    )
    low_blocks = segment[0]
    high_blocks = segment[1]
    targets = jnp.concatenate([own_blocks, low_blocks])
    lattice_cols = columns * QUAD_COLS + 1
    geometry = block_geometry(
        vertices, panel_vertices, jnp.concatenate([targets, high_blocks]), lattice_cols
    )
    geometry, later = lax.optimization_barrier((geometry, later))
    target_geometry = [part[: targets.shape[0]] for part in geometry]
    source_geometry = [part[targets.shape[0] :] for part in geometry]
    self_tiles = self_tile_block([part[:band_rows] for part in target_geometry])
    pair_tiles = pair_tile_block([part[band_rows:] for part in target_geometry], source_geometry)
    low_row = low_blocks // columns - first_row
    high_row = high_blocks // columns - first_row
    low_pos = position_of[low_blocks % columns]
    high_pos = position_of[high_blocks % columns]
    slot_table = (low_row, low_pos, high_row, high_pos)
    return (self_tiles, pair_tiles, slot_table), later


def near_product(block_values, later, prepared, both_ways):
    self_tiles, pair_tiles, slot_table = prepared
    band_rows = block_values.shape[0]
    low_row, low_pos, high_row, high_pos = slot_table
    self_term = apply_tiles(block_values[:, 0], self_tiles)
    source_table = lax.all_gather(
        jnp.concatenate([block_values, later], axis=0), "col", axis=1, tiled=True
    )
    table_rows, columns = source_table.shape[:2]
    flat_table = source_table.reshape(table_rows * columns, -1)
    slots = jnp.arange(table_rows * columns, dtype=jnp.int32)
    low_pick = (slots[None, :] == (low_row * columns + low_pos)[:, None]).astype(jnp.float32)
    high_pick = (slots[None, :] == (high_row * columns + high_pos)[:, None]).astype(jnp.float32)
    shape = (low_row.shape[0],) + source_table.shape[2:]
    high_values = jnp.dot(high_pick, flat_table, precision=lax.Precision.HIGHEST).reshape(shape)
    low_values = jnp.dot(low_pick, flat_table, precision=lax.Precision.HIGHEST).reshape(shape)
    to_low = apply_tiles(high_values, pair_tiles).reshape(low_row.shape[0], -1)
    to_high = apply_transposed(low_values, pair_tiles).reshape(low_row.shape[0], -1)
    partial_value = jnp.dot(
        jnp.concatenate([low_pick, high_pick]).T,
        jnp.concatenate([to_low, to_high]),
        precision=lax.Precision.HIGHEST,
    ).reshape(source_table.shape)
    summed = jnp.sum(lax.all_to_all(partial_value, "col", 1, 1, tiled=True), axis=1)
    own_partial = summed[:band_rows] + self_term
    reaching = summed[band_rows:]
    if not both_ways:
        carried_down = shifted(reaching, "row", 1)
        head = own_partial[:REACH] + carried_down
        own = jnp.concatenate([head, own_partial[REACH:]], axis=0)[:, None]
        return own, None
    bands = lax.axis_size("row")
    band_index = lax.axis_index("row")
    slot = jnp.arange(bands, dtype=jnp.int32)[:, None, None, None]
    outgoing = jnp.where(
        slot == band_index - 1,
        own_partial[None, :REACH],
        jnp.where(slot == band_index + 1, reaching[None], 0.0),
    )
    incoming = lax.all_to_all(outgoing, "row", 0, 0, tiled=True)
    carried_down = jnp.sum(jnp.where(slot == band_index - 1, incoming, 0.0), axis=0)
    sent_up = jnp.sum(jnp.where(slot == band_index + 1, incoming, 0.0), axis=0)
    head = own_partial[:REACH] + carried_down
    own = jnp.concatenate([head, own_partial[REACH:]], axis=0)[:, None]
    return own, (sent_up + reaching)[:, None]


def body(charges, column_order, vertices, panel_vertices, near_pairs):
    later = shifted(charges[:REACH], "row", -1)
    prepared, later = prepare(
        column_order, vertices, panel_vertices, near_pairs, charges.shape[0], later
    )
    potential_one, later_one = near_product(charges, later, prepared, True)
    potential_two, _ = near_product(potential_one, later_one, prepared, False)
    return (potential_one, potential_two)


def solution(mesh):
    return jax.shard_map(
        body,
        mesh=mesh,
        in_specs=(P("row", "col", None, None), P(), P(), P(), P()),
        out_specs=(P("row", "col", None, None), P("row", "col", None, None)),
        check_vma=False,
    )
```

```python
import math

import jax
import jax.numpy as jnp
import numpy as np
from jax import lax
from jax.experimental import pallas as pl
from jax.experimental.pallas import tpu as pltpu
from jax.sharding import PartitionSpec as P

PANELS = 256
REACH = 3
QUAD_ROWS = 8
QUAD_COLS = 16
FEATURES = 32


def shifted(value, axis, by):
    length = lax.axis_size(axis)
    pairs = [(i, i + by) for i in range(length) if 0 <= i + by < length]
    return lax.ppermute(value, axis, pairs)


def rule_tables():
    gauss_two = np.array([-1.0, 1.0]) / math.sqrt(3.0)
    gauss_four = np.array(
        [-0.8611363115940526, -0.3399810435848563, 0.3399810435848563, 0.8611363115940526]
    )
    weight_four = np.array(
        [0.3478548451374538, 0.6521451548625461, 0.6521451548625461, 0.3478548451374538]
    )
    corner_weights = []
    point_weights = []
    for first_index in range(2):
        for second_index in range(4):
            along = 0.5 * (1.0 + gauss_two[first_index])
            across = 0.5 * (1.0 + gauss_four[second_index])
            corner_weights.append([along, (1.0 - along) * across, (1.0 - along) * (1.0 - across)])
            point_weights.append(2.0 * 0.5 * 0.5 * weight_four[second_index] * (1.0 - along))
    return (np.array(corner_weights), np.array(point_weights))


def block_corners(vertices, panel_vertices, block_ids, lattice_cols):
    patch_rows, patch_cols = QUAD_ROWS + 1, QUAD_COLS + 1
    panels = panel_vertices.reshape(3, -1, PANELS)[:, block_ids]
    lattice_row = panels // lattice_cols
    lattice_col = panels % lattice_cols
    base_row = jnp.min(lattice_row, axis=(0, 2))
    base_col = jnp.min(lattice_col, axis=(0, 2))
    local = (lattice_row - base_row[None, :, None]) * patch_cols + (
        lattice_col - base_col[None, :, None]
    )
    grid = jnp.transpose(vertices.reshape(3, -1, lattice_cols), (1, 0, 2))
    row_pick = (
        (base_row[:, None] + jnp.arange(patch_rows, dtype=jnp.int32))[:, :, None]
        == jnp.arange(grid.shape[0], dtype=jnp.int32)
    ).astype(jnp.float32)
    col_pick = (
        jnp.arange(lattice_cols, dtype=jnp.int32)[None, :, None]
        == (base_col[:, None] + jnp.arange(patch_cols, dtype=jnp.int32))[:, None, :]
    ).astype(jnp.float32)
    band = jnp.einsum("grR,Rxc->grxc", row_pick, grid, precision=lax.Precision.HIGHEST)
    patch = jnp.einsum("grxc,gcj->gxrj", band, col_pick, precision=lax.Precision.HIGHEST)
    patch = patch.reshape(block_ids.shape[0], 3, patch_rows * patch_cols)
    pick = (
        local[:, :, :, None] == jnp.arange(patch_rows * patch_cols, dtype=jnp.int32)
    ).astype(jnp.float32)
    return jnp.einsum("gxl,cgpl->gcxp", patch, pick, precision=lax.Precision.HIGHEST)


def block_geometry(vertices, panel_vertices, block_ids, lattice_cols):
    corners = block_corners(vertices, panel_vertices, block_ids, lattice_cols)
    centre = (corners[:, 0] + corners[:, 1] + corners[:, 2]) / 3.0
    first_edge = corners[:, 1] - corners[:, 0]
    second_edge = corners[:, 2] - corners[:, 0]
    normal_x = first_edge[:, 1] * second_edge[:, 2] - first_edge[:, 2] * second_edge[:, 1]
    normal_y = first_edge[:, 2] * second_edge[:, 0] - first_edge[:, 0] * second_edge[:, 2]
    normal_z = first_edge[:, 0] * second_edge[:, 1] - first_edge[:, 1] * second_edge[:, 0]
    panel_area = 0.5 * jnp.sqrt(normal_x * normal_x + normal_y * normal_y + normal_z * normal_z)
    corner_weights, _ = rule_tables()
    points = jnp.einsum(
        "kc,gcxp->gxkp",
        jnp.asarray(corner_weights, corners.dtype),
        corners,
        precision=lax.Precision.HIGHEST,
    )
    return (centre, points, panel_area)


def tile_block(target, source):
    target_centre, target_points, target_area = target
    source_centre, source_points, source_area = source
    _, point_weights = rule_tables()
    kernel_sum = jnp.zeros(
        (target_centre.shape[0], target_centre.shape[2], source_centre.shape[2]), jnp.float32
    )
    for point_index in range(8):
        weight = float(point_weights[point_index])
        distance = target_centre[:, :, :, None] - source_points[:, :, point_index, None, :]
        kernel_sum = kernel_sum + weight * lax.rsqrt(jnp.sum(distance * distance, axis=1) + 0.01)
        distance = target_points[:, :, point_index, :, None] - source_centre[:, :, None, :]
        kernel_sum = kernel_sum + weight * lax.rsqrt(jnp.sum(distance * distance, axis=1) + 0.01)
    return kernel_sum * target_area[:, :, None] * source_area[:, None, :] / (8.0 * math.pi)


def feature_rows(geometry):
    centre, points, area = geometry
    count = centre.shape[0]
    flat_points = jnp.transpose(points, (0, 2, 1, 3)).reshape(count, -1, PANELS)
    pad = jnp.zeros((count, FEATURES - 4 - flat_points.shape[1], PANELS), jnp.float32)
    return jnp.concatenate([centre, flat_points, area[:, None], pad], axis=1)


def pair_tile_block(target, source):
    _, point_weights = rule_tables()
    target_rows = feature_rows(target)
    source_rows = feature_rows(source)
    count = target_rows.shape[0]
    area_at = 3 + 3 * len(point_weights)
    chunk = 8

    def kernel(target_ref, source_ref, out_ref, turned_ref):
        turned_ref[...] = target_ref[0].T
        source_centre = [
            jnp.broadcast_to(source_ref[0, axis : axis + 1, :], (chunk, PANELS))
            for axis in range(3)
        ]
        source_area = source_ref[0, area_at : area_at + 1, :]

        def body(step, carry):
            rows = pl.ds(pl.multiple_of(step * chunk, chunk), chunk)
            held = turned_ref[rows, :]
            target_centre = [
                jnp.broadcast_to(held[:, axis : axis + 1], (chunk, PANELS)) for axis in range(3)
            ]
            total = jnp.zeros((chunk, PANELS), jnp.float32)
            for point_index, weight in enumerate(point_weights):
                at = 3 + 3 * point_index
                squared = 0.01
                for axis in range(3):
                    gap = target_centre[axis] - source_ref[0, at + axis : at + axis + 1, :]
                    squared = squared + gap * gap
                total = total + float(weight) * lax.rsqrt(squared)
                squared = 0.01
                for axis in range(3):
                    gap = held[:, at + axis : at + axis + 1] - source_centre[axis]
                    squared = squared + gap * gap
                total = total + float(weight) * lax.rsqrt(squared)
            scale = held[:, area_at : area_at + 1] * source_area
            out_ref[0, rows, :] = total * scale * (1.0 / (8.0 * math.pi))
            return carry

        lax.fori_loop(0, PANELS // chunk, body, 0)

    return pl.pallas_call(
        kernel,
        out_shape=jax.ShapeDtypeStruct((count, PANELS, PANELS), jnp.float32),
        grid=(count,),
        in_specs=[
            pl.BlockSpec((1, FEATURES, PANELS), lambda i: (i, 0, 0)),
            pl.BlockSpec((1, FEATURES, PANELS), lambda i: (i, 0, 0)),
        ],
        out_specs=pl.BlockSpec((1, PANELS, PANELS), lambda i: (i, 0, 0)),
        scratch_shapes=[pltpu.VMEM((PANELS, FEATURES), jnp.float32)],
        cost_estimate=pl.CostEstimate(
            flops=count * PANELS * PANELS * 16 * 11,
            transcendentals=count * PANELS * PANELS * 16,
            bytes_accessed=count * PANELS * (PANELS + 2 * FEATURES) * 4,
        ),
    )(target_rows, source_rows)


def self_tile_block(geometry):
    centre, points, area = geometry
    _, point_weights = rule_tables()
    half_sum = jnp.zeros((centre.shape[0], centre.shape[2], centre.shape[2]), jnp.float32)
    for point_index in range(8):
        weight = float(point_weights[point_index])
        distance = centre[:, :, :, None] - points[:, :, point_index, None, :]
        half_sum = half_sum + weight * lax.rsqrt(jnp.sum(distance * distance, axis=1) + 0.01)
    kernel_sum = half_sum + jnp.swapaxes(half_sum, 1, 2)
    return kernel_sum * area[:, :, None] * area[:, None, :] / (8.0 * math.pi)


def apply_tiles(source_values, tile_stack):
    return jnp.einsum("grq,gpq->grp", source_values, tile_stack, precision=lax.Precision.HIGHEST)


def apply_transposed(source_values, tile_stack):
    return jnp.einsum("grp,gpq->grq", source_values, tile_stack, precision=lax.Precision.HIGHEST)


def prepare(column_order, vertices, panel_vertices, near_pairs, band_rows, later):
    columns = lax.axis_size("col")
    band_count = lax.axis_size("row")
    band_index = lax.axis_index("row")
    column_index = lax.axis_index("col")
    positions = jnp.arange(columns, dtype=jnp.int32)
    position_of = jnp.sum(
        jnp.where(column_order[:, None] == positions[None, :], positions[:, None], 0), axis=0
    )
    home_column = jnp.sum(jnp.where(positions == column_index, column_order, 0))
    first_row = band_index * band_rows
    own_blocks = (first_row + jnp.arange(band_rows, dtype=jnp.int32)) * columns + home_column
    band_pairs = near_pairs.shape[1] // band_count
    share = band_pairs // columns
    segment = lax.dynamic_slice_in_dim(
        near_pairs, band_index * band_pairs + column_index * share, share, 1
    )
    low_blocks = segment[0]
    high_blocks = segment[1]
    targets = jnp.concatenate([own_blocks, low_blocks])
    lattice_cols = columns * QUAD_COLS + 1
    geometry = block_geometry(
        vertices, panel_vertices, jnp.concatenate([targets, high_blocks]), lattice_cols
    )
    geometry, later = lax.optimization_barrier((geometry, later))
    target_geometry = [part[: targets.shape[0]] for part in geometry]
    source_geometry = [part[targets.shape[0] :] for part in geometry]
    self_tiles = self_tile_block([part[:band_rows] for part in target_geometry])
    pair_tiles = pair_tile_block([part[band_rows:] for part in target_geometry], source_geometry)
    low_row = low_blocks // columns - first_row
    high_row = high_blocks // columns - first_row
    low_pos = position_of[low_blocks % columns]
    high_pos = position_of[high_blocks % columns]
    slot_table = (low_row, low_pos, high_row, high_pos)
    return (self_tiles, pair_tiles, slot_table), later


def near_product(block_values, later, prepared, both_ways):
    self_tiles, pair_tiles, slot_table = prepared
    band_rows = block_values.shape[0]
    low_row, low_pos, high_row, high_pos = slot_table
    self_term = apply_tiles(block_values[:, 0], self_tiles)
    source_table = lax.all_gather(
        jnp.concatenate([block_values, later], axis=0), "col", axis=1, tiled=True
    )
    table_rows, columns = source_table.shape[:2]
    flat_table = source_table.reshape(table_rows * columns, -1)
    slots = jnp.arange(table_rows * columns, dtype=jnp.int32)
    low_pick = (slots[None, :] == (low_row * columns + low_pos)[:, None]).astype(jnp.float32)
    high_pick = (slots[None, :] == (high_row * columns + high_pos)[:, None]).astype(jnp.float32)
    shape = (low_row.shape[0],) + source_table.shape[2:]
    high_values = jnp.dot(high_pick, flat_table, precision=lax.Precision.HIGHEST).reshape(shape)
    low_values = jnp.dot(low_pick, flat_table, precision=lax.Precision.HIGHEST).reshape(shape)
    to_low = apply_tiles(high_values, pair_tiles).reshape(low_row.shape[0], -1)
    to_high = apply_transposed(low_values, pair_tiles).reshape(low_row.shape[0], -1)
    partial_value = jnp.dot(
        jnp.concatenate([low_pick, high_pick]).T,
        jnp.concatenate([to_low, to_high]),
        precision=lax.Precision.HIGHEST,
    ).reshape(source_table.shape)
    summed = jnp.sum(lax.all_to_all(partial_value, "col", 1, 1, tiled=True), axis=1)
    own_partial = summed[:band_rows] + self_term
    reaching = summed[band_rows:]
    if not both_ways:
        carried_down = shifted(reaching, "row", 1)
        head = own_partial[:REACH] + carried_down
        own = jnp.concatenate([head, own_partial[REACH:]], axis=0)[:, None]
        return own, None
    bands = lax.axis_size("row")
    band_index = lax.axis_index("row")
    slot = jnp.arange(bands, dtype=jnp.int32)[:, None, None, None]
    outgoing = jnp.where(
        slot == band_index - 1,
        own_partial[None, :REACH],
        jnp.where(slot == band_index + 1, reaching[None], 0.0),
    )
    incoming = lax.all_to_all(outgoing, "row", 0, 0, tiled=True)
    carried_down = jnp.sum(jnp.where(slot == band_index - 1, incoming, 0.0), axis=0)
    sent_up = jnp.sum(jnp.where(slot == band_index + 1, incoming, 0.0), axis=0)
    head = own_partial[:REACH] + carried_down
    own = jnp.concatenate([head, own_partial[REACH:]], axis=0)[:, None]
    return own, (sent_up + reaching)[:, None]


def body(charges, column_order, vertices, panel_vertices, near_pairs):
    later = shifted(charges[:REACH], "row", -1)
    prepared, later = prepare(
        column_order, vertices, panel_vertices, near_pairs, charges.shape[0], later
    )
    potential_one, later_one = near_product(charges, later, prepared, True)
    potential_two, _ = near_product(potential_one, later_one, prepared, False)
    return (potential_one, potential_two)


def solution(mesh):
    return jax.shard_map(
        body,
        mesh=mesh,
        in_specs=(P("row", "col", None, None), P(), P(), P(), P()),
        out_specs=(P("row", "col", None, None), P("row", "col", None, None)),
        check_vma=False,
    )
```

```python
import math

import jax
import jax.numpy as jnp
import numpy as np
from jax import lax
from jax.experimental import pallas as pl
from jax.experimental.pallas import tpu as pltpu
from jax.sharding import PartitionSpec as P

PANELS = 256
REACH = 3
QUAD_ROWS = 8
QUAD_COLS = 16
FEATURES = 32


def shifted(value, axis, by):
    length = lax.axis_size(axis)
    pairs = [(i, i + by) for i in range(length) if 0 <= i + by < length]
    return lax.ppermute(value, axis, pairs)


def rule_tables():
    gauss_two = np.array([-1.0, 1.0]) / math.sqrt(3.0)
    gauss_four = np.array(
        [-0.8611363115940526, -0.3399810435848563, 0.3399810435848563, 0.8611363115940526]
    )
    weight_four = np.array(
        [0.3478548451374538, 0.6521451548625461, 0.6521451548625461, 0.3478548451374538]
    )
    corner_weights = []
    point_weights = []
    for first_index in range(2):
        for second_index in range(4):
            along = 0.5 * (1.0 + gauss_two[first_index])
            across = 0.5 * (1.0 + gauss_four[second_index])
            corner_weights.append([along, (1.0 - along) * across, (1.0 - along) * (1.0 - across)])
            point_weights.append(2.0 * 0.5 * 0.5 * weight_four[second_index] * (1.0 - along))
    return (np.array(corner_weights), np.array(point_weights))


def block_corners(vertices, panel_vertices, block_ids, lattice_cols):
    patch_rows, patch_cols = QUAD_ROWS + 1, QUAD_COLS + 1
    panels = panel_vertices.reshape(3, -1, PANELS)[:, block_ids]
    lattice_row = panels // lattice_cols
    lattice_col = panels % lattice_cols
    base_row = jnp.min(lattice_row, axis=(0, 2))
    base_col = jnp.min(lattice_col, axis=(0, 2))
    local = (lattice_row - base_row[None, :, None]) * patch_cols + (
        lattice_col - base_col[None, :, None]
    )
    grid = jnp.transpose(vertices.reshape(3, -1, lattice_cols), (1, 0, 2))
    row_pick = (
        (base_row[:, None] + jnp.arange(patch_rows, dtype=jnp.int32))[:, :, None]
        == jnp.arange(grid.shape[0], dtype=jnp.int32)
    ).astype(jnp.float32)
    col_pick = (
        jnp.arange(lattice_cols, dtype=jnp.int32)[None, :, None]
        == (base_col[:, None] + jnp.arange(patch_cols, dtype=jnp.int32))[:, None, :]
    ).astype(jnp.float32)
    band = jnp.einsum("grR,Rxc->grxc", row_pick, grid, precision=lax.Precision.HIGHEST)
    patch = jnp.einsum("grxc,gcj->gxrj", band, col_pick, precision=lax.Precision.HIGHEST)
    patch = patch.reshape(block_ids.shape[0], 3, patch_rows * patch_cols)
    pick = (
        local[:, :, :, None] == jnp.arange(patch_rows * patch_cols, dtype=jnp.int32)
    ).astype(jnp.float32)
    return jnp.einsum("gxl,cgpl->gcxp", patch, pick, precision=lax.Precision.HIGHEST)


def block_geometry(vertices, panel_vertices, block_ids, lattice_cols):
    corners = block_corners(vertices, panel_vertices, block_ids, lattice_cols)
    centre = (corners[:, 0] + corners[:, 1] + corners[:, 2]) / 3.0
    first_edge = corners[:, 1] - corners[:, 0]
    second_edge = corners[:, 2] - corners[:, 0]
    normal_x = first_edge[:, 1] * second_edge[:, 2] - first_edge[:, 2] * second_edge[:, 1]
    normal_y = first_edge[:, 2] * second_edge[:, 0] - first_edge[:, 0] * second_edge[:, 2]
    normal_z = first_edge[:, 0] * second_edge[:, 1] - first_edge[:, 1] * second_edge[:, 0]
    panel_area = 0.5 * jnp.sqrt(normal_x * normal_x + normal_y * normal_y + normal_z * normal_z)
    corner_weights, _ = rule_tables()
    points = jnp.einsum(
        "kc,gcxp->gxkp",
        jnp.asarray(corner_weights, corners.dtype),
        corners,
        precision=lax.Precision.HIGHEST,
    )
    return (centre, points, panel_area)


def tile_block(target, source):
    target_centre, target_points, target_area = target
    source_centre, source_points, source_area = source
    _, point_weights = rule_tables()
    kernel_sum = jnp.zeros(
        (target_centre.shape[0], target_centre.shape[2], source_centre.shape[2]), jnp.float32
    )
    for point_index in range(8):
        weight = float(point_weights[point_index])
        distance = target_centre[:, :, :, None] - source_points[:, :, point_index, None, :]
        kernel_sum = kernel_sum + weight * lax.rsqrt(jnp.sum(distance * distance, axis=1) + 0.01)
        distance = target_points[:, :, point_index, :, None] - source_centre[:, :, None, :]
        kernel_sum = kernel_sum + weight * lax.rsqrt(jnp.sum(distance * distance, axis=1) + 0.01)
    return kernel_sum * target_area[:, :, None] * source_area[:, None, :] / (8.0 * math.pi)


def feature_rows(geometry):
    centre, points, area = geometry
    count = centre.shape[0]
    flat_points = jnp.transpose(points, (0, 2, 1, 3)).reshape(count, -1, PANELS)
    pad = jnp.zeros((count, FEATURES - 4 - flat_points.shape[1], PANELS), jnp.float32)
    return jnp.concatenate([centre, flat_points, area[:, None], pad], axis=1)


def pair_tile_block(target, source):
    _, point_weights = rule_tables()
    target_rows = feature_rows(target)
    source_rows = feature_rows(source)
    count = target_rows.shape[0]
    area_at = 3 + 3 * len(point_weights)
    chunk = 32

    def kernel(target_ref, source_ref, out_ref, turned_ref):
        turned_ref[...] = target_ref[0].T
        source_centre = [
            jnp.broadcast_to(source_ref[0, axis : axis + 1, :], (chunk, PANELS))
            for axis in range(3)
        ]
        source_area = source_ref[0, area_at : area_at + 1, :]

        def body(step, carry):
            rows = pl.ds(pl.multiple_of(step * chunk, chunk), chunk)
            held = turned_ref[rows, :]
            target_centre = [
                jnp.broadcast_to(held[:, axis : axis + 1], (chunk, PANELS)) for axis in range(3)
            ]
            total = jnp.zeros((chunk, PANELS), jnp.float32)
            for point_index, weight in enumerate(point_weights):
                at = 3 + 3 * point_index
                squared = 0.01
                for axis in range(3):
                    gap = target_centre[axis] - source_ref[0, at + axis : at + axis + 1, :]
                    squared = squared + gap * gap
                total = total + float(weight) * lax.rsqrt(squared)
                squared = 0.01
                for axis in range(3):
                    gap = held[:, at + axis : at + axis + 1] - source_centre[axis]
                    squared = squared + gap * gap
                total = total + float(weight) * lax.rsqrt(squared)
            scale = held[:, area_at : area_at + 1] * source_area
            out_ref[0, rows, :] = total * scale * (1.0 / (8.0 * math.pi))
            return carry

        lax.fori_loop(0, PANELS // chunk, body, 0)

    return pl.pallas_call(
        kernel,
        out_shape=jax.ShapeDtypeStruct((count, PANELS, PANELS), jnp.float32),
        grid=(count,),
        in_specs=[
            pl.BlockSpec((1, FEATURES, PANELS), lambda i: (i, 0, 0)),
            pl.BlockSpec((1, FEATURES, PANELS), lambda i: (i, 0, 0)),
        ],
        out_specs=pl.BlockSpec((1, PANELS, PANELS), lambda i: (i, 0, 0)),
        scratch_shapes=[pltpu.VMEM((PANELS, FEATURES), jnp.float32)],
        cost_estimate=pl.CostEstimate(
            flops=count * PANELS * PANELS * 16 * 11,
            transcendentals=count * PANELS * PANELS * 16,
            bytes_accessed=count * PANELS * (PANELS + 2 * FEATURES) * 4,
        ),
    )(target_rows, source_rows)


def self_tile_block(geometry):
    centre, points, area = geometry
    _, point_weights = rule_tables()
    half_sum = jnp.zeros((centre.shape[0], centre.shape[2], centre.shape[2]), jnp.float32)
    for point_index in range(8):
        weight = float(point_weights[point_index])
        distance = centre[:, :, :, None] - points[:, :, point_index, None, :]
        half_sum = half_sum + weight * lax.rsqrt(jnp.sum(distance * distance, axis=1) + 0.01)
    kernel_sum = half_sum + jnp.swapaxes(half_sum, 1, 2)
    return kernel_sum * area[:, :, None] * area[:, None, :] / (8.0 * math.pi)


def apply_tiles(source_values, tile_stack):
    return jnp.einsum("grq,gpq->grp", source_values, tile_stack, precision=lax.Precision.HIGHEST)


def apply_transposed(source_values, tile_stack):
    return jnp.einsum("grp,gpq->grq", source_values, tile_stack, precision=lax.Precision.HIGHEST)


def prepare(column_order, vertices, panel_vertices, near_pairs, band_rows, later):
    columns = lax.axis_size("col")
    band_count = lax.axis_size("row")
    band_index = lax.axis_index("row")
    column_index = lax.axis_index("col")
    positions = jnp.arange(columns, dtype=jnp.int32)
    position_of = jnp.sum(
        jnp.where(column_order[:, None] == positions[None, :], positions[:, None], 0), axis=0
    )
    home_column = jnp.sum(jnp.where(positions == column_index, column_order, 0))
    first_row = band_index * band_rows
    own_blocks = (first_row + jnp.arange(band_rows, dtype=jnp.int32)) * columns + home_column
    band_pairs = near_pairs.shape[1] // band_count
    share = band_pairs // columns
    segment = lax.dynamic_slice_in_dim(
        near_pairs, band_index * band_pairs + column_index * share, share, 1
    )
    low_blocks = segment[0]
    high_blocks = segment[1]
    targets = jnp.concatenate([own_blocks, low_blocks])
    lattice_cols = columns * QUAD_COLS + 1
    geometry = block_geometry(
        vertices, panel_vertices, jnp.concatenate([targets, high_blocks]), lattice_cols
    )
    geometry, later = lax.optimization_barrier((geometry, later))
    target_geometry = [part[: targets.shape[0]] for part in geometry]
    source_geometry = [part[targets.shape[0] :] for part in geometry]
    self_tiles = self_tile_block([part[:band_rows] for part in target_geometry])
    pair_tiles = pair_tile_block([part[band_rows:] for part in target_geometry], source_geometry)
    low_row = low_blocks // columns - first_row
    high_row = high_blocks // columns - first_row
    low_pos = position_of[low_blocks % columns]
    high_pos = position_of[high_blocks % columns]
    slot_table = (low_row, low_pos, high_row, high_pos)
    return (self_tiles, pair_tiles, slot_table), later


def near_product(block_values, later, prepared, both_ways):
    self_tiles, pair_tiles, slot_table = prepared
    band_rows = block_values.shape[0]
    low_row, low_pos, high_row, high_pos = slot_table
    self_term = apply_tiles(block_values[:, 0], self_tiles)
    source_table = lax.all_gather(
        jnp.concatenate([block_values, later], axis=0), "col", axis=1, tiled=True
    )
    table_rows, columns = source_table.shape[:2]
    flat_table = source_table.reshape(table_rows * columns, -1)
    slots = jnp.arange(table_rows * columns, dtype=jnp.int32)
    low_pick = (slots[None, :] == (low_row * columns + low_pos)[:, None]).astype(jnp.float32)
    high_pick = (slots[None, :] == (high_row * columns + high_pos)[:, None]).astype(jnp.float32)
    shape = (low_row.shape[0],) + source_table.shape[2:]
    high_values = jnp.dot(high_pick, flat_table, precision=lax.Precision.HIGHEST).reshape(shape)
    low_values = jnp.dot(low_pick, flat_table, precision=lax.Precision.HIGHEST).reshape(shape)
    to_low = apply_tiles(high_values, pair_tiles).reshape(low_row.shape[0], -1)
    to_high = apply_transposed(low_values, pair_tiles).reshape(low_row.shape[0], -1)
    partial_value = jnp.dot(
        jnp.concatenate([low_pick, high_pick]).T,
        jnp.concatenate([to_low, to_high]),
        precision=lax.Precision.HIGHEST,
    ).reshape(source_table.shape)
    summed = jnp.sum(lax.all_to_all(partial_value, "col", 1, 1, tiled=True), axis=1)
    own_partial = summed[:band_rows] + self_term
    reaching = summed[band_rows:]
    if not both_ways:
        carried_down = shifted(reaching, "row", 1)
        head = own_partial[:REACH] + carried_down
        own = jnp.concatenate([head, own_partial[REACH:]], axis=0)[:, None]
        return own, None
    bands = lax.axis_size("row")
    band_index = lax.axis_index("row")
    slot = jnp.arange(bands, dtype=jnp.int32)[:, None, None, None]
    outgoing = jnp.where(
        slot == band_index - 1,
        own_partial[None, :REACH],
        jnp.where(slot == band_index + 1, reaching[None], 0.0),
    )
    incoming = lax.all_to_all(outgoing, "row", 0, 0, tiled=True)
    carried_down = jnp.sum(jnp.where(slot == band_index - 1, incoming, 0.0), axis=0)
    sent_up = jnp.sum(jnp.where(slot == band_index + 1, incoming, 0.0), axis=0)
    head = own_partial[:REACH] + carried_down
    own = jnp.concatenate([head, own_partial[REACH:]], axis=0)[:, None]
    return own, (sent_up + reaching)[:, None]


def body(charges, column_order, vertices, panel_vertices, near_pairs):
    later = shifted(charges[:REACH], "row", -1)
    prepared, later = prepare(
        column_order, vertices, panel_vertices, near_pairs, charges.shape[0], later
    )
    potential_one, later_one = near_product(charges, later, prepared, True)
    potential_two, _ = near_product(potential_one, later_one, prepared, False)
    return (potential_one, potential_two)


def solution(mesh):
    return jax.shard_map(
        body,
        mesh=mesh,
        in_specs=(P("row", "col", None, None), P(), P(), P(), P()),
        out_specs=(P("row", "col", None, None), P("row", "col", None, None)),
        check_vma=False,
    )
```

```python
import math

import jax
import jax.numpy as jnp
import numpy as np
from jax import lax
from jax.experimental import pallas as pl
from jax.experimental.pallas import tpu as pltpu
from jax.sharding import PartitionSpec as P

PANELS = 256
REACH = 3
QUAD_ROWS = 8
QUAD_COLS = 16
FEATURES = 32


def shifted(value, axis, by):
    length = lax.axis_size(axis)
    pairs = [(i, i + by) for i in range(length) if 0 <= i + by < length]
    return lax.ppermute(value, axis, pairs)


def rule_tables():
    gauss_two = np.array([-1.0, 1.0]) / math.sqrt(3.0)
    gauss_four = np.array(
        [-0.8611363115940526, -0.3399810435848563, 0.3399810435848563, 0.8611363115940526]
    )
    weight_four = np.array(
        [0.3478548451374538, 0.6521451548625461, 0.6521451548625461, 0.3478548451374538]
    )
    corner_weights = []
    point_weights = []
    for first_index in range(2):
        for second_index in range(4):
            along = 0.5 * (1.0 + gauss_two[first_index])
            across = 0.5 * (1.0 + gauss_four[second_index])
            corner_weights.append([along, (1.0 - along) * across, (1.0 - along) * (1.0 - across)])
            point_weights.append(2.0 * 0.5 * 0.5 * weight_four[second_index] * (1.0 - along))
    return (np.array(corner_weights), np.array(point_weights))


def block_corners(vertices, panel_vertices, block_ids, lattice_cols):
    patch_rows, patch_cols = QUAD_ROWS + 1, QUAD_COLS + 1
    panels = panel_vertices.reshape(3, -1, PANELS)[:, block_ids]
    lattice_row = panels // lattice_cols
    lattice_col = panels % lattice_cols
    base_row = jnp.min(lattice_row, axis=(0, 2))
    base_col = jnp.min(lattice_col, axis=(0, 2))
    local = (lattice_row - base_row[None, :, None]) * patch_cols + (
        lattice_col - base_col[None, :, None]
    )
    grid = jnp.transpose(vertices.reshape(3, -1, lattice_cols), (1, 0, 2))
    row_pick = (
        (base_row[:, None] + jnp.arange(patch_rows, dtype=jnp.int32))[:, :, None]
        == jnp.arange(grid.shape[0], dtype=jnp.int32)
    ).astype(jnp.float32)
    col_pick = (
        jnp.arange(lattice_cols, dtype=jnp.int32)[None, :, None]
        == (base_col[:, None] + jnp.arange(patch_cols, dtype=jnp.int32))[:, None, :]
    ).astype(jnp.float32)
    band = jnp.einsum("grR,Rxc->grxc", row_pick, grid, precision=lax.Precision.HIGHEST)
    patch = jnp.einsum("grxc,gcj->gxrj", band, col_pick, precision=lax.Precision.HIGHEST)
    patch = patch.reshape(block_ids.shape[0], 3, patch_rows * patch_cols)
    pick = (
        local[:, :, :, None] == jnp.arange(patch_rows * patch_cols, dtype=jnp.int32)
    ).astype(jnp.float32)
    return jnp.einsum("gxl,cgpl->gcxp", patch, pick, precision=lax.Precision.HIGHEST)


def block_geometry(vertices, panel_vertices, block_ids, lattice_cols):
    corners = block_corners(vertices, panel_vertices, block_ids, lattice_cols)
    centre = (corners[:, 0] + corners[:, 1] + corners[:, 2]) / 3.0
    first_edge = corners[:, 1] - corners[:, 0]
    second_edge = corners[:, 2] - corners[:, 0]
    normal_x = first_edge[:, 1] * second_edge[:, 2] - first_edge[:, 2] * second_edge[:, 1]
    normal_y = first_edge[:, 2] * second_edge[:, 0] - first_edge[:, 0] * second_edge[:, 2]
    normal_z = first_edge[:, 0] * second_edge[:, 1] - first_edge[:, 1] * second_edge[:, 0]
    panel_area = 0.5 * jnp.sqrt(normal_x * normal_x + normal_y * normal_y + normal_z * normal_z)
    corner_weights, _ = rule_tables()
    points = jnp.einsum(
        "kc,gcxp->gxkp",
        jnp.asarray(corner_weights, corners.dtype),
        corners,
        precision=lax.Precision.HIGHEST,
    )
    return (centre, points, panel_area)


def tile_block(target, source):
    target_centre, target_points, target_area = target
    source_centre, source_points, source_area = source
    _, point_weights = rule_tables()
    kernel_sum = jnp.zeros(
        (target_centre.shape[0], target_centre.shape[2], source_centre.shape[2]), jnp.float32
    )
    for point_index in range(8):
        weight = float(point_weights[point_index])
        distance = target_centre[:, :, :, None] - source_points[:, :, point_index, None, :]
        kernel_sum = kernel_sum + weight * lax.rsqrt(jnp.sum(distance * distance, axis=1) + 0.01)
        distance = target_points[:, :, point_index, :, None] - source_centre[:, :, None, :]
        kernel_sum = kernel_sum + weight * lax.rsqrt(jnp.sum(distance * distance, axis=1) + 0.01)
    return kernel_sum * target_area[:, :, None] * source_area[:, None, :] / (8.0 * math.pi)


def feature_rows(geometry):
    centre, points, area = geometry
    count = centre.shape[0]
    flat_points = jnp.transpose(points, (0, 2, 1, 3)).reshape(count, -1, PANELS)
    pad = jnp.zeros((count, FEATURES - 4 - flat_points.shape[1], PANELS), jnp.float32)
    return jnp.concatenate([centre, flat_points, area[:, None], pad], axis=1)


def pair_tile_block(target, source):
    _, point_weights = rule_tables()
    target_rows = feature_rows(target)
    source_rows = feature_rows(source)
    count = target_rows.shape[0]
    area_at = 3 + 3 * len(point_weights)
    chunk = 64

    def kernel(target_ref, source_ref, out_ref, turned_ref):
        turned_ref[...] = target_ref[0].T
        source_centre = [
            jnp.broadcast_to(source_ref[0, axis : axis + 1, :], (chunk, PANELS))
            for axis in range(3)
        ]
        source_area = source_ref[0, area_at : area_at + 1, :]

        def body(step, carry):
            rows = pl.ds(pl.multiple_of(step * chunk, chunk), chunk)
            held = turned_ref[rows, :]
            target_centre = [
                jnp.broadcast_to(held[:, axis : axis + 1], (chunk, PANELS)) for axis in range(3)
            ]
            total = jnp.zeros((chunk, PANELS), jnp.float32)
            for point_index, weight in enumerate(point_weights):
                at = 3 + 3 * point_index
                squared = 0.01
                for axis in range(3):
                    gap = target_centre[axis] - source_ref[0, at + axis : at + axis + 1, :]
                    squared = squared + gap * gap
                total = total + float(weight) * lax.rsqrt(squared)
                squared = 0.01
                for axis in range(3):
                    gap = held[:, at + axis : at + axis + 1] - source_centre[axis]
                    squared = squared + gap * gap
                total = total + float(weight) * lax.rsqrt(squared)
            scale = held[:, area_at : area_at + 1] * source_area
            out_ref[0, rows, :] = total * scale * (1.0 / (8.0 * math.pi))
            return carry

        lax.fori_loop(0, PANELS // chunk, body, 0)

    return pl.pallas_call(
        kernel,
        out_shape=jax.ShapeDtypeStruct((count, PANELS, PANELS), jnp.float32),
        grid=(count,),
        in_specs=[
            pl.BlockSpec((1, FEATURES, PANELS), lambda i: (i, 0, 0)),
            pl.BlockSpec((1, FEATURES, PANELS), lambda i: (i, 0, 0)),
        ],
        out_specs=pl.BlockSpec((1, PANELS, PANELS), lambda i: (i, 0, 0)),
        scratch_shapes=[pltpu.VMEM((PANELS, FEATURES), jnp.float32)],
        cost_estimate=pl.CostEstimate(
            flops=count * PANELS * PANELS * 16 * 11,
            transcendentals=count * PANELS * PANELS * 16,
            bytes_accessed=count * PANELS * (PANELS + 2 * FEATURES) * 4,
        ),
    )(target_rows, source_rows)


def self_tile_block(geometry):
    centre, points, area = geometry
    _, point_weights = rule_tables()
    half_sum = jnp.zeros((centre.shape[0], centre.shape[2], centre.shape[2]), jnp.float32)
    for point_index in range(8):
        weight = float(point_weights[point_index])
        distance = centre[:, :, :, None] - points[:, :, point_index, None, :]
        half_sum = half_sum + weight * lax.rsqrt(jnp.sum(distance * distance, axis=1) + 0.01)
    kernel_sum = half_sum + jnp.swapaxes(half_sum, 1, 2)
    return kernel_sum * area[:, :, None] * area[:, None, :] / (8.0 * math.pi)


def apply_tiles(source_values, tile_stack):
    return jnp.einsum("grq,gpq->grp", source_values, tile_stack, precision=lax.Precision.HIGHEST)


def apply_transposed(source_values, tile_stack):
    return jnp.einsum("grp,gpq->grq", source_values, tile_stack, precision=lax.Precision.HIGHEST)


def prepare(column_order, vertices, panel_vertices, near_pairs, band_rows, later):
    columns = lax.axis_size("col")
    band_count = lax.axis_size("row")
    band_index = lax.axis_index("row")
    column_index = lax.axis_index("col")
    positions = jnp.arange(columns, dtype=jnp.int32)
    position_of = jnp.sum(
        jnp.where(column_order[:, None] == positions[None, :], positions[:, None], 0), axis=0
    )
    home_column = jnp.sum(jnp.where(positions == column_index, column_order, 0))
    first_row = band_index * band_rows
    own_blocks = (first_row + jnp.arange(band_rows, dtype=jnp.int32)) * columns + home_column
    band_pairs = near_pairs.shape[1] // band_count
    share = band_pairs // columns
    segment = lax.dynamic_slice_in_dim(
        near_pairs, band_index * band_pairs + column_index * share, share, 1
    )
    low_blocks = segment[0]
    high_blocks = segment[1]
    targets = jnp.concatenate([own_blocks, low_blocks])
    lattice_cols = columns * QUAD_COLS + 1
    geometry = block_geometry(
        vertices, panel_vertices, jnp.concatenate([targets, high_blocks]), lattice_cols
    )
    geometry, later = lax.optimization_barrier((geometry, later))
    target_geometry = [part[: targets.shape[0]] for part in geometry]
    source_geometry = [part[targets.shape[0] :] for part in geometry]
    self_tiles = self_tile_block([part[:band_rows] for part in target_geometry])
    pair_tiles = pair_tile_block([part[band_rows:] for part in target_geometry], source_geometry)
    low_row = low_blocks // columns - first_row
    high_row = high_blocks // columns - first_row
    low_pos = position_of[low_blocks % columns]
    high_pos = position_of[high_blocks % columns]
    slot_table = (low_row, low_pos, high_row, high_pos)
    return (self_tiles, pair_tiles, slot_table), later


def near_product(block_values, later, prepared, both_ways):
    self_tiles, pair_tiles, slot_table = prepared
    band_rows = block_values.shape[0]
    low_row, low_pos, high_row, high_pos = slot_table
    self_term = apply_tiles(block_values[:, 0], self_tiles)
    source_table = lax.all_gather(
        jnp.concatenate([block_values, later], axis=0), "col", axis=1, tiled=True
    )
    table_rows, columns = source_table.shape[:2]
    flat_table = source_table.reshape(table_rows * columns, -1)
    slots = jnp.arange(table_rows * columns, dtype=jnp.int32)
    low_pick = (slots[None, :] == (low_row * columns + low_pos)[:, None]).astype(jnp.float32)
    high_pick = (slots[None, :] == (high_row * columns + high_pos)[:, None]).astype(jnp.float32)
    shape = (low_row.shape[0],) + source_table.shape[2:]
    high_values = jnp.dot(high_pick, flat_table, precision=lax.Precision.HIGHEST).reshape(shape)
    low_values = jnp.dot(low_pick, flat_table, precision=lax.Precision.HIGHEST).reshape(shape)
    to_low = apply_tiles(high_values, pair_tiles).reshape(low_row.shape[0], -1)
    to_high = apply_transposed(low_values, pair_tiles).reshape(low_row.shape[0], -1)
    partial_value = jnp.dot(
        jnp.concatenate([low_pick, high_pick]).T,
        jnp.concatenate([to_low, to_high]),
        precision=lax.Precision.HIGHEST,
    ).reshape(source_table.shape)
    summed = jnp.sum(lax.all_to_all(partial_value, "col", 1, 1, tiled=True), axis=1)
    own_partial = summed[:band_rows] + self_term
    reaching = summed[band_rows:]
    if not both_ways:
        carried_down = shifted(reaching, "row", 1)
        head = own_partial[:REACH] + carried_down
        own = jnp.concatenate([head, own_partial[REACH:]], axis=0)[:, None]
        return own, None
    bands = lax.axis_size("row")
    band_index = lax.axis_index("row")
    slot = jnp.arange(bands, dtype=jnp.int32)[:, None, None, None]
    outgoing = jnp.where(
        slot == band_index - 1,
        own_partial[None, :REACH],
        jnp.where(slot == band_index + 1, reaching[None], 0.0),
    )
    incoming = lax.all_to_all(outgoing, "row", 0, 0, tiled=True)
    carried_down = jnp.sum(jnp.where(slot == band_index - 1, incoming, 0.0), axis=0)
    sent_up = jnp.sum(jnp.where(slot == band_index + 1, incoming, 0.0), axis=0)
    head = own_partial[:REACH] + carried_down
    own = jnp.concatenate([head, own_partial[REACH:]], axis=0)[:, None]
    return own, (sent_up + reaching)[:, None]


def body(charges, column_order, vertices, panel_vertices, near_pairs):
    later = shifted(charges[:REACH], "row", -1)
    prepared, later = prepare(
        column_order, vertices, panel_vertices, near_pairs, charges.shape[0], later
    )
    potential_one, later_one = near_product(charges, later, prepared, True)
    potential_two, _ = near_product(potential_one, later_one, prepared, False)
    return (potential_one, potential_two)


def solution(mesh):
    return jax.shard_map(
        body,
        mesh=mesh,
        in_specs=(P("row", "col", None, None), P(), P(), P(), P()),
        out_specs=(P("row", "col", None, None), P("row", "col", None, None)),
        check_vma=False,
    )
```
